32 devices in a mesh: dp: 8 (over z, x), head: 4 (over y, core).
Axes of the slice: x: 2, y: 2, z: 4, core: 2. Of those that a mesh axis runs over, the one named last changes fastest.
Arguments:
- input_segments: float32 [16384, 32], P(('dp', 'head')), may hold values from -6 to 6
- filler_flags: int32 [16384, 32], P(('dp', 'head')), may hold values 0 or 1
- sequence_owner: int32 [16384], P(('dp', 'head')), may hold values from 0 to 127, never falling along the last dimension, each value on 1 to 256 neighbouring positions
- prediction_adjoint: bfloat16 [16384, 1280], P('dp', 'head'), may hold values from -6 to 6
- quadratic_params: float32 [6, 1280, 1280], P(None, ('dp', 'head')), may hold values from -0.3354102 to 0.3354102, as said below
- quadratic_velocity: float32 [6, 1280, 1280], P(None, ('dp', 'head')), may hold values from -384 to 384
- quadratic_mean: float32 [6, 1280, 1280], P(None, ('dp', 'head')), may hold values from -0.15625 to 0.15625
- perceptron_params: float32 [2, 1280, 5120], P(None, ('dp', 'head')), may hold values from -0.15625 to 0.15625
- perceptron_velocity: float32 [2, 1280, 5120], P(None, ('dp', 'head')), may hold values from -384 to 384
- perceptron_mean: float32 [2, 1280, 5120], P(None, ('dp', 'head')), may hold values from -0.15625 to 0.15625
- embedder_params: float32 [2, 1280, 64], P(None, ('dp', 'head')), may hold values from -0.75 to 0.75
- embedder_velocity: float32 [2, 1280, 64], P(None, ('dp', 'head')), may hold values from -384 to 384
- embedder_mean: float32 [2, 1280, 64], P(None, ('dp', 'head')), may hold values from -0.75 to 0.75
- bias_gain_params: float32 [5, 1280], P(None, ('dp', 'head')), may hold values from -1.6 to 1.6, as said below
- bias_gain_velocity: float32 [5, 1280], P(None, ('dp', 'head')), may hold values from -384 to 384
- bias_gain_mean: float32 [5, 1280], P(None, ('dp', 'head')), may hold values from -1.6 to 1.6, as said below
- readout_params: float32 [2, 1280, 1280], P(None, 'dp', 'head'), may hold values from -0.15625 to 0.15625
- readout_velocity: float32 [2, 1280, 1280], P(None, 'dp', 'head'), may hold values from -384 to 384
- readout_mean: float32 [2, 1280, 1280], P(None, 'dp', 'head'), may hold values from -0.15625 to 0.15625
Outputs:
- prediction: bfloat16 [16384, 1280], P('dp', 'head')
- segment_derivative: float32 [16384, 32], P(('dp', 'head'))
- quadratic_params_fresh: float32 [6, 1280, 1280], P(None, ('dp', 'head'))
- quadratic_velocity_fresh: float32 [6, 1280, 1280], P(None, ('dp', 'head'))
- quadratic_mean_fresh: float32 [6, 1280, 1280], P(None, ('dp', 'head'))
- perceptron_params_fresh: float32 [2, 1280, 5120], P(None, ('dp', 'head'))
- perceptron_velocity_fresh: float32 [2, 1280, 5120], P(None, ('dp', 'head'))
- perceptron_mean_fresh: float32 [2, 1280, 5120], P(None, ('dp', 'head'))
- embedder_params_fresh: float32 [2, 1280, 64], P(None, ('dp', 'head'))
- embedder_velocity_fresh: float32 [2, 1280, 64], P(None, ('dp', 'head'))
- embedder_mean_fresh: float32 [2, 1280, 64], P(None, ('dp', 'head'))
- bias_gain_params_fresh: float32 [5, 1280], P(None, ('dp', 'head'))
- bias_gain_velocity_fresh: float32 [5, 1280], P(None, ('dp', 'head'))
- bias_gain_mean_fresh: float32 [5, 1280], P(None, ('dp', 'head'))
- readout_params_fresh: float32 [2, 1280, 1280], P(None, 'dp', 'head')
- readout_velocity_fresh: float32 [2, 1280, 1280], P(None, 'dp', 'head')
- readout_mean_fresh: float32 [2, 1280, 1280], P(None, 'dp', 'head')
The draws below stay inside these ranges and needn't reach their ends.
Inputs may be any that keep to these rules, and one draw needn't show every extreme that they name: quadratic_params entries lie within this range. bias_gain_params entries lie within this range. bias_gain_mean entries lie within this range.
All inputs are finite; a program needn't handle non-finite values. No bound on the sum of `filler_flags` on one device may be relied on, other than what follows from the above.
Results may differ from the reference program's by a relative error of at most 0.019.
Values may be sent and summed in bfloat16 or wider, within the bound.
A program may use at most 448 MiB of HBM per device.

```python
import math
import jax
import jax.numpy as jnp
import numpy as np
from jax import lax

D = 1280
HEADS = 16
HEAD_DIM = 80
FF = 5120
PATCH = 32
QUANTILE_FIELDS = 1280
SEQ = 512
SEGMENT_NUMBER = 16384


def draw_quadratic_params(key, part):
    noise = jnp.clip(jax.random.normal(jax.random.fold_in(key, 11), (6, D, D), jnp.float32), -4.0, 4.0)
    factor = jnp.where(jnp.arange(6) == 4, 3.0, 1.0)[:, None, None]
    return noise * factor * D ** (-0.5)


def vector_rows(key, salt):
    noise = jnp.clip(jax.random.normal(jax.random.fold_in(key, salt), (5, D), jnp.float32), -4.0, 4.0)
    gain_rows = jnp.arange(5)[:, None] < 2
    return jnp.where(gain_rows, 1.0 + 0.15 * noise, 0.4 * noise)


def draw_bias_gain_params(key, part):
    return vector_rows(key, 21)


def draw_bias_gain_mean(key, part):
    return vector_rows(key, 22)


def touch_ends(values, stream_key, low, high):
    index_at = [jax.random.randint(jax.random.fold_in(stream_key, axis), (), 0, length) for axis, length in enumerate(values.shape)]
    main_axis = values.shape.index(max(values.shape))
    neighbour = index_at[:main_axis] + [(index_at[main_axis] + 1) % values.shape[main_axis]] + index_at[main_axis + 1:]
    return values.at[tuple(index_at)].set(low).at[tuple(neighbour)].set(high)


def shard_levels(rng, extent, cuts, low, largest):
    def one(dim, blocks):
        steps = jax.random.uniform(jax.random.fold_in(jax.random.fold_in(rng, 6), dim), (blocks,), jnp.float32, low / len(cuts), largest / len(cuts))
        return jnp.repeat(jnp.exp(steps), extent[dim] // blocks).reshape((-1,) + (1,) * (len(extent) - dim - 1))

    loudness = one(*cuts[0])
    for cut in cuts[1:]:
        loudness = loudness * one(*cut)
    return loudness


def profile(count, total, limit, lean):
    weights = [(1 << 20) // math.isqrt(grade ** lean) + 1 for grade in range(2, count + 1)]
    surplus, holding = total - limit - (count - 1), [1] * (count - 1)
    while surplus > 0:
        movable = [i for i in range(count - 1) if holding[i] < limit]
        whole, remaining = sum([weights[i] for i in movable]), surplus
        for i in movable:
            addition = min(limit - holding[i], max(1, remaining * weights[i] // whole), surplus)
            holding[i] = holding[i] + addition
            surplus = surplus - addition
    return np.array([limit] + holding)


def uneven(own_key, amount, total, bound, skew):
    if amount == 2:
        one = jax.random.randint(own_key, (), max(1, total - bound), min(bound, total - 1) + 1)
        return jnp.stack([one, total - one])
    lengths = jnp.asarray(profile(amount, total, bound, skew), jnp.int32)
    couples = (amount - 1) // 2
    giver, taker = lengths[1:1 + 2 * couples:2], lengths[2:2 + 2 * couples:2]
    room = jnp.minimum(giver - 1, bound - taker)
    moved = jax.random.randint(jax.random.fold_in(own_key, 1), (couples,), 0, 1 << 20) % (room + 1)
    lengths = lengths.at[1:1 + 2 * couples:2].set(giver - moved).at[2:2 + 2 * couples:2].set(taker + moved)
    return lengths[jax.random.permutation(jax.random.fold_in(own_key, 2), amount)]


def bell_draw(stream_key, shape, width, limit, split=(), held_as=jnp.bfloat16):
    entries = jax.random.normal(stream_key, shape, jnp.float32) * width
    if len(split) > 0:
        entries = shard_levels(stream_key, shape, split, -0.22, 0.18) * entries
    return jnp.clip(entries, min=-limit, max=limit).astype(held_as)


def setup_inputs(seed: int = 0) -> dict:
    arg_keys = jax.random.split(jax.random.key(seed), 20)
    return {
        "input_segments": bell_draw(arg_keys[0], (SEGMENT_NUMBER, PATCH), 1.0, 6.0, ((0, 32),), jnp.float32),
        "filler_flags": touch_ends((jax.random.randint(arg_keys[1], (SEGMENT_NUMBER, PATCH), 0, 4) < 1).astype(jnp.int32), jax.random.fold_in(arg_keys[1], 1), 0, 1),
        "sequence_owner": jnp.searchsorted(jnp.cumsum(uneven(arg_keys[2], SEGMENT_NUMBER * 4 // SEQ, SEGMENT_NUMBER, SEQ // 2, 2)), jnp.arange(SEGMENT_NUMBER), side="right").astype(jnp.int32),
        "prediction_adjoint": bell_draw(arg_keys[3], (SEGMENT_NUMBER, QUANTILE_FIELDS), 1.0, 6.0, ((0, 8), (1, 4))),
        "quadratic_params": draw_quadratic_params(jax.random.fold_in(arg_keys[19], 71), 0),
        "quadratic_velocity": bell_draw(arg_keys[5], (6, D, D), (0.5 * SEGMENT_NUMBER ** 0.5), 384.0, ((1, 32),), jnp.float32),
        "quadratic_mean": bell_draw(arg_keys[6], (6, D, D), D ** -0.5, 0.15625, ((1, 32),), jnp.float32),
        "perceptron_params": bell_draw(arg_keys[7], (2, D, FF), D ** -0.5, 0.15625, ((1, 32),), jnp.float32),
        "perceptron_velocity": bell_draw(arg_keys[8], (2, D, FF), (0.5 * SEGMENT_NUMBER ** 0.5), 384.0, ((1, 32),), jnp.float32),
        "perceptron_mean": bell_draw(arg_keys[9], (2, D, FF), D ** -0.5, 0.15625, ((1, 32),), jnp.float32),
        "embedder_params": bell_draw(arg_keys[10], (2, D, 2 * PATCH), (2 * PATCH) ** -0.5, 0.75, ((1, 32),), jnp.float32),
        "embedder_velocity": bell_draw(arg_keys[11], (2, D, 2 * PATCH), (0.5 * SEGMENT_NUMBER ** 0.5), 384.0, ((1, 32),), jnp.float32),
        "embedder_mean": bell_draw(arg_keys[12], (2, D, 2 * PATCH), (2 * PATCH) ** -0.5, 0.75, ((1, 32),), jnp.float32),
        "bias_gain_params": draw_bias_gain_params(jax.random.fold_in(arg_keys[19], 71), 0),
        "bias_gain_velocity": bell_draw(arg_keys[14], (5, D), (0.5 * SEGMENT_NUMBER ** 0.5), 384.0, ((1, 32),), jnp.float32),
        "bias_gain_mean": draw_bias_gain_mean(jax.random.fold_in(arg_keys[19], 71), 0),
        "readout_params": bell_draw(arg_keys[16], (2, D, QUANTILE_FIELDS), D ** -0.5, 0.15625, ((1, 8), (2, 4)), jnp.float32),
        "readout_velocity": bell_draw(arg_keys[17], (2, D, QUANTILE_FIELDS), (0.5 * SEGMENT_NUMBER ** 0.5), 384.0, ((1, 8), (2, 4)), jnp.float32),
        "readout_mean": bell_draw(arg_keys[18], (2, D, QUANTILE_FIELDS), D ** -0.5, 0.15625, ((1, 8), (2, 4)), jnp.float32),
    }


EPSILON = 1e-06
MOMENTUM = 0.9
AVG_DECAY = 0.9
HIGHEST = lax.Precision.HIGHEST

@jax.custom_vjp
def low(v):
    return lax.optimization_barrier(v.astype(jnp.bfloat16)).astype(jnp.float32)

@jax.custom_vjp
def low_back(v):
    return v

def low_keep(v):
    return (low(v), None)

def low_pass(kept, grad):
    return (grad,)

def back_keep(v):
    return (v, None)

def back_low(kept, grad):
    return (low(grad),)
low.defvjp(low_keep, low_pass)
low_back.defvjp(back_keep, back_low)

def product(left_mat, right_mat):
    return jnp.dot(left_mat, right_mat, precision=HIGHEST, preferred_element_type=jnp.float32)

def rms_gain(values_in, gains_in):
    return values_in * lax.rsqrt(lax.optimization_barrier(jnp.mean(values_in * values_in, axis=-1, keepdims=True)) + EPSILON) * gains_in

def rope_tables():
    half_dim = HEAD_DIM // 2
    position = jnp.arange(SEQ, dtype=jnp.float32)[:, None]
    spacing = 10000.0 ** (-jnp.arange(half_dim, dtype=jnp.float32) / half_dim)
    angles = position * spacing[None, :]
    return (jnp.cos(angles), jnp.sin(angles))

def rotate(heads_in, cosines, sines):
    half_dim = heads_in.shape[-1] // 2
    lower_half = heads_in[..., :half_dim]
    upper_half = heads_in[..., half_dim:]
    cos_rows = cosines[:, None, :]
    sin_rows = sines[:, None, :]
    return jnp.concatenate([lower_half * cos_rows - upper_half * sin_rows, upper_half * cos_rows + lower_half * sin_rows], axis=-1)

def attend_sequence(bundle):
    query_heads, key_heads, value_heads, segments = bundle
    scores = jnp.einsum('qhd,khd->hqk', query_heads, key_heads, precision=HIGHEST) * HEAD_DIM ** (-0.5)
    scores = low_back(scores)
    places = jnp.arange(SEQ)
    allowed = (places[:, None] >= places[None, :]) & (segments[:, None] == segments[None, :])
    scores = jnp.where(allowed[None], scores, -1e+30)
    weights = jax.nn.softmax(scores, axis=-1)
    mixed = jnp.einsum('hqk,khd->qhd', low(weights), value_heads, precision=HIGHEST)
    return low_back(mixed)

def group_forward(masters, group_values, group_masks, group_segments):
    square, ffn, token, vectors, readout_outcome = [low(master) for master in masters]
    tok_count = group_values.shape[0]
    seq_rows = tok_count // SEQ
    tok_input = low(jnp.concatenate([group_values * (1.0 - group_masks), group_masks], axis=-1))
    tok_pre = low_back(product(tok_input, token[0].T) + vectors[2])
    tok_act = low(jax.nn.silu(tok_pre))
    stream_in = low_back(product(tok_act, square[0]) + product(tok_input, token[1].T)) + vectors[3]
    normed_attn = low(rms_gain(stream_in, vectors[0]))
    cosines, sines = rope_tables()
    query_pre = low_back(product(normed_attn, square[1])).reshape(seq_rows, SEQ, HEADS, HEAD_DIM)
    key_pre = low_back(product(normed_attn, square[2])).reshape(seq_rows, SEQ, HEADS, HEAD_DIM)
    query_heads = low(rotate(query_pre, cosines, sines))
    key_heads = low(rotate(key_pre, cosines, sines))
    value_heads = low(low_back(product(normed_attn, square[3]))).reshape(seq_rows, SEQ, HEADS, HEAD_DIM)
    seg_rows = group_segments.reshape(seq_rows, SEQ)
    mixed = lax.map(jax.checkpoint(attend_sequence), (query_heads, key_heads, value_heads, seg_rows))
    attn_mix = low(mixed.reshape(tok_count, D))
    stream_mid = stream_in + low_back(product(attn_mix, square[4]))
    normed_ffn = low(rms_gain(stream_mid, vectors[1]))
    ffn_pre = low_back(product(normed_ffn, ffn[0]))
    ffn_act = low(jax.nn.silu(ffn_pre))
    stream_out = stream_mid + low_back(product(ffn_act, ffn[1].T))
    stream_low = low(stream_out)
    head_pre = low_back(product(stream_low, square[5]) + vectors[4])
    head_act = low(jax.nn.silu(head_pre))
    return product(head_act, readout_outcome[0]) + product(stream_low, readout_outcome[1])

def update(master, moment, average, gradient, rate):
    moment_new = MOMENTUM * moment + gradient
    master_new = master - rate * (gradient + MOMENTUM * moment_new)
    average_new = AVG_DECAY * average + (1.0 - AVG_DECAY) * master_new
    return (master_new, moment_new, average_new)

def reference(input_segments, filler_flags, sequence_owner, prediction_adjoint, quadratic_params, quadratic_velocity, quadratic_mean, perceptron_params, perceptron_velocity, perceptron_mean, embedder_params, embedder_velocity, embedder_mean, bias_gain_params, bias_gain_velocity, bias_gain_mean, readout_params, readout_velocity, readout_mean):
    masters = (quadratic_params, perceptron_params, embedder_params, bias_gain_params, readout_params)
    total_rows = SEGMENT_NUMBER // SEQ
    group_rows = math.gcd(total_rows, max(1, 4096 // SEQ))
    sequence_batch_number = total_rows // group_rows
    sequence_batch_piece = group_rows * SEQ
    all_values = input_segments.reshape(sequence_batch_number, sequence_batch_piece, PATCH)
    all_masks = filler_flags.astype(jnp.float32).reshape(sequence_batch_number, sequence_batch_piece, PATCH)
    all_segments = sequence_owner.reshape(sequence_batch_number, sequence_batch_piece)
    complete_adjoints = prediction_adjoint.astype(jnp.float32).reshape(sequence_batch_number, sequence_batch_piece, QUANTILE_FIELDS)

    def one_group(carry, bundle):
        group_values, group_masks, group_segments, group_cot = bundle

        def forward(params, inputs):
            return group_forward(params, inputs, group_masks, group_segments)
        predicted, pull = jax.vjp(forward, masters, group_values)
        grad_params, grad_values = pull(group_cot)
        carry = jax.tree.map(lambda total_grad, fresh_grad: total_grad + fresh_grad, carry, grad_params)
        return (carry, (predicted.astype(jnp.bfloat16), grad_values))
    zeros = jax.tree.map(jnp.zeros_like, masters)
    grads, final_yield = lax.scan(one_group, zeros, (all_values, all_masks, all_segments, complete_adjoints))
    prediction = final_yield[0].reshape(SEGMENT_NUMBER, QUANTILE_FIELDS)
    segment_derivative = final_yield[1].reshape(SEGMENT_NUMBER, PATCH)
    quadratic_params_fresh, quadratic_velocity_fresh, quadratic_mean_fresh = update(quadratic_params, quadratic_velocity, quadratic_mean, grads[0], 0.5 / math.sqrt(D * SEGMENT_NUMBER))
    perceptron_params_fresh, perceptron_velocity_fresh, perceptron_mean_fresh = update(perceptron_params, perceptron_velocity, perceptron_mean, grads[1], 0.5 / math.sqrt(D * SEGMENT_NUMBER))
    embedder_params_fresh, embedder_velocity_fresh, embedder_mean_fresh = update(embedder_params, embedder_velocity, embedder_mean, grads[2], 0.5 / math.sqrt(2 * PATCH * SEGMENT_NUMBER))
    bias_gain_params_fresh, bias_gain_velocity_fresh, bias_gain_mean_fresh = update(bias_gain_params, bias_gain_velocity, bias_gain_mean, grads[3], 0.3 / math.sqrt(SEGMENT_NUMBER))
    readout_params_fresh, readout_velocity_fresh, readout_mean_fresh = update(readout_params, readout_velocity, readout_mean, grads[4], 0.5 / math.sqrt(D * SEGMENT_NUMBER))
    return (prediction, segment_derivative, quadratic_params_fresh, quadratic_velocity_fresh, quadratic_mean_fresh, perceptron_params_fresh, perceptron_velocity_fresh, perceptron_mean_fresh, embedder_params_fresh, embedder_velocity_fresh, embedder_mean_fresh, bias_gain_params_fresh, bias_gain_velocity_fresh, bias_gain_mean_fresh, readout_params_fresh, readout_velocity_fresh, readout_mean_fresh)
```

```python
import functools
import jax, jax.numpy as jnp
from jax import lax
from jax.experimental import pallas as pl
from jax.experimental.pallas import tpu as pltpu
from jax.sharding import PartitionSpec as P

MESH = pl.DeviceIdType.MESH
ROWS = 40

def place():
    dp, hd = lax.axis_index("dp"), lax.axis_index("head")
    return dp // 2, dp % 2, hd // 2, hd % 2

def device(z, x, y, c):
    return (z * 2 + x, y * 2 + c)

def partners(z, x, y, c):
    found = [device((z + d) % 4, x, y, c) for d in (1, 2, 3)]
    return found + [device(z, 1 - x, y, c), device(z, x, 1 - y, c), device(z, x, y, 1 - c)]

def meet(z, x, y, c):
    barrier = pltpu.get_barrier_semaphore()
    for partner in partners(z, x, y, c):
        pl.semaphore_signal(barrier, inc=1, device_id=partner, device_id_type=MESH)
    pl.semaphore_wait(barrier, 6)

def gather_kernel(pieces, count, *refs):
    shards, full = refs[:count], refs[count:2 * count]
    own_sem, send_z, recv_z, send_b, recv_b, send_s, recv_s = refs[2 * count:]
    z, x, y, c = place()
    meet(z, x, y, c)
    n = len(pieces)

    def remote(src, dst, send, recv, where):
        return pltpu.make_async_remote_copy(
            src_ref=src, dst_ref=dst, send_sem=send, recv_sem=recv, device_id=where, device_id_type=MESH)

    own, along_z, second, third, sibling = [], [], [], [], []
    for k, (j, start, width) in enumerate(pieces):
        cols = pl.ds(start, width)
        first, last = pl.ds(start, width // 2), pl.ds(start + width // 2, width // 2)
        home, shard = full[j], shards[j]
        own.append(pltpu.make_async_copy(shard.at[:, cols], home.at[z, x, y, c, :, cols], own_sem.at[k]))
        along_z.append([remote(shard.at[:, cols], home.at[z, x, y, c, :, cols], send_z.at[k, d - 1],
                               recv_z.at[k, d - 1], device((z + d) % 4, x, y, c)) for d in (1, 2, 3)])
        a, b = home.at[:, x, y, c, :, first], home.at[:, x, y, c, :, last]
        second.append([remote(a, a, send_b.at[k, 0], recv_b.at[k, 0], device(z, x, 1 - y, c)),
                       remote(b, b, send_b.at[k, 1], recv_b.at[k, 1], device(z, 1 - x, y, c))])
        a, b = home.at[:, x, :, c, :, first], home.at[:, :, y, c, :, last]
        third.append([remote(a, a, send_b.at[k, 2], recv_b.at[k, 2], device(z, 1 - x, y, c)),
                      remote(b, b, send_b.at[k, 3], recv_b.at[k, 3], device(z, x, 1 - y, c))])
        a = home.at[:, :, :, c, :, cols]
        sibling.append(remote(a, a, send_s.at[k], recv_s.at[k], device(z, x, y, 1 - c)))
    ahead = 4
    for t in range(-ahead, n + 2):
        k = t + ahead
        if k < n:
            for copy in along_z[k]:
                copy.start()
            own[k].start()
        if 0 <= t < n:
            own[t].wait()
            for copy in along_z[t]:
                copy.wait_recv()
            for copy in second[t]:
                copy.start()
        k = t - 1
        if 0 <= k < n:
            for copy in second[k]:
                copy.wait_recv()
            for copy in third[k]:
                copy.start()
        k = t - 2
        if 0 <= k < n:
            for copy in third[k]:
                copy.wait_recv()
            sibling[k].start()
    for k in range(n):
        sibling[k].wait_recv()
        for copy in along_z[k] + second[k] + third[k] + [sibling[k]]:
            copy.wait_send()

def gather(shards, step=1280, cid=1):
    count = len(shards)
    pieces = []
    for j, shard in enumerate(shards):
        width = shard.shape[1]
        s = step if width % step == 0 else width
        pieces += [(j, start, s) for start in range(0, width, s)]
    n = len(pieces)
    total = sum(s.shape[1] for s in shards)
    dma = pltpu.SemaphoreType.DMA
    full = pl.pallas_call(
        functools.partial(gather_kernel, tuple(pieces), count),
        out_shape=[jax.ShapeDtypeStruct((4, 2, 2, 2, ROWS, s.shape[1]), jnp.bfloat16) for s in shards],
        in_specs=[pl.BlockSpec(memory_space=pltpu.VMEM)] * count,
        out_specs=[pl.BlockSpec(memory_space=pl.ANY)] * count,
        scratch_shapes=[dma((n,)), dma((n, 3)), dma((n, 3)), dma((n, 4)), dma((n, 4)), dma((n,)), dma((n,))],
        compiler_params=pltpu.CompilerParams(collective_id=cid, has_side_effects=True),
        name="gather_weights",
    )(*shards)
    return [f.reshape(32 * ROWS, f.shape[-1]) for f in full]


RING = 3

def reduce_kernel(pieces, lefts_n, rights_n, n, width, small_width, *refs):
    lefts, rights, small = refs[:lefts_n], refs[lefts_n:lefts_n + rights_n], refs[lefts_n + rights_n]
    refs = refs[lefts_n + rights_n + 1:]
    out, small_out = refs[:2]
    left_buf, right_buf, load_sem = refs[2:5]
    main_bufs, small_bufs = refs[5:5 + 17], refs[5 + 17:5 + 34]
    z, x, y, c = place()
    meet(z, x, y, c)
    f32, low = jnp.float32, jnp.bfloat16

    def lane(bufs, ring, total, columns):
        out_s, kept, in_s, in_a, in_b, sum_a, sum_b, in_c, in_d, last, in_z, s_sem, p_sem, q_sem, z_sem, credit, credit_z = bufs
        half = columns // 2
        front, back = pl.ds(0, half), pl.ds(half, half)
        to_x, to_y, to_c = device(z, 1 - x, y, c), device(z, x, 1 - y, c), device(z, x, y, 1 - c)

        def remote(src, dst, sems, where):
            return pltpu.make_async_remote_copy(
                src_ref=src, dst_ref=dst, send_sem=sems[0], recv_sem=sems[1], device_id=where, device_id_type=MESH)

        def sibling(k):
            s = k % ring
            return remote(out_s.at[s], in_s.at[s], (s_sem.at[s, 0], s_sem.at[s, 1]), to_c)

        def first(k):
            s = k % ring
            return (remote(kept.at[s, :, :, 1 - y, :, front], in_a.at[s], (p_sem.at[s, 0], p_sem.at[s, 1]), to_y),
                    remote(kept.at[s, :, 1 - x, :, :, back], in_b.at[s], (p_sem.at[s, 2], p_sem.at[s, 3]), to_x))

        def second(k):
            s = k % ring
            return (remote(sum_a.at[s, :, 1 - x], in_c.at[s], (q_sem.at[s, 0], q_sem.at[s, 1]), to_x),
                    remote(sum_b.at[s, :, 1 - y], in_d.at[s], (q_sem.at[s, 2], q_sem.at[s, 3]), to_y))

        def third(k):
            s = k % ring
            return tuple(remote(last.at[s, (z + d) % 4], in_z.at[s, d - 1], (z_sem.at[s, d - 1], z_sem.at[s, d + 2]),
                                device((z + d) % 4, x, y, c)) for d in (1, 2, 3))

        def give(index, k, where):
            @pl.when(k + ring < total)
            def _():
                pl.semaphore_signal(credit.at[index], inc=1, device_id=where, device_id_type=MESH)

        def take(ref, k):
            @pl.when(k >= ring)
            def _():
                pl.semaphore_wait(ref, 1)

        def reuse(k, copies):
            @pl.when(k >= ring)
            def _():
                for copy in copies(k - ring):
                    copy.wait_send()

        def add(left, right):
            return (left.astype(f32) + right.astype(f32)).astype(low)

        def send_sibling(k):
            take(credit.at[0], k)
            sibling(k).start()

        def stage_one(k):
            s = k % ring
            sibling(k).wait_recv()

            def body(i, carry):
                kept[s, i] = add(kept[s, i], in_s[s, i])
                return carry
            lax.fori_loop(0, 4, body, 0)
            give(0, k, to_c)
            take(credit.at[1], k)
            take(credit.at[2], k)
            for copy in first(k):
                copy.start()

        def stage_two(k):
            s = k % ring
            reuse(k, second)
            for copy in first(k):
                copy.wait_recv()

            def body(i, carry):
                for j in range(2):
                    sum_a[s, i, j] = add(kept[s, i, j, y, :, :half], in_a[s, i, j])
                    sum_b[s, i, j] = add(kept[s, i, x, j, :, half:], in_b[s, i, j])
                return carry
            lax.fori_loop(0, 4, body, 0)
            give(1, k, to_y)
            give(2, k, to_x)
            take(credit.at[3], k)
            take(credit.at[4], k)
            for copy in second(k):
                copy.start()

        def stage_three(k):
            s = k % ring
            reuse(k, third)
            for copy in second(k):
                copy.wait_recv()

            def body(i, carry):
                last[s, i, :, :half] = add(sum_a[s, i, x], in_c[s, i])
                last[s, i, :, half:] = add(sum_b[s, i, y], in_d[s, i])
                return carry
            lax.fori_loop(0, 4, body, 0)
            give(3, k, to_x)
            give(4, k, to_y)
            for d in (1, 2, 3):
                take(credit_z.at[d - 1], k)
            for copy in third(k):
                copy.start()

        def stage_four(k, target):
            s = k % ring
            for copy in third(k):
                copy.wait_recv()
            value = last[s, z].astype(f32)
            for d in (1, 2, 3):
                value = value + in_z[s, d - 1].astype(f32)
            target[...] = value
            for d in (1, 2, 3):
                @pl.when(k + ring < total)
                def _():
                    pl.semaphore_signal(credit_z.at[d - 1], inc=1, device_id=device((z + 4 - d) % 4, x, y, c), device_id_type=MESH)

        def drain(k):
            for copies in ((sibling(k),), first(k), second(k), third(k)):
                for copy in copies:
                    copy.wait_send()

        def fresh(k):
            reuse(k, lambda j: (sibling(j),) + first(j))

        return fresh, send_sibling, stage_one, stage_two, stage_three, stage_four, drain

    fresh, send_sibling, one, two, three, four, drain = lane(main_bufs, RING, n, width)
    _, small_sibling, small_one, small_two, small_three, small_four, small_drain = lane(small_bufs, 1, 1, small_width)
    out_s, kept = main_bufs[:2]
    small_s, small_kept = small_bufs[:2]

    def load(k, start):
        for number, (i, j, begin) in enumerate(pieces):
            @pl.when(k == number)
            def _():
                s = number % 2
                for copy in (pltpu.make_async_copy(lefts[i], left_buf.at[s], load_sem.at[s, 0]),
                             pltpu.make_async_copy(rights[j].at[:, pl.ds(begin, width)], right_buf.at[s], load_sem.at[s, 1])):
                    copy.start() if start else copy.wait()

    def multiply(k, parity, target):
        tile = 256

        def body(j, carry):
            cols = pl.ds(pl.multiple_of(j * tile, tile), tile)
            value = jnp.dot(left_buf[k % 2, parity], right_buf[k % 2, :, cols], preferred_element_type=f32)
            for i in range(16):
                target[k % RING, i // 4, (i // 2) % 2, i % 2, :, cols] = value[i * ROWS:(i + 1) * ROWS].astype(low)
            return carry
        lax.fori_loop(0, width // tile, body, 0)

    load(0, True)
    small_s[0] = small[1 - c]
    small_kept[0] = small[c]

    def step(t, carry):
        @pl.when(t < n)
        def _():
            load(t + 1, True)
            load(t, False)
            fresh(t)
            multiply(t, 1 - c, out_s)
            send_sibling(t)
            multiply(t, c, kept)
        for j, work in enumerate((lambda: small_sibling(0), lambda: small_one(0), lambda: small_two(0),
                                  lambda: small_three(0), lambda: small_four(0, small_out))):
            @pl.when(t == j)
            def _():
                work()
        for lag, work in ((1, one), (2, two), (3, three)):
            @pl.when((t >= lag) & (t < n + lag))
            def _():
                work(t - lag)

        @pl.when(t >= 4)
        def _():
            four(t - 4, out.at[t - 4])
        return carry
    lax.fori_loop(0, n + 4, step, 0)
    for k in range(n - RING, n):
        drain(k)
    small_drain(0)

def buffers(ring, columns):
    dma, reg = pltpu.SemaphoreType.DMA, pltpu.SemaphoreType.REGULAR
    half, low = columns // 2, jnp.bfloat16
    block = [pltpu.VMEM((ring, 4, 2, 2, ROWS, columns), low)] * 3
    halves = [pltpu.VMEM((ring, 4, 2, ROWS, half), low)] * 4
    quarters = [pltpu.VMEM((ring, 4, ROWS, half), low)] * 2
    ends = [pltpu.VMEM((ring, 4, ROWS, columns), low), pltpu.VMEM((ring, 3, ROWS, columns), low)]
    return block + halves + quarters + ends + [dma((ring, 2)), dma((ring, 4)), dma((ring, 4)), dma((ring, 6)), reg((5,)), reg((3,))]

def turned(value):
    tokens = value.shape[0]
    return value.T.reshape(16, 2, ROWS, tokens).swapaxes(0, 1).reshape(2, 16 * ROWS, tokens)

def reduce_products(lefts, rights, pieces, small, width=1280, cid=2):
    n = len(pieces)
    small_width = small.shape[-1]
    tokens = rights[0].shape[0]
    hbm, vmem = pl.BlockSpec(memory_space=pl.ANY), pl.BlockSpec(memory_space=pltpu.VMEM)
    return pl.pallas_call(
        functools.partial(reduce_kernel, tuple(pieces), len(lefts), len(rights), n, width, small_width),
        out_shape=[jax.ShapeDtypeStruct((n, ROWS, width), jnp.float32), jax.ShapeDtypeStruct((ROWS, small_width), jnp.float32)],
        in_specs=[hbm] * (len(lefts) + len(rights)) + [vmem],
        out_specs=[vmem, vmem],
        scratch_shapes=[pltpu.VMEM((2, 2, 16 * ROWS, tokens), jnp.bfloat16), pltpu.VMEM((2, tokens, width), jnp.bfloat16),
                        pltpu.SemaphoreType.DMA((2, 2))] + buffers(RING, width) + buffers(1, small_width),
        compiler_params=pltpu.CompilerParams(collective_id=cid, has_side_effects=True, vmem_limit_bytes=60 * 1024 * 1024),
        name="reduce_products",
    )(*lefts, *rights, small)

D = 1280
HEADS = 16
HEAD_DIM = 80
PATCH = 32
SEQ = 512


EPSILON = 1e-06
MOMENTUM = 0.9
AVG_DECAY = 0.9


def matrix_multiply(left_mat, right_mat):
    return jnp.dot(left_mat, right_mat, preferred_element_type=jnp.float32)


def flipped_bilinear(left_mat, right_mat):
    return lax.dot_general(
        left_mat, right_mat, (((1,), (1,)), ((), ())), preferred_element_type=jnp.float32
    )


def bilinear_flipped(left_mat, right_mat):
    return lax.dot_general(
        left_mat, right_mat, (((0,), (0,)), ((), ())), preferred_element_type=jnp.float32
    )


def rounded(values_in):
    return values_in.astype(jnp.bfloat16)


def rms_gain(values_in, gains_in):
    return (
        values_in
        * lax.rsqrt(jnp.mean(values_in * values_in, axis=-1, keepdims=True) + EPSILON)
        * gains_in
    )


def silu_slope(values_in):
    logistic = jax.nn.sigmoid(values_in)
    return logistic * (1.0 + values_in * (1.0 - logistic))


def rope_tables():
    half_dim = HEAD_DIM // 2
    position = jnp.arange(SEQ, dtype=jnp.float32)[:, None]
    spacing = 10000.0 ** (-jnp.arange(half_dim, dtype=jnp.float32) / half_dim)
    angles = position * spacing[None, :]
    return (jnp.cos(angles), jnp.sin(angles))


def rotate(heads_in, cosines, sines):
    half_dim = heads_in.shape[-1] // 2
    lower_half = heads_in[..., :half_dim]
    upper_half = heads_in[..., half_dim:]
    cos_rows = cosines[:, None, :]
    sin_rows = sines[:, None, :]
    return jnp.concatenate(
        [
            lower_half * cos_rows - upper_half * sin_rows,
            upper_half * cos_rows + lower_half * sin_rows,
        ],
        axis=-1,
    )


def masked_scores(query_heads, key_heads, segments):
    scores = jnp.einsum(
        "qhd,khd->hqk", query_heads, key_heads, preferred_element_type=jnp.float32
    ) * HEAD_DIM ** (-0.5)
    places = jnp.arange(SEQ)
    allowed = (places[:, None] >= places[None, :]) & (segments[:, None] == segments[None, :])
    return jnp.where(allowed[None], scores, -1e30)


def attend(bundle):
    query_heads, key_heads, value_heads, segments = bundle
    scores = masked_scores(query_heads, key_heads, segments)
    row_max = jnp.max(scores, axis=-1, keepdims=True)
    expo = jnp.exp(scores - row_max)
    row_total = jnp.sum(expo, axis=-1, keepdims=True)
    probability = expo / row_total
    mixed = jnp.einsum(
        "hqk,khd->qhd", rounded(probability), value_heads, preferred_element_type=jnp.float32
    )
    return (rounded(mixed), (row_max + jnp.log(row_total))[..., 0])


def attend_back(bundle):
    query_heads, key_heads, value_heads, segments, log_totals, grad_mixed = bundle
    scores = masked_scores(query_heads, key_heads, segments)
    probability = jnp.exp(scores - log_totals[..., None])
    grad_probs = jnp.einsum(
        "qhd,khd->hqk", grad_mixed, value_heads, preferred_element_type=jnp.float32
    )
    grad_values = jnp.einsum(
        "hqk,qhd->khd", rounded(probability), grad_mixed, preferred_element_type=jnp.float32
    )
    inner_sum = jnp.sum(probability * grad_probs, axis=-1, keepdims=True)
    grad_scores = rounded(probability * (grad_probs - inner_sum))
    grad_queries = jnp.einsum(
        "hqk,khd->qhd", grad_scores, key_heads, preferred_element_type=jnp.float32
    ) * HEAD_DIM ** (-0.5)
    grad_keys = jnp.einsum(
        "hqk,qhd->khd", grad_scores, query_heads, preferred_element_type=jnp.float32
    ) * HEAD_DIM ** (-0.5)
    return (grad_queries, grad_keys, grad_values)


def update(master, moment, average, gradient, rate):
    moment_new = MOMENTUM * moment + gradient
    master_new = master - rate * (gradient + MOMENTUM * moment_new)
    average_new = AVG_DECAY * average + (1.0 - AVG_DECAY) * master_new
    return (master_new, moment_new, average_new)


EVERYONE = ("dp", "head")


def summed(partial):
    return lax.psum_scatter(rounded(partial), EVERYONE, scatter_dimension=0, tiled=True).astype(
        jnp.float32
    )


def owned(values):
    return values.reshape(16, 2, ROWS, -1).swapaxes(0, 1).reshape(2, 4, 2, 2, ROWS, -1)


def on_device(
    input_segments,
    filler_flags,
    sequence_owner,
    prediction_adjoint,
    quadratic_params,
    quadratic_velocity,
    quadratic_mean,
    perceptron_params,
    perceptron_velocity,
    perceptron_mean,
    embedder_params,
    embedder_velocity,
    embedder_mean,
    bias_gain_params,
    bias_gain_velocity,
    bias_gain_mean,
    readout_params,
    readout_velocity,
    readout_mean,
):
    dp_size, head_size = lax.axis_size("dp"), lax.axis_size("head")
    low_square, low_ffn = rounded(quadratic_params), rounded(perceptron_params)
    low_token, low_readout = rounded(embedder_params), rounded(readout_params)
    vector_columns = jnp.pad(rounded(bias_gain_params).T, ((0, 0), (0, 123)))
    own_readout = lax.all_to_all(low_readout, "head", split_axis=1, concat_axis=2, tiled=True)
    adjoint = lax.all_to_all(prediction_adjoint, "head", split_axis=0, concat_axis=1, tiled=True)
    shards = [
        jnp.concatenate([low_square[0], low_token[0], low_token[1], vector_columns], axis=1),
        jnp.concatenate([low_square[1], low_square[2], low_square[3]], axis=1),
        low_square[4],
        low_ffn[0],
        low_ffn[1],
        low_square[5],
        own_readout[0],
        own_readout[1],
    ]
    fast = (dp_size, head_size) == (8, 4) and input_segments.shape[0] == SEQ
    first, qkv_w, attn_out_w, up_w, down_w, hidden_w, readout_w, shortcut_w = (
        gather(shards) if fast else [lax.all_gather(s, EVERYONE, axis=0, tiled=True) for s in shards]
    )
    tok_out_w, tok_hidden_w, tok_skip_w = first[:, :D], first[:, D : D + 64], first[:, D + 64 : D + 128]
    vectors = first[:, D + 128 : D + 133].T.astype(jnp.float32)

    tok_count = input_segments.shape[0]
    seq_rows = tok_count // SEQ
    mask_float = filler_flags.astype(jnp.float32)
    tok_input = rounded(jnp.concatenate([input_segments * (1.0 - mask_float), mask_float], axis=1))
    tok_pre = flipped_bilinear(tok_input, tok_hidden_w) + vectors[2]
    tok_act = rounded(jax.nn.silu(tok_pre))
    stream_in = (
        matrix_multiply(tok_act, tok_out_w) + flipped_bilinear(tok_input, tok_skip_w) + vectors[3]
    )
    normed_one, norm_pull_one = jax.vjp(rms_gain, stream_in, vectors[0])
    normed_attn = rounded(normed_one)
    cosines, sines = rope_tables()
    qkv = matrix_multiply(normed_attn, qkv_w)
    query_heads = rounded(
        rotate(qkv[:, :D].reshape(seq_rows, SEQ, HEADS, HEAD_DIM), cosines, sines)
    )
    key_heads = rounded(
        rotate(qkv[:, D : 2 * D].reshape(seq_rows, SEQ, HEADS, HEAD_DIM), cosines, sines)
    )
    value_heads = rounded(qkv[:, 2 * D :]).reshape(seq_rows, SEQ, HEADS, HEAD_DIM)
    seg_rows = sequence_owner.reshape(seq_rows, SEQ)
    mixed, log_totals = lax.map(attend, (query_heads, key_heads, value_heads, seg_rows))
    attn_mix = mixed.reshape(tok_count, D)
    stream_mid = stream_in + matrix_multiply(attn_mix, attn_out_w)
    normed_two, norm_pull_two = jax.vjp(rms_gain, stream_mid, vectors[1])
    normed_ffn = rounded(normed_two)
    ffn_pre = matrix_multiply(normed_ffn, up_w)
    ffn_act = rounded(jax.nn.silu(ffn_pre))
    stream_out = stream_mid + flipped_bilinear(ffn_act, down_w)
    stream_low = rounded(stream_out)
    head_pre = matrix_multiply(stream_low, hidden_w) + vectors[4]
    head_act = rounded(jax.nn.silu(head_pre))
    own_prediction = rounded(
        matrix_multiply(head_act, readout_w) + matrix_multiply(stream_low, shortcut_w)
    )
    prediction = lax.all_to_all(own_prediction, "head", split_axis=1, concat_axis=0, tiled=True)

    grad_head_act = flipped_bilinear(adjoint, readout_w)
    grad_skip = flipped_bilinear(adjoint, shortcut_w)
    grad_head_pre = rounded(grad_head_act * silu_slope(head_pre))
    grad_bias_head = jnp.sum(grad_head_pre.astype(jnp.float32), axis=0)
    grad_stream_out = grad_skip + flipped_bilinear(grad_head_pre, hidden_w)
    grad_ffn_out = rounded(grad_stream_out)
    grad_ffn_pre = rounded(matrix_multiply(grad_ffn_out, down_w) * silu_slope(ffn_pre))
    grad_stream_norm, grad_gain_two = norm_pull_two(flipped_bilinear(grad_ffn_pre, up_w))
    grad_stream_mid = grad_stream_out + grad_stream_norm
    grad_attn_out = rounded(grad_stream_mid)
    grad_attn_mix = rounded(flipped_bilinear(grad_attn_out, attn_out_w)).reshape(
        seq_rows, SEQ, HEADS, HEAD_DIM
    )
    grad_queries, grad_keys, grad_values = lax.map(
        attend_back, (query_heads, key_heads, value_heads, seg_rows, log_totals, grad_attn_mix)
    )
    grad_qkv_pre = jnp.concatenate(
        [
            rounded(rotate(grad_queries, cosines, -sines).reshape(tok_count, D)),
            rounded(rotate(grad_keys, cosines, -sines).reshape(tok_count, D)),
            rounded(grad_values.reshape(tok_count, D)),
        ],
        axis=1,
    )
    grad_normed = flipped_bilinear(grad_qkv_pre, qkv_w)
    grad_stream_first, grad_gain_one = norm_pull_one(grad_normed)
    grad_stream_in = grad_stream_mid + grad_stream_first
    grad_bias_out = jnp.sum(grad_stream_in, axis=0)
    grad_tok_out = rounded(grad_stream_in)
    grad_skip_tok = bilinear_flipped(grad_tok_out, tok_input)
    grad_tok_pre = rounded(flipped_bilinear(grad_tok_out, tok_out_w) * silu_slope(tok_pre))
    grad_bias_tok = jnp.sum(grad_tok_pre.astype(jnp.float32), axis=0)
    grad_hidden_tok = bilinear_flipped(grad_tok_pre, tok_input)
    grad_input = matrix_multiply(grad_tok_out, tok_skip_w) + matrix_multiply(
        grad_tok_pre, tok_hidden_w
    )
    segment_derivative = grad_input[:, :PATCH] * (1.0 - mask_float)
    grad_vector = jnp.stack(
        [grad_gain_one, grad_gain_two, grad_bias_tok, grad_bias_out, grad_bias_head], axis=1
    )
    small = rounded(
        jnp.concatenate([grad_hidden_tok, grad_skip_tok, jnp.pad(grad_vector, ((0, 0), (0, 123)))], axis=1)
    )
    wide = ffn_act.shape[1] // D
    pieces = [(0, 0, 0), (1, 0, 0), (1, 1, 0)]
    pieces += [(2, 2, D * j) for j in range(wide)] + [(3, 3, D * j) for j in range(wide)]
    pieces += [(4, 4, 0)] + [(5, 5, D * j) for j in range(3)] + [(6, 6, 0)]
    lefts = [head_act, stream_low, grad_ffn_out, normed_ffn, attn_mix, normed_attn, tok_act]
    rights = [adjoint, grad_head_pre, ffn_act, grad_ffn_pre, grad_attn_out, grad_qkv_pre, grad_tok_out]
    if fast:
        shares, small_share = reduce_products([turned(v) for v in lefts], rights, pieces, owned(small))
    else:
        shares = [
            summed(bilinear_flipped(lefts[i], rights[j][:, start : start + D])) for i, j, start in pieces
        ]
        small_share = summed(small)
    head_share = lax.all_to_all(
        jnp.stack([shares[0], shares[1]]), "head", split_axis=2, concat_axis=1, tiled=True
    )
    down_at = 3
    up_at = down_at + wide
    wo_at = up_at + wide
    square_share = jnp.stack(
        [shares[wo_at + 4], shares[wo_at + 1], shares[wo_at + 2], shares[wo_at + 3], shares[wo_at], shares[2]]
    )
    ffn_share = jnp.stack(
        [
            jnp.concatenate([shares[up_at + j] for j in range(wide)], axis=1),
            jnp.concatenate([shares[down_at + j] for j in range(wide)], axis=1),
        ]
    )
    token_share = jnp.stack([small_share[:, :64], small_share[:, 64:128]])
    vector_share = small_share[:, 128:133].T
    all_tokens = tok_count * lax.axis_size("dp") * lax.axis_size("head")
    matrix_rate = 0.5 / (D * all_tokens) ** 0.5
    quadratic_params_fresh, quadratic_velocity_fresh, quadratic_mean_fresh = update(
        quadratic_params, quadratic_velocity, quadratic_mean, square_share, matrix_rate
    )
    perceptron_params_fresh, perceptron_velocity_fresh, perceptron_mean_fresh = update(
        perceptron_params, perceptron_velocity, perceptron_mean, ffn_share, matrix_rate
    )
    embedder_params_fresh, embedder_velocity_fresh, embedder_mean_fresh = update(
        embedder_params,
        embedder_velocity,
        embedder_mean,
        token_share,
        0.5 / (2 * PATCH * all_tokens) ** 0.5,
    )
    bias_gain_params_fresh, bias_gain_velocity_fresh, bias_gain_mean_fresh = update(
        bias_gain_params, bias_gain_velocity, bias_gain_mean, vector_share, 0.3 / all_tokens**0.5
    )
    readout_params_fresh, readout_velocity_fresh, readout_mean_fresh = update(
        readout_params, readout_velocity, readout_mean, head_share, matrix_rate
    )
    return (
        prediction,
        segment_derivative,
        quadratic_params_fresh,
        quadratic_velocity_fresh,
        quadratic_mean_fresh,
        perceptron_params_fresh,
        perceptron_velocity_fresh,
        perceptron_mean_fresh,
        embedder_params_fresh,
        embedder_velocity_fresh,
        embedder_mean_fresh,
        bias_gain_params_fresh,
        bias_gain_velocity_fresh,
        bias_gain_mean_fresh,
        readout_params_fresh,
        readout_velocity_fresh,
        readout_mean_fresh,
    )


def solution(mesh):
    placed = (
        P(("dp", "head"), None),
        P(("dp", "head"), None),
        P(("dp", "head")),
        P("dp", "head"),
        P(None, ("dp", "head"), None),
        P(None, ("dp", "head"), None),
        P(None, ("dp", "head"), None),
        P(None, ("dp", "head"), None),
        P(None, ("dp", "head"), None),
        P(None, ("dp", "head"), None),
        P(None, ("dp", "head"), None),
        P(None, ("dp", "head"), None),
        P(None, ("dp", "head"), None),
        P(None, ("dp", "head")),
        P(None, ("dp", "head")),
        P(None, ("dp", "head")),
        P(None, "dp", "head"),
        P(None, "dp", "head"),
        P(None, "dp", "head"),
    )
    return jax.shard_map(
        on_device,
        mesh=mesh,
        in_specs=placed,
        out_specs=(
            P("dp", "head"),
            P(("dp", "head"), None),
            P(None, ("dp", "head"), None),
            P(None, ("dp", "head"), None),
            P(None, ("dp", "head"), None),
            P(None, ("dp", "head"), None),
            P(None, ("dp", "head"), None),
            P(None, ("dp", "head"), None),
            P(None, ("dp", "head"), None),
            P(None, ("dp", "head"), None),
            P(None, ("dp", "head"), None),
            P(None, ("dp", "head")),
            P(None, ("dp", "head")),
            P(None, ("dp", "head")),
            P(None, "dp", "head"),
            P(None, "dp", "head"),
            P(None, "dp", "head"),
        ),
        check_vma=False,
    )
```

```python
import functools
import jax, jax.numpy as jnp
from jax import lax
from jax.experimental import pallas as pl
from jax.experimental.pallas import tpu as pltpu
from jax.sharding import PartitionSpec as P

MESH = pl.DeviceIdType.MESH
ROWS = 40

def place():
    dp, hd = lax.axis_index("dp"), lax.axis_index("head")
    return dp // 2, dp % 2, hd // 2, hd % 2

def device(z, x, y, c):
    return (z * 2 + x, y * 2 + c)

def partners(z, x, y, c):
    found = [device((z + d) % 4, x, y, c) for d in (1, 2, 3)]
    return found + [device(z, 1 - x, y, c), device(z, x, 1 - y, c), device(z, x, y, 1 - c)]

def meet(z, x, y, c):
    barrier = pltpu.get_barrier_semaphore()
    for partner in partners(z, x, y, c):
        pl.semaphore_signal(barrier, inc=1, device_id=partner, device_id_type=MESH)
    pl.semaphore_wait(barrier, 6)

def gather_kernel(pieces, count, *refs):
    shards, full = refs[:count], refs[count:2 * count]
    own_sem, send_z, recv_z, send_b, recv_b, send_s, recv_s = refs[2 * count:]
    z, x, y, c = place()
    meet(z, x, y, c)
    n = len(pieces)

    def remote(src, dst, send, recv, where):
        return pltpu.make_async_remote_copy(
            src_ref=src, dst_ref=dst, send_sem=send, recv_sem=recv, device_id=where, device_id_type=MESH)

    own, along_z, second, third, sibling = [], [], [], [], []
    for k, (j, start, width) in enumerate(pieces):
        cols = pl.ds(start, width)
        first, last = pl.ds(start, width // 2), pl.ds(start + width // 2, width // 2)
        home, shard = full[j], shards[j]
        own.append(pltpu.make_async_copy(shard.at[:, cols], home.at[z, x, y, c, :, cols], own_sem.at[k]))
        along_z.append([remote(shard.at[:, cols], home.at[z, x, y, c, :, cols], send_z.at[k, d - 1],
                               recv_z.at[k, d - 1], device((z + d) % 4, x, y, c)) for d in (1, 2, 3)])
        a, b = home.at[:, x, y, c, :, first], home.at[:, x, y, c, :, last]
        second.append([remote(a, a, send_b.at[k, 0], recv_b.at[k, 0], device(z, x, 1 - y, c)),
                       remote(b, b, send_b.at[k, 1], recv_b.at[k, 1], device(z, 1 - x, y, c))])
        a, b = home.at[:, x, :, c, :, first], home.at[:, :, y, c, :, last]
        third.append([remote(a, a, send_b.at[k, 2], recv_b.at[k, 2], device(z, 1 - x, y, c)),
                      remote(b, b, send_b.at[k, 3], recv_b.at[k, 3], device(z, x, 1 - y, c))])
        a = home.at[:, :, :, c, :, cols]
        sibling.append(remote(a, a, send_s.at[k], recv_s.at[k], device(z, x, y, 1 - c)))
    ahead = 4
    for t in range(-ahead, n + 2):
        k = t + ahead
        if k < n:
            for copy in along_z[k]:
                copy.start()
            own[k].start()
        if 0 <= t < n:
            own[t].wait()
            for copy in along_z[t]:
                copy.wait_recv()
            for copy in second[t]:
                copy.start()
        k = t - 1
        if 0 <= k < n:
            for copy in second[k]:
                copy.wait_recv()
            for copy in third[k]:
                copy.start()
        k = t - 2
        if 0 <= k < n:
            for copy in third[k]:
                copy.wait_recv()
            sibling[k].start()
    for k in range(n):
        sibling[k].wait_recv()
        for copy in along_z[k] + second[k] + third[k] + [sibling[k]]:
            copy.wait_send()

def gather(shards, step=1280, cid=1):
    count = len(shards)
    pieces = []
    for j, shard in enumerate(shards):
        width = shard.shape[1]
        s = step if width % step == 0 else width
        pieces += [(j, start, s) for start in range(0, width, s)]
    n = len(pieces)
    total = sum(s.shape[1] for s in shards)
    dma = pltpu.SemaphoreType.DMA
    full = pl.pallas_call(
        functools.partial(gather_kernel, tuple(pieces), count),
        out_shape=[jax.ShapeDtypeStruct((4, 2, 2, 2, ROWS, s.shape[1]), jnp.bfloat16) for s in shards],
        in_specs=[pl.BlockSpec(memory_space=pltpu.VMEM)] * count,
        out_specs=[pl.BlockSpec(memory_space=pl.ANY)] * count,
        scratch_shapes=[dma((n,)), dma((n, 3)), dma((n, 3)), dma((n, 4)), dma((n, 4)), dma((n,)), dma((n,))],
        compiler_params=pltpu.CompilerParams(collective_id=cid, has_side_effects=True),
        name="gather_weights",
    )(*shards)
    return [f.reshape(32 * ROWS, f.shape[-1]) for f in full]


RING = 3

def reduce_kernel(pieces, lefts_n, rights_n, n, width, small_width, *refs):
    lefts, rights, small = refs[:lefts_n], refs[lefts_n:lefts_n + rights_n], refs[lefts_n + rights_n]
    refs = refs[lefts_n + rights_n + 1:]
    out, small_out = refs[:2]
    left_buf, right_buf, load_sem = refs[2:5]
    main_bufs, small_bufs = refs[5:5 + 17], refs[5 + 17:5 + 34]
    z, x, y, c = place()
    meet(z, x, y, c)
    f32, low = jnp.float32, jnp.bfloat16

    def lane(bufs, ring, total, columns):
        out_s, kept, in_s, in_a, in_b, sum_a, sum_b, in_c, in_d, last, in_z, s_sem, p_sem, q_sem, z_sem, credit, credit_z = bufs
        half = columns // 2
        front, back = pl.ds(0, half), pl.ds(half, half)
        to_x, to_y, to_c = device(z, 1 - x, y, c), device(z, x, 1 - y, c), device(z, x, y, 1 - c)

        def remote(src, dst, sems, where):
            return pltpu.make_async_remote_copy(
                src_ref=src, dst_ref=dst, send_sem=sems[0], recv_sem=sems[1], device_id=where, device_id_type=MESH)

        def sibling(k):
            s = k % ring
            return remote(out_s.at[s], in_s.at[s], (s_sem.at[s, 0], s_sem.at[s, 1]), to_c)

        def first(k):
            s = k % ring
            return (remote(kept.at[s, :, :, 1 - y, :, front], in_a.at[s], (p_sem.at[s, 0], p_sem.at[s, 1]), to_y),
                    remote(kept.at[s, :, 1 - x, :, :, back], in_b.at[s], (p_sem.at[s, 2], p_sem.at[s, 3]), to_x))

        def second(k):
            s = k % ring
            return (remote(sum_a.at[s, :, 1 - x], in_c.at[s], (q_sem.at[s, 0], q_sem.at[s, 1]), to_x),
                    remote(sum_b.at[s, :, 1 - y], in_d.at[s], (q_sem.at[s, 2], q_sem.at[s, 3]), to_y))

        def third(k):
            s = k % ring
            return tuple(remote(last.at[s, (z + d) % 4], in_z.at[s, d - 1], (z_sem.at[s, d - 1], z_sem.at[s, d + 2]),
                                device((z + d) % 4, x, y, c)) for d in (1, 2, 3))

        def give(index, k, where):
            @pl.when(k + ring < total)
            def _():
                pl.semaphore_signal(credit.at[index], inc=1, device_id=where, device_id_type=MESH)

        def take(ref, k):
            @pl.when(k >= ring)
            def _():
                pl.semaphore_wait(ref, 1)

        def reuse(k, copies):
            @pl.when(k >= ring)
            def _():
                for copy in copies(k - ring):
                    copy.wait_send()

        def add(left, right):
            return (left.astype(f32) + right.astype(f32)).astype(low)

        def send_sibling(k):
            take(credit.at[0], k)
            sibling(k).start()

        def stage_one(k):
            s = k % ring
            sibling(k).wait_recv()

            def body(i, carry):
                kept[s, i] = add(kept[s, i], in_s[s, i])
                return carry
            lax.fori_loop(0, 4, body, 0)
            give(0, k, to_c)
            take(credit.at[1], k)
            take(credit.at[2], k)
            for copy in first(k):
                copy.start()

        def stage_two(k):
            s = k % ring
            reuse(k, second)
            for copy in first(k):
                copy.wait_recv()

            def body(i, carry):
                for j in range(2):
                    sum_a[s, i, j] = add(kept[s, i, j, y, :, :half], in_a[s, i, j])
                    sum_b[s, i, j] = add(kept[s, i, x, j, :, half:], in_b[s, i, j])
                return carry
            lax.fori_loop(0, 4, body, 0)
            give(1, k, to_y)
            give(2, k, to_x)
            take(credit.at[3], k)
            take(credit.at[4], k)
            for copy in second(k):
                copy.start()

        def stage_three(k):
            s = k % ring
            reuse(k, third)
            for copy in second(k):
                copy.wait_recv()

            def body(i, carry):
                last[s, i, :, :half] = add(sum_a[s, i, x], in_c[s, i])
                last[s, i, :, half:] = add(sum_b[s, i, y], in_d[s, i])
                return carry
            lax.fori_loop(0, 4, body, 0)
            give(3, k, to_x)
            give(4, k, to_y)
            for d in (1, 2, 3):
                take(credit_z.at[d - 1], k)
            for copy in third(k):
                copy.start()

        def stage_four(k, target):
            s = k % ring
            for copy in third(k):
                copy.wait_recv()
            value = last[s, z].astype(f32)
            for d in (1, 2, 3):
                value = value + in_z[s, d - 1].astype(f32)
            target[...] = value
            for d in (1, 2, 3):
                @pl.when(k + ring < total)
                def _():
                    pl.semaphore_signal(credit_z.at[d - 1], inc=1, device_id=device((z + 4 - d) % 4, x, y, c), device_id_type=MESH)

        def drain(k):
            for copies in ((sibling(k),), first(k), second(k), third(k)):
                for copy in copies:
                    copy.wait_send()

        def fresh(k):
            reuse(k, lambda j: (sibling(j),) + first(j))

        return fresh, send_sibling, stage_one, stage_two, stage_three, stage_four, drain

    fresh, send_sibling, one, two, three, four, drain = lane(main_bufs, RING, n, width)
    _, small_sibling, small_one, small_two, small_three, small_four, small_drain = lane(small_bufs, 1, 1, small_width)
    out_s, kept = main_bufs[:2]
    small_s, small_kept = small_bufs[:2]

    def load(k, start):
        for number, (i, j, begin) in enumerate(pieces):
            @pl.when(k == number)
            def _():
                s = number % 2
                for copy in (pltpu.make_async_copy(lefts[i], left_buf.at[s], load_sem.at[s, 0]),
                             pltpu.make_async_copy(rights[j].at[:, pl.ds(begin, width)], right_buf.at[s], load_sem.at[s, 1])):
                    copy.start() if start else copy.wait()

    def multiply(k, parity, target):
        tile = 256

        def body(j, carry):
            cols = pl.ds(pl.multiple_of(j * tile, tile), tile)
            value = jnp.dot(left_buf[k % 2, parity], right_buf[k % 2, :, cols], preferred_element_type=f32)
            for i in range(16):
                target[k % RING, i // 4, (i // 2) % 2, i % 2, :, cols] = value[i * ROWS:(i + 1) * ROWS].astype(low)
            return carry
        lax.fori_loop(0, width // tile, body, 0)

    load(0, True)
    small_s[0] = small[1 - c]
    small_kept[0] = small[c]

    def step(t, carry):
        @pl.when(t < n)
        def _():
            load(t + 1, True)
            load(t, False)
            fresh(t)
            multiply(t, 1 - c, out_s)
            send_sibling(t)
            multiply(t, c, kept)
        for j, work in enumerate((lambda: small_sibling(0), lambda: small_one(0), lambda: small_two(0),
                                  lambda: small_three(0), lambda: small_four(0, small_out))):
            @pl.when(t == j)
            def _():
                work()
        for lag, work in ((1, one), (2, two), (3, three)):
            @pl.when((t >= lag) & (t < n + lag))
            def _():
                work(t - lag)

        @pl.when(t >= 4)
        def _():
            four(t - 4, out.at[t - 4])
        return carry
    lax.fori_loop(0, n + 4, step, 0)
    for k in range(n - RING, n):
        drain(k)
    small_drain(0)

def buffers(ring, columns):
    dma, reg = pltpu.SemaphoreType.DMA, pltpu.SemaphoreType.REGULAR
    half, low = columns // 2, jnp.bfloat16
    block = [pltpu.VMEM((ring, 4, 2, 2, ROWS, columns), low)] * 3
    halves = [pltpu.VMEM((ring, 4, 2, ROWS, half), low)] * 4
    quarters = [pltpu.VMEM((ring, 4, ROWS, half), low)] * 2
    ends = [pltpu.VMEM((ring, 4, ROWS, columns), low), pltpu.VMEM((ring, 3, ROWS, columns), low)]
    return block + halves + quarters + ends + [dma((ring, 2)), dma((ring, 4)), dma((ring, 4)), dma((ring, 6)), reg((5,)), reg((3,))]

def turned(value):
    tokens = value.shape[0]
    return value.T.reshape(16, 2, ROWS, tokens).swapaxes(0, 1).reshape(2, 16 * ROWS, tokens)

def reduce_products(lefts, rights, pieces, small, width=1280, cid=2):
    n = len(pieces)
    small_width = small.shape[-1]
    tokens = rights[0].shape[0]
    hbm, vmem = pl.BlockSpec(memory_space=pl.ANY), pl.BlockSpec(memory_space=pltpu.VMEM)
    return pl.pallas_call(
        functools.partial(reduce_kernel, tuple(pieces), len(lefts), len(rights), n, width, small_width),
        out_shape=[jax.ShapeDtypeStruct((n, ROWS, width), jnp.float32), jax.ShapeDtypeStruct((ROWS, small_width), jnp.float32)],
        in_specs=[hbm] * (len(lefts) + len(rights)) + [vmem],
        out_specs=[vmem, vmem],
        scratch_shapes=[pltpu.VMEM((2, 2, 16 * ROWS, tokens), jnp.bfloat16), pltpu.VMEM((2, tokens, width), jnp.bfloat16),
                        pltpu.SemaphoreType.DMA((2, 2))] + buffers(RING, width) + buffers(1, small_width),
        compiler_params=pltpu.CompilerParams(collective_id=cid, has_side_effects=True, vmem_limit_bytes=60 * 1024 * 1024),
        name="reduce_products",
    )(*lefts, *rights, small)

D = 1280
HEADS = 16
HEAD_DIM = 80
PATCH = 32
SEQ = 512


EPSILON = 1e-06
MOMENTUM = 0.9
AVG_DECAY = 0.9


def matrix_multiply(left_mat, right_mat):
    return jnp.dot(left_mat, right_mat, preferred_element_type=jnp.float32)


def flipped_bilinear(left_mat, right_mat):
    return lax.dot_general(
        left_mat, right_mat, (((1,), (1,)), ((), ())), preferred_element_type=jnp.float32
    )


def bilinear_flipped(left_mat, right_mat):
    return lax.dot_general(
        left_mat, right_mat, (((0,), (0,)), ((), ())), preferred_element_type=jnp.float32
    )


def rounded(values_in):
    return values_in.astype(jnp.bfloat16)


def rms_gain(values_in, gains_in):
    return (
        values_in
        * lax.rsqrt(jnp.mean(values_in * values_in, axis=-1, keepdims=True) + EPSILON)
        * gains_in
    )


def silu_slope(values_in):
    logistic = jax.nn.sigmoid(values_in)
    return logistic * (1.0 + values_in * (1.0 - logistic))


def rope_tables():
    half_dim = HEAD_DIM // 2
    position = jnp.arange(SEQ, dtype=jnp.float32)[:, None]
    spacing = 10000.0 ** (-jnp.arange(half_dim, dtype=jnp.float32) / half_dim)
    angles = (position * spacing[None, :]).T
    return (jnp.cos(angles), jnp.sin(angles))


def contract_rows(left_mat, right_mat):
    return lax.dot_general(
        left_mat, right_mat, (((0,), (0,)), ((), ())), preferred_element_type=jnp.float32
    )


def contract_columns(left_mat, right_mat):
    return lax.dot_general(
        left_mat, right_mat, (((1,), (1,)), ((), ())), preferred_element_type=jnp.float32
    )


def turned_head(head, cosines, sines):
    lower, upper = head[: HEAD_DIM // 2], head[HEAD_DIM // 2 :]
    return jnp.concatenate([lower * cosines - upper * sines, upper * cosines + lower * sines], axis=0)


def fill_bias(bias, owner_column, owner_row):
    @pl.when(pl.program_id(0) == 0)
    def _():
        keys = lax.broadcasted_iota(jnp.int32, (SEQ, SEQ), 0)
        queries = lax.broadcasted_iota(jnp.int32, (SEQ, SEQ), 1)
        allowed = (keys <= queries) & (owner_column[...] == owner_row[...])
        bias[...] = jnp.where(allowed, 0.0, -1e30)


def spread(target, block):
    target[...] = block.astype(jnp.float32).T.reshape(target.shape)


def gathered_heads(source):
    return source[...].reshape(STEP_HEADS * HEAD_DIM, SEQ).T.astype(jnp.bfloat16)


def attend_kernel(
    query_in, key_in, value_in, cosines, sines, owner_column, owner_row, mixed, log_totals, bias, heads, outcome
):
    fill_bias(bias, owner_column, owner_row)
    cos, sin = cosines[...], sines[...]
    for i, block in enumerate((query_in, key_in, value_in)):
        spread(heads.at[i], block[...])

    def one(i):
        query = rounded(turned_head(heads[0, i], cos, sin))
        key = rounded(turned_head(heads[1, i], cos, sin))
        value = rounded(heads[2, i])
        for j in range(SEQ // TILE):
            cols, rows = slice(j * TILE, (j + 1) * TILE), (j + 1) * TILE
            scores = contract_rows(key[:, :rows], query[:, cols]) * HEAD_DIM ** (-0.5) + bias[:rows, cols]
            top = jnp.max(scores, axis=0, keepdims=True)
            expo = jnp.exp(scores - top)
            total = jnp.sum(expo, axis=0, keepdims=True)
            probability = rounded(expo * (1.0 / total))
            outcome[i, :, cols] = matrix_multiply(value[:, :rows], probability)
            log_totals[i, :, cols] = top + jnp.log(total)

    def pair(i, carry):
        one(2 * i)
        one(2 * i + 1)
        return carry

    lax.fori_loop(0, STEP_HEADS // 2, pair, 0)
    mixed[...] = gathered_heads(outcome)


def attend_back_kernel(
    query_in,
    key_in,
    value_in,
    cosines,
    sines,
    owner_column,
    owner_row,
    log_totals,
    grad_mixed,
    grad_query_out,
    grad_key_out,
    grad_value_out,
    bias,
    heads,
    outcome,
):
    fill_bias(bias, owner_column, owner_row)
    cos, sin = cosines[...], sines[...]
    scale = HEAD_DIM ** (-0.5)
    for i, block in enumerate((query_in, key_in, value_in, grad_mixed)):
        spread(heads.at[i], block[...])

    def one(i):
        query = rounded(turned_head(heads[0, i], cos, sin))
        key = rounded(turned_head(heads[1, i], cos, sin))
        value, grad_mix = rounded(heads[2, i]), rounded(heads[3, i])
        grad_key, grad_value = [], []
        for j in range(SEQ // TILE):
            cols, rows = slice(j * TILE, (j + 1) * TILE), (j + 1) * TILE
            scores = contract_rows(key[:, :rows], query[:, cols]) * scale + bias[:rows, cols]
            probability = jnp.exp(scores - log_totals[i, :, cols])
            grad_probs = contract_rows(value[:, :rows], grad_mix[:, cols])
            inner_sum = jnp.sum(probability * grad_probs, axis=0, keepdims=True)
            grad_scores = rounded(probability * (grad_probs - inner_sum))
            grad_query = matrix_multiply(key[:, :rows], grad_scores) * scale
            outcome[0, i, :, cols] = turned_head(grad_query, cos[:, cols], -sin[:, cols])
            grad_key.append(contract_columns(query[:, cols], grad_scores))
            grad_value.append(contract_columns(grad_mix[:, cols], rounded(probability)))
        for j in range(SEQ // TILE):
            cols = slice(j * TILE, (j + 1) * TILE)
            key_part = sum(g[:, cols] for g in grad_key[j:]) * scale
            outcome[1, i, :, cols] = turned_head(key_part, cos[:, cols], -sin[:, cols])
            outcome[2, i, :, cols] = sum(g[:, cols] for g in grad_value[j:])

    def pair(i, carry):
        one(2 * i)
        one(2 * i + 1)
        return carry

    lax.fori_loop(0, STEP_HEADS // 2, pair, 0)
    for i, block in enumerate((grad_query_out, grad_key_out, grad_value_out)):
        block[...] = gathered_heads(outcome.at[i])


STEP_HEADS = 8
TILE = 256


def token_block(third=0):
    steps = HEADS // STEP_HEADS
    return pl.BlockSpec((SEQ, STEP_HEADS * HEAD_DIM), lambda h: (0, third * steps + h))


def attention_specs():
    half = pl.BlockSpec((HEAD_DIM // 2, SEQ), lambda h: (0, 0))
    return [
        token_block(0),
        token_block(1),
        token_block(2),
        half,
        half,
        pl.BlockSpec((SEQ, 1), lambda h: (0, 0)),
        pl.BlockSpec((1, SEQ), lambda h: (0, 0)),
    ]


def attention_call(kernel, in_specs, out_shape, out_specs, name, held, operands):
    return pl.pallas_call(
        kernel,
        grid=(HEADS // STEP_HEADS,),
        out_shape=out_shape,
        in_specs=in_specs,
        out_specs=out_specs,
        scratch_shapes=[pltpu.VMEM((SEQ, SEQ), jnp.float32)]
        + [pltpu.VMEM((*lead, STEP_HEADS, HEAD_DIM, SEQ), jnp.float32) for lead in held],
        cost_estimate=pl.CostEstimate(
            flops=8 * HEADS * SEQ * SEQ * HEAD_DIM,
            bytes_accessed=20 * HEADS * HEAD_DIM * SEQ,
            transcendentals=HEADS * SEQ * SEQ,
        ),
        compiler_params=pltpu.CompilerParams(vmem_limit_bytes=30 * 1024 * 1024),
        name=name,
    )(*operands)


TOTALS = pl.BlockSpec((STEP_HEADS, 1, SEQ), lambda h: (h, 0, 0))


def attend(qkv, cosines, sines, owners):
    operands = (qkv, qkv, qkv, cosines, sines, owners[:, None], owners[None, :])
    return attention_call(
        attend_kernel,
        attention_specs(),
        [
            jax.ShapeDtypeStruct((SEQ, HEADS * HEAD_DIM), jnp.bfloat16),
            jax.ShapeDtypeStruct((HEADS, 1, SEQ), jnp.float32),
        ],
        [token_block(), TOTALS],
        "attend",
        [(3,), ()],
        operands,
    )


def attend_back(qkv, cosines, sines, owners, log_totals, grad_mixed):
    operands = (qkv, qkv, qkv, cosines, sines, owners[:, None], owners[None, :], log_totals, grad_mixed)
    return attention_call(
        attend_back_kernel,
        attention_specs() + [TOTALS, token_block()],
        [jax.ShapeDtypeStruct((SEQ, HEADS * HEAD_DIM), jnp.bfloat16)] * 3,
        [token_block()] * 3,
        "attend_back",
        [(4,), (3,)],
        operands,
    )


def update(master, moment, average, gradient, rate):
    moment_new = MOMENTUM * moment + gradient
    master_new = master - rate * (gradient + MOMENTUM * moment_new)
    average_new = AVG_DECAY * average + (1.0 - AVG_DECAY) * master_new
    return (master_new, moment_new, average_new)


EVERYONE = ("dp", "head")


def summed(partial):
    return lax.psum_scatter(rounded(partial), EVERYONE, scatter_dimension=0, tiled=True).astype(
        jnp.float32
    )


def gather_in_parts(shards):
    early = gather(shards[:6])
    late, _ = lax.optimization_barrier((jnp.concatenate(shards[6:], axis=1), early[0]))
    late = lax.all_gather(late, EVERYONE, axis=0, tiled=True)
    return early + [late[:, :D], late[:, D:]]


def owned(values):
    return values.reshape(16, 2, ROWS, -1).swapaxes(0, 1).reshape(2, 4, 2, 2, ROWS, -1)


def on_device(
    input_segments,
    filler_flags,
    sequence_owner,
    prediction_adjoint,
    quadratic_params,
    quadratic_velocity,
    quadratic_mean,
    perceptron_params,
    perceptron_velocity,
    perceptron_mean,
    embedder_params,
    embedder_velocity,
    embedder_mean,
    bias_gain_params,
    bias_gain_velocity,
    bias_gain_mean,
    readout_params,
    readout_velocity,
    readout_mean,
):
    dp_size, head_size = lax.axis_size("dp"), lax.axis_size("head")
    low_square, low_ffn = rounded(quadratic_params), rounded(perceptron_params)
    low_token, low_readout = rounded(embedder_params), rounded(readout_params)
    vector_columns = jnp.pad(rounded(bias_gain_params).T, ((0, 0), (0, 123)))
    own_readout = lax.all_to_all(low_readout, "head", split_axis=1, concat_axis=2, tiled=True)
    adjoint = lax.all_to_all(prediction_adjoint, "head", split_axis=0, concat_axis=1, tiled=True)
    shards = [
        jnp.concatenate([low_square[0], low_token[0], low_token[1], vector_columns], axis=1),
        jnp.concatenate([low_square[1], low_square[2], low_square[3]], axis=1),
        low_square[4],
        low_ffn[0],
        low_ffn[1],
        low_square[5],
        own_readout[0],
        own_readout[1],
    ]
    fast = (dp_size, head_size) == (8, 4) and input_segments.shape[0] == SEQ
    first, qkv_w, attn_out_w, up_w, down_w, hidden_w, readout_w, shortcut_w = (
        gather_in_parts(shards)
        if fast
        else [lax.all_gather(s, EVERYONE, axis=0, tiled=True) for s in shards]
    )
    tok_out_w, tok_hidden_w, tok_skip_w = first[:, :D], first[:, D : D + 64], first[:, D + 64 : D + 128]
    vectors = first[:, D + 128 : D + 133].T.astype(jnp.float32)

    tok_count = input_segments.shape[0]
    seq_rows = tok_count // SEQ
    mask_float = filler_flags.astype(jnp.float32)
    tok_input = rounded(jnp.concatenate([input_segments * (1.0 - mask_float), mask_float], axis=1))
    tok_pre = flipped_bilinear(tok_input, tok_hidden_w) + vectors[2]
    tok_act = rounded(jax.nn.silu(tok_pre))
    stream_in = (
        matrix_multiply(tok_act, tok_out_w) + flipped_bilinear(tok_input, tok_skip_w) + vectors[3]
    )
    normed_one, norm_pull_one = jax.vjp(rms_gain, stream_in, vectors[0])
    normed_attn = rounded(normed_one)
    cosines, sines = rope_tables()
    row_tokens = [slice(r * SEQ, (r + 1) * SEQ) for r in range(seq_rows)]
    qkv = matrix_multiply(normed_attn, qkv_w)
    qkv = [qkv[part] for part in row_tokens]
    attended = [
        attend(heads, cosines, sines, sequence_owner[part]) for heads, part in zip(qkv, row_tokens)
    ]
    attn_mix = jnp.concatenate([mixed for mixed, _ in attended], axis=0)
    stream_mid = stream_in + matrix_multiply(attn_mix, attn_out_w)
    normed_two, norm_pull_two = jax.vjp(rms_gain, stream_mid, vectors[1])
    normed_ffn = rounded(normed_two)
    ffn_pre = matrix_multiply(normed_ffn, up_w)
    ffn_act = rounded(jax.nn.silu(ffn_pre))
    stream_out = stream_mid + flipped_bilinear(ffn_act, down_w)
    stream_low = rounded(stream_out)
    head_pre = matrix_multiply(stream_low, hidden_w) + vectors[4]
    head_act = rounded(jax.nn.silu(head_pre))
    own_prediction = rounded(
        matrix_multiply(head_act, readout_w) + matrix_multiply(stream_low, shortcut_w)
    )
    prediction = lax.all_to_all(own_prediction, "head", split_axis=1, concat_axis=0, tiled=True)

    head_share = summed(
        jnp.concatenate(
            [rounded(bilinear_flipped(head_act, adjoint)), rounded(bilinear_flipped(stream_low, adjoint))],
            axis=1,
        )
    )
    head_share = jnp.stack([head_share[:, :D], head_share[:, D:]])
    grad_head_act = flipped_bilinear(adjoint, readout_w)
    grad_skip = flipped_bilinear(adjoint, shortcut_w)
    grad_head_pre = rounded(grad_head_act * silu_slope(head_pre))
    grad_bias_head = jnp.sum(grad_head_pre.astype(jnp.float32), axis=0)
    grad_stream_out = grad_skip + flipped_bilinear(grad_head_pre, hidden_w)
    grad_ffn_out = rounded(grad_stream_out)
    grad_ffn_pre = rounded(matrix_multiply(grad_ffn_out, down_w) * silu_slope(ffn_pre))
    grad_stream_norm, grad_gain_two = norm_pull_two(flipped_bilinear(grad_ffn_pre, up_w))
    grad_stream_mid = grad_stream_out + grad_stream_norm
    grad_attn_out = rounded(grad_stream_mid)
    grad_attn_mix = rounded(flipped_bilinear(grad_attn_out, attn_out_w))
    grad_heads = [
        attend_back(heads, cosines, sines, sequence_owner[part], log_totals, grad_attn_mix[part])
        for heads, part, (_, log_totals) in zip(qkv, row_tokens, attended)
    ]
    grad_qkv_pre = [jnp.concatenate([heads[i] for heads in grad_heads], axis=0) for i in range(3)]
    grad_normed = sum(
        flipped_bilinear(grad, qkv_w[:, D * i : D * (i + 1)]) for i, grad in enumerate(grad_qkv_pre)
    )
    grad_stream_first, grad_gain_one = norm_pull_one(grad_normed)
    grad_stream_in = grad_stream_mid + grad_stream_first
    grad_bias_out = jnp.sum(grad_stream_in, axis=0)
    grad_tok_out = rounded(grad_stream_in)
    grad_skip_tok = bilinear_flipped(grad_tok_out, tok_input)
    grad_tok_pre = rounded(flipped_bilinear(grad_tok_out, tok_out_w) * silu_slope(tok_pre))
    grad_bias_tok = jnp.sum(grad_tok_pre.astype(jnp.float32), axis=0)
    grad_hidden_tok = bilinear_flipped(grad_tok_pre, tok_input)
    grad_input = matrix_multiply(grad_tok_out, tok_skip_w) + matrix_multiply(
        grad_tok_pre, tok_hidden_w
    )
    segment_derivative = grad_input[:, :PATCH] * (1.0 - mask_float)
    grad_vector = jnp.stack(
        [grad_gain_one, grad_gain_two, grad_bias_tok, grad_bias_out, grad_bias_head], axis=1
    )
    small = rounded(
        jnp.concatenate([grad_hidden_tok, grad_skip_tok, jnp.pad(grad_vector, ((0, 0), (0, 123)))], axis=1)
    )
    wide = ffn_act.shape[1] // D
    pieces = [(0, 0, 0)]
    pieces += [(1, 1, D * j) for j in range(wide)] + [(2, 2, D * j) for j in range(wide)]
    pieces += [(3, 3, 0)] + [(4, 4 + j, 0) for j in range(3)] + [(5, 7, 0)]
    lefts = [stream_low, grad_ffn_out, normed_ffn, attn_mix, normed_attn, tok_act]
    rights = [grad_head_pre, ffn_act, grad_ffn_pre, grad_attn_out, *grad_qkv_pre, grad_tok_out]
    if fast:
        shares, small_share = reduce_products([turned(v) for v in lefts], rights, pieces, owned(small))
    else:
        shares = [
            summed(bilinear_flipped(lefts[i], rights[j][:, start : start + D])) for i, j, start in pieces
        ]
        small_share = summed(small)
    head_share = lax.all_to_all(
        head_share, "head", split_axis=2, concat_axis=1, tiled=True
    )
    down_at = 1
    up_at = down_at + wide
    wo_at = up_at + wide
    square_share = jnp.stack(
        [shares[wo_at + 4], shares[wo_at + 1], shares[wo_at + 2], shares[wo_at + 3], shares[wo_at], shares[0]]
    )
    ffn_share = jnp.stack(
        [
            jnp.concatenate([shares[up_at + j] for j in range(wide)], axis=1),
            jnp.concatenate([shares[down_at + j] for j in range(wide)], axis=1),
        ]
    )
    token_share = jnp.stack([small_share[:, :64], small_share[:, 64:128]])
    vector_share = small_share[:, 128:133].T
    all_tokens = tok_count * lax.axis_size("dp") * lax.axis_size("head")
    matrix_rate = 0.5 / (D * all_tokens) ** 0.5
    quadratic_params_fresh, quadratic_velocity_fresh, quadratic_mean_fresh = update(
        quadratic_params, quadratic_velocity, quadratic_mean, square_share, matrix_rate
    )
    perceptron_params_fresh, perceptron_velocity_fresh, perceptron_mean_fresh = update(
        perceptron_params, perceptron_velocity, perceptron_mean, ffn_share, matrix_rate
    )
    embedder_params_fresh, embedder_velocity_fresh, embedder_mean_fresh = update(
        embedder_params,
        embedder_velocity,
        embedder_mean,
        token_share,
        0.5 / (2 * PATCH * all_tokens) ** 0.5,
    )
    bias_gain_params_fresh, bias_gain_velocity_fresh, bias_gain_mean_fresh = update(
        bias_gain_params, bias_gain_velocity, bias_gain_mean, vector_share, 0.3 / all_tokens**0.5
    )
    readout_params_fresh, readout_velocity_fresh, readout_mean_fresh = update(
        readout_params, readout_velocity, readout_mean, head_share, matrix_rate
    )
    return (
        prediction,
        segment_derivative,
        quadratic_params_fresh,
        quadratic_velocity_fresh,
        quadratic_mean_fresh,
        perceptron_params_fresh,
        perceptron_velocity_fresh,
        perceptron_mean_fresh,
        embedder_params_fresh,
        embedder_velocity_fresh,
        embedder_mean_fresh,
        bias_gain_params_fresh,
        bias_gain_velocity_fresh,
        bias_gain_mean_fresh,
        readout_params_fresh,
        readout_velocity_fresh,
        readout_mean_fresh,
    )


def solution(mesh):
    placed = (
        P(("dp", "head"), None),
        P(("dp", "head"), None),
        P(("dp", "head")),
        P("dp", "head"),
        P(None, ("dp", "head"), None),
        P(None, ("dp", "head"), None),
        P(None, ("dp", "head"), None),
        P(None, ("dp", "head"), None),
        P(None, ("dp", "head"), None),
        P(None, ("dp", "head"), None),
        P(None, ("dp", "head"), None),
        P(None, ("dp", "head"), None),
        P(None, ("dp", "head"), None),
        P(None, ("dp", "head")),
        P(None, ("dp", "head")),
        P(None, ("dp", "head")),
        P(None, "dp", "head"),
        P(None, "dp", "head"),
        P(None, "dp", "head"),
    )
    return jax.shard_map(
        on_device,
        mesh=mesh,
        in_specs=placed,
        out_specs=(
            P("dp", "head"),
            P(("dp", "head"), None),
            P(None, ("dp", "head"), None),
            P(None, ("dp", "head"), None),
            P(None, ("dp", "head"), None),
            P(None, ("dp", "head"), None),
            P(None, ("dp", "head"), None),
            P(None, ("dp", "head"), None),
            P(None, ("dp", "head"), None),
            P(None, ("dp", "head"), None),
            P(None, ("dp", "head"), None),
            P(None, ("dp", "head")),
            P(None, ("dp", "head")),
            P(None, ("dp", "head")),
            P(None, "dp", "head"),
            P(None, "dp", "head"),
            P(None, "dp", "head"),
        ),
        check_vma=False,
    )
```

```python
import functools
import jax, jax.numpy as jnp
from jax import lax
from jax.experimental import pallas as pl
from jax.experimental.pallas import tpu as pltpu
from jax.sharding import PartitionSpec as P

MESH = pl.DeviceIdType.MESH
ROWS = 40

def place():
    dp, hd = lax.axis_index("dp"), lax.axis_index("head")
    return dp // 2, dp % 2, hd // 2, hd % 2

def device(z, x, y, c):
    return (z * 2 + x, y * 2 + c)

def partners(z, x, y, c):
    found = [device((z + d) % 4, x, y, c) for d in (1, 2, 3)]
    return found + [device(z, 1 - x, y, c), device(z, x, 1 - y, c), device(z, x, y, 1 - c)]

def meet(z, x, y, c):
    barrier = pltpu.get_barrier_semaphore()
    for partner in partners(z, x, y, c):
        pl.semaphore_signal(barrier, inc=1, device_id=partner, device_id_type=MESH)
    pl.semaphore_wait(barrier, 6)

def gather_kernel(early, late, count, *refs):
    shards, full = refs[:count], refs[count : 2 * count]
    own_sem, z_sem, b_sem, s_sem, own_late, b_late, hop_sem, s_late = refs[2 * count :]
    z, x, y, c = place()
    meet(z, x, y, c)
    n, m = len(early), len(late)
    to_x, to_y, to_c = device(z, 1 - x, y, c), device(z, x, 1 - y, c), device(z, x, y, 1 - c)

    def remote(src, dst, sems, where):
        return pltpu.make_async_remote_copy(
            src_ref=src, dst_ref=dst, send_sem=sems[0], recv_sem=sems[1], device_id=where, device_id_type=MESH
        )

    def pair(sems, k, i):
        return sems.at[k, 2 * i], sems.at[k, 2 * i + 1]

    def halves(piece):
        _, start, width = piece
        return pl.ds(start, width), pl.ds(start, width // 2), pl.ds(start + width // 2, width // 2)

    own, along_z, second, third, sibling = [], [], [], [], []
    for k, piece in enumerate(early):
        cols, front, back = halves(piece)
        home, shard = full[piece[0]], shards[piece[0]]
        own.append(pltpu.make_async_copy(shard.at[:, cols], home.at[z, x, y, c, :, cols], own_sem.at[k]))
        along_z.append(
            [
                remote(
                    shard.at[:, cols],
                    home.at[z, x, y, c, :, cols],
                    pair(z_sem, k, d - 1),
                    device((z + d) % 4, x, y, c),
                )
                for d in (1, 2, 3)
            ]
        )
        a, b = home.at[:, x, y, c, :, front], home.at[:, x, y, c, :, back]
        second.append([remote(a, a, pair(b_sem, k, 0), to_y), remote(b, b, pair(b_sem, k, 1), to_x)])
        a, b = home.at[:, x, :, c, :, front], home.at[:, :, y, c, :, back]
        third.append([remote(a, a, pair(b_sem, k, 2), to_x), remote(b, b, pair(b_sem, k, 3), to_y)])
        a = home.at[:, :, :, c, :, cols]
        sibling.append(remote(a, a, pair(s_sem, k, 0), to_c))

    own_q, first_q, second_q, sibling_q = [], [], [], []
    for k, piece in enumerate(late):
        cols, front, back = halves(piece)
        home, shard = full[piece[0]], shards[piece[0]]
        own_q.append(pltpu.make_async_copy(shard.at[:, cols], home.at[z, x, y, c, :, cols], own_late.at[k]))
        first_q.append(
            [
                remote(shard.at[:, front], home.at[z, x, y, c, :, front], pair(b_late, k, 0), to_x),
                remote(shard.at[:, back], home.at[z, x, y, c, :, back], pair(b_late, k, 1), to_y),
            ]
        )
        a, b = home.at[z, :, y, c, :, front], home.at[z, x, :, c, :, back]
        second_q.append([remote(a, a, pair(b_late, k, 2), to_y), remote(b, b, pair(b_late, k, 3), to_x)])
        a = home.at[:, :, :, c, :, cols]
        sibling_q.append(remote(a, a, pair(s_late, k, 0), to_c))

    def hop(k, h, work):
        cols = halves(late[k])[0]
        home = full[late[k][0]]

        def copy(plane, direction, where):
            a = home.at[plane, :, :, c, :, cols]
            return remote(a, a, pair(hop_sem, k, 2 * h + direction), where)

        if work == "recv":
            cases = [(z >= h + 1, z - 1 - h, 0, (z + 3) % 4), (z <= 2 - h, z + 1 + h, 1, (z + 1) % 4)]
        else:
            cases = [((z <= 2) & (z >= h), z - h, 0, (z + 1) % 4), ((z >= 1) & (z <= 3 - h), z + h, 1, (z + 3) % 4)]
        for taken, plane, direction, other in cases:

            @pl.when(taken)
            def _():
                made = copy(plane, direction, device(other, x, y, c))
                if work == "recv":
                    made.wait_recv()
                elif work == "start":
                    made.start()
                else:
                    made.wait_send()

    ahead = 2

    def start_z(k):
        if k < n:
            for copy in along_z[k]:
                copy.start()
            own[k].start()

    for k in range(ahead):
        start_z(k)
    for k in range(m):
        own_q[k].start()
        for copy in first_q[k]:
            copy.start()
    for k in range(m):
        own_q[k].wait()
        for copy in first_q[k]:
            copy.wait_recv()
        for copy in second_q[k]:
            copy.start()
    hops = {}
    for k in range(m):
        begin = (3 * k) // 2
        for h in range(4):
            hops.setdefault(begin + 2 * h, []).append((k, h))
    for t in range(max(n + 2, max(hops) + 1)):
        start_z(t + ahead)
        if t < n:
            own[t].wait()
            for copy in along_z[t]:
                copy.wait_recv()
            for copy in second[t]:
                copy.start()
        k = t - 1
        if 0 <= k < n:
            for copy in second[k]:
                copy.wait_recv()
            for copy in third[k]:
                copy.start()
        for k, h in hops.get(t, []):
            if h == 0:
                for copy in second_q[k]:
                    copy.wait_recv()
            else:
                hop(k, h - 1, "recv")
            if h < 3:
                hop(k, h, "start")
            else:
                sibling_q[k].start()
        k = t - 2
        if 0 <= k < n:
            for copy in third[k]:
                copy.wait_recv()
            sibling[k].start()
    for k in range(m):
        sibling_q[k].wait_recv()
        for copy in first_q[k] + second_q[k] + [sibling_q[k]]:
            copy.wait_send()
        for h in range(3):
            hop(k, h, "sent")
    for k in range(n):
        sibling[k].wait_recv()
        for copy in along_z[k] + second[k] + third[k] + [sibling[k]]:
            copy.wait_send()


def gather(shards, early, late, cid=1):
    count, n, m = len(shards), len(early), len(late)
    dma = pltpu.SemaphoreType.DMA
    full = pl.pallas_call(
        functools.partial(gather_kernel, tuple(early), tuple(late), count),
        out_shape=[jax.ShapeDtypeStruct((4, 2, 2, 2, ROWS, s.shape[1]), jnp.bfloat16) for s in shards],
        in_specs=[pl.BlockSpec(memory_space=pltpu.VMEM)] * count,
        out_specs=[pl.BlockSpec(memory_space=pl.ANY)] * count,
        scratch_shapes=[dma((n,)), dma((n, 6)), dma((n, 8)), dma((n, 2))]
        + [dma((m,)), dma((m, 8)), dma((m, 12)), dma((m, 2))],
        compiler_params=pltpu.CompilerParams(collective_id=cid, has_side_effects=True),
        name="gather_weights",
    )(*shards)
    return [f.reshape(32 * ROWS, f.shape[-1]) for f in full]


EARLY = (
    [(0, 1280, 256), (0, 0, 1280)]
    + [(1, 1280 * j, 1280) for j in range(3)]
    + [(2, 0, 1280)]
    + [(4, 1280 * j, 1280) for j in range(4)]
    + [(3, 3072, 768), (3, 3840, 1280), (5, 0, 768), (5, 768, 512)]
)
LATE = [(3, 512 * j, 512) for j in range(6)]


RING = 3

def reduce_kernel(pieces, lefts_n, rights_n, n, width, small_width, *refs):
    lefts, rights, small = refs[:lefts_n], refs[lefts_n:lefts_n + rights_n], refs[lefts_n + rights_n]
    refs = refs[lefts_n + rights_n + 1:]
    out, small_out = refs[:2]
    left_buf, right_buf, load_sem = refs[2:5]
    main_bufs, small_bufs = refs[5:5 + 17], refs[5 + 17:5 + 34]
    z, x, y, c = place()
    meet(z, x, y, c)
    f32, low = jnp.float32, jnp.bfloat16

    def lane(bufs, ring, total, columns):
        out_s, kept, in_s, in_a, in_b, sum_a, sum_b, in_c, in_d, last, in_z, s_sem, p_sem, q_sem, z_sem, credit, credit_z = bufs
        half = columns // 2
        front, back = pl.ds(0, half), pl.ds(half, half)
        to_x, to_y, to_c = device(z, 1 - x, y, c), device(z, x, 1 - y, c), device(z, x, y, 1 - c)

        def remote(src, dst, sems, where):
            return pltpu.make_async_remote_copy(
                src_ref=src, dst_ref=dst, send_sem=sems[0], recv_sem=sems[1], device_id=where, device_id_type=MESH)

        def sibling(k):
            s = k % ring
            return remote(out_s.at[s], in_s.at[s], (s_sem.at[s, 0], s_sem.at[s, 1]), to_c)

        def first(k):
            s = k % ring
            return (remote(kept.at[s, :, :, 1 - y, :, front], in_a.at[s], (p_sem.at[s, 0], p_sem.at[s, 1]), to_y),
                    remote(kept.at[s, :, 1 - x, :, :, back], in_b.at[s], (p_sem.at[s, 2], p_sem.at[s, 3]), to_x))

        def second(k):
            s = k % ring
            return (remote(sum_a.at[s, :, 1 - x], in_c.at[s], (q_sem.at[s, 0], q_sem.at[s, 1]), to_x),
                    remote(sum_b.at[s, :, 1 - y], in_d.at[s], (q_sem.at[s, 2], q_sem.at[s, 3]), to_y))

        def third(k):
            s = k % ring
            return tuple(remote(last.at[s, (z + d) % 4], in_z.at[s, d - 1], (z_sem.at[s, d - 1], z_sem.at[s, d + 2]),
                                device((z + d) % 4, x, y, c)) for d in (1, 2, 3))

        def give(index, k, where):
            @pl.when(k + ring < total)
            def _():
                pl.semaphore_signal(credit.at[index], inc=1, device_id=where, device_id_type=MESH)

        def take(ref, k):
            @pl.when(k >= ring)
            def _():
                pl.semaphore_wait(ref, 1)

        def reuse(k, copies):
            @pl.when(k >= ring)
            def _():
                for copy in copies(k - ring):
                    copy.wait_send()

        def add(left, right):
            return (left.astype(f32) + right.astype(f32)).astype(low)

        def send_sibling(k):
            take(credit.at[0], k)
            sibling(k).start()

        def stage_one(k):
            s = k % ring
            sibling(k).wait_recv()

            def body(i, carry):
                kept[s, i] = add(kept[s, i], in_s[s, i])
                return carry
            lax.fori_loop(0, 4, body, 0)
            give(0, k, to_c)
            take(credit.at[1], k)
            take(credit.at[2], k)
            for copy in first(k):
                copy.start()

        def stage_two(k):
            s = k % ring
            reuse(k, second)
            for copy in first(k):
                copy.wait_recv()

            def body(i, carry):
                for j in range(2):
                    sum_a[s, i, j] = add(kept[s, i, j, y, :, :half], in_a[s, i, j])
                    sum_b[s, i, j] = add(kept[s, i, x, j, :, half:], in_b[s, i, j])
                return carry
            lax.fori_loop(0, 4, body, 0)
            give(1, k, to_y)
            give(2, k, to_x)
            take(credit.at[3], k)
            take(credit.at[4], k)
            for copy in second(k):
                copy.start()

        def stage_three(k):
            s = k % ring
            reuse(k, third)
            for copy in second(k):
                copy.wait_recv()

            def body(i, carry):
                last[s, i, :, :half] = add(sum_a[s, i, x], in_c[s, i])
                last[s, i, :, half:] = add(sum_b[s, i, y], in_d[s, i])
                return carry
            lax.fori_loop(0, 4, body, 0)
            give(3, k, to_x)
            give(4, k, to_y)
            for d in (1, 2, 3):
                take(credit_z.at[d - 1], k)
            for copy in third(k):
                copy.start()

        def stage_four(k, target):
            s = k % ring
            for copy in third(k):
                copy.wait_recv()
            value = last[s, z].astype(f32)
            for d in (1, 2, 3):
                value = value + in_z[s, d - 1].astype(f32)
            target[...] = value
            for d in (1, 2, 3):
                @pl.when(k + ring < total)
                def _():
                    pl.semaphore_signal(credit_z.at[d - 1], inc=1, device_id=device((z + 4 - d) % 4, x, y, c), device_id_type=MESH)

        def drain(k):
            for copies in ((sibling(k),), first(k), second(k), third(k)):
                for copy in copies:
                    copy.wait_send()

        def fresh(k):
            reuse(k, lambda j: (sibling(j),) + first(j))

        return fresh, send_sibling, stage_one, stage_two, stage_three, stage_four, drain

    fresh, send_sibling, one, two, three, four, drain = lane(main_bufs, RING, n, width)
    _, small_sibling, small_one, small_two, small_three, small_four, small_drain = lane(small_bufs, 1, 1, small_width)
    out_s, kept = main_bufs[:2]
    small_s, small_kept = small_bufs[:2]

    def load(k, start):
        for number, (i, j, begin) in enumerate(pieces):
            @pl.when(k == number)
            def _():
                s = number % 2
                for copy in (pltpu.make_async_copy(lefts[i], left_buf.at[s], load_sem.at[s, 0]),
                             pltpu.make_async_copy(rights[j].at[:, pl.ds(begin, width)], right_buf.at[s], load_sem.at[s, 1])):
                    copy.start() if start else copy.wait()

    def multiply(k, parity, target):
        tile = 256

        def body(j, carry):
            cols = pl.ds(pl.multiple_of(j * tile, tile), tile)
            value = jnp.dot(left_buf[k % 2, parity], right_buf[k % 2, :, cols], preferred_element_type=f32)
            for i in range(16):
                target[k % RING, i // 4, (i // 2) % 2, i % 2, :, cols] = value[i * ROWS:(i + 1) * ROWS].astype(low)
            return carry
        lax.fori_loop(0, width // tile, body, 0)

    load(0, True)
    small_s[0] = small[1 - c]
    small_kept[0] = small[c]

    def step(t, carry):
        @pl.when(t < n)
        def _():
            load(t + 1, True)
            load(t, False)
            fresh(t)
            multiply(t, 1 - c, out_s)
            send_sibling(t)
            multiply(t, c, kept)
        for j, work in enumerate((lambda: small_sibling(0), lambda: small_one(0), lambda: small_two(0),
                                  lambda: small_three(0), lambda: small_four(0, small_out))):
            @pl.when(t == j)
            def _():
                work()
        for lag, work in ((1, one), (2, two), (3, three)):
            @pl.when((t >= lag) & (t < n + lag))
            def _():
                work(t - lag)

        @pl.when(t >= 4)
        def _():
            four(t - 4, out.at[t - 4])
        return carry
    lax.fori_loop(0, n + 4, step, 0)
    for k in range(n - RING, n):
        drain(k)
    small_drain(0)

def buffers(ring, columns):
    dma, reg = pltpu.SemaphoreType.DMA, pltpu.SemaphoreType.REGULAR
    half, low = columns // 2, jnp.bfloat16
    block = [pltpu.VMEM((ring, 4, 2, 2, ROWS, columns), low)] * 3
    halves = [pltpu.VMEM((ring, 4, 2, ROWS, half), low)] * 4
    quarters = [pltpu.VMEM((ring, 4, ROWS, half), low)] * 2
    ends = [pltpu.VMEM((ring, 4, ROWS, columns), low), pltpu.VMEM((ring, 3, ROWS, columns), low)]
    return block + halves + quarters + ends + [dma((ring, 2)), dma((ring, 4)), dma((ring, 4)), dma((ring, 6)), reg((5,)), reg((3,))]

def turned(value):
    tokens = value.shape[0]
    return value.T.reshape(16, 2, ROWS, tokens).swapaxes(0, 1).reshape(2, 16 * ROWS, tokens)

def reduce_products(lefts, rights, pieces, small, width=1280, cid=2):
    n = len(pieces)
    small_width = small.shape[-1]
    tokens = rights[0].shape[0]
    hbm, vmem = pl.BlockSpec(memory_space=pl.ANY), pl.BlockSpec(memory_space=pltpu.VMEM)
    return pl.pallas_call(
        functools.partial(reduce_kernel, tuple(pieces), len(lefts), len(rights), n, width, small_width),
        out_shape=[jax.ShapeDtypeStruct((n, ROWS, width), jnp.float32), jax.ShapeDtypeStruct((ROWS, small_width), jnp.float32)],
        in_specs=[hbm] * (len(lefts) + len(rights)) + [vmem],
        out_specs=[vmem, vmem],
        scratch_shapes=[pltpu.VMEM((2, 2, 16 * ROWS, tokens), jnp.bfloat16), pltpu.VMEM((2, tokens, width), jnp.bfloat16),
                        pltpu.SemaphoreType.DMA((2, 2))] + buffers(RING, width) + buffers(1, small_width),
        compiler_params=pltpu.CompilerParams(collective_id=cid, has_side_effects=True, vmem_limit_bytes=60 * 1024 * 1024),
        name="reduce_products",
    )(*lefts, *rights, small)

D = 1280
HEADS = 16
HEAD_DIM = 80
PATCH = 32
SEQ = 512


EPSILON = 1e-06
MOMENTUM = 0.9
AVG_DECAY = 0.9


def matrix_multiply(left_mat, right_mat):
    return jnp.dot(left_mat, right_mat, preferred_element_type=jnp.float32)


def flipped_bilinear(left_mat, right_mat):
    return lax.dot_general(
        left_mat, right_mat, (((1,), (1,)), ((), ())), preferred_element_type=jnp.float32
    )


def bilinear_flipped(left_mat, right_mat):
    return lax.dot_general(
        left_mat, right_mat, (((0,), (0,)), ((), ())), preferred_element_type=jnp.float32
    )


def rounded(values_in):
    return values_in.astype(jnp.bfloat16)


def rms_gain(values_in, gains_in):
    return (
        values_in
        * lax.rsqrt(jnp.mean(values_in * values_in, axis=-1, keepdims=True) + EPSILON)
        * gains_in
    )


def silu_slope(values_in):
    logistic = jax.nn.sigmoid(values_in)
    return logistic * (1.0 + values_in * (1.0 - logistic))


def rope_tables():
    half_dim = HEAD_DIM // 2
    position = jnp.arange(SEQ, dtype=jnp.float32)[:, None]
    spacing = 10000.0 ** (-jnp.arange(half_dim, dtype=jnp.float32) / half_dim)
    angles = (position * spacing[None, :]).T
    return (jnp.cos(angles), jnp.sin(angles))


def contract_rows(left_mat, right_mat):
    return lax.dot_general(
        left_mat, right_mat, (((0,), (0,)), ((), ())), preferred_element_type=jnp.float32
    )


def contract_columns(left_mat, right_mat):
    return lax.dot_general(
        left_mat, right_mat, (((1,), (1,)), ((), ())), preferred_element_type=jnp.float32
    )


def turned_head(head, cosines, sines):
    lower, upper = head[: HEAD_DIM // 2], head[HEAD_DIM // 2 :]
    return jnp.concatenate([lower * cosines - upper * sines, upper * cosines + lower * sines], axis=0)


def fill_bias(bias, owner_column, owner_row):
    @pl.when(pl.program_id(0) == 0)
    def _():
        keys = lax.broadcasted_iota(jnp.int32, (SEQ, SEQ), 0)
        queries = lax.broadcasted_iota(jnp.int32, (SEQ, SEQ), 1)
        allowed = (keys <= queries) & (owner_column[...] == owner_row[...])
        bias[...] = jnp.where(allowed, 0.0, -1e30)


def spread(target, block):
    target[...] = block.astype(jnp.float32).T.reshape(target.shape)


def gathered_heads(source):
    return source[...].reshape(STEP_HEADS * HEAD_DIM, SEQ).T.astype(jnp.bfloat16)


def attend_kernel(
    query_in, key_in, value_in, cosines, sines, owner_column, owner_row, mixed, log_totals, bias, heads, outcome
):
    fill_bias(bias, owner_column, owner_row)
    cos, sin = cosines[...], sines[...]
    for i, block in enumerate((query_in, key_in, value_in)):
        spread(heads.at[i], block[...])

    def one(i):
        query = rounded(turned_head(heads[0, i], cos, sin))
        key = rounded(turned_head(heads[1, i], cos, sin))
        value = rounded(heads[2, i])
        for j in range(SEQ // TILE):
            cols, rows = slice(j * TILE, (j + 1) * TILE), (j + 1) * TILE
            scores = contract_rows(key[:, :rows], query[:, cols]) * HEAD_DIM ** (-0.5) + bias[:rows, cols]
            top = jnp.max(scores, axis=0, keepdims=True)
            expo = jnp.exp(scores - top)
            total = jnp.sum(expo, axis=0, keepdims=True)
            probability = rounded(expo * (1.0 / total))
            outcome[i, :, cols] = matrix_multiply(value[:, :rows], probability)
            log_totals[i, :, cols] = top + jnp.log(total)

    def pair(i, carry):
        one(2 * i)
        one(2 * i + 1)
        return carry

    lax.fori_loop(0, STEP_HEADS // 2, pair, 0)
    mixed[...] = gathered_heads(outcome)


def attend_back_kernel(
    query_in,
    key_in,
    value_in,
    cosines,
    sines,
    owner_column,
    owner_row,
    log_totals,
    grad_mixed,
    grad_query_out,
    grad_key_out,
    grad_value_out,
    bias,
    heads,
    outcome,
):
    fill_bias(bias, owner_column, owner_row)
    cos, sin = cosines[...], sines[...]
    scale = HEAD_DIM ** (-0.5)
    for i, block in enumerate((query_in, key_in, value_in, grad_mixed)):
        spread(heads.at[i], block[...])

    def one(i):
        query = rounded(turned_head(heads[0, i], cos, sin))
        key = rounded(turned_head(heads[1, i], cos, sin))
        value, grad_mix = rounded(heads[2, i]), rounded(heads[3, i])
        grad_key, grad_value = [], []
        for j in range(SEQ // TILE):
            cols, rows = slice(j * TILE, (j + 1) * TILE), (j + 1) * TILE
            scores = contract_rows(key[:, :rows], query[:, cols]) * scale + bias[:rows, cols]
            probability = jnp.exp(scores - log_totals[i, :, cols])
            grad_probs = contract_rows(value[:, :rows], grad_mix[:, cols])
            inner_sum = jnp.sum(probability * grad_probs, axis=0, keepdims=True)
            grad_scores = rounded(probability * (grad_probs - inner_sum))
            grad_query = matrix_multiply(key[:, :rows], grad_scores) * scale
            outcome[0, i, :, cols] = turned_head(grad_query, cos[:, cols], -sin[:, cols])
            grad_key.append(contract_columns(query[:, cols], grad_scores))
            grad_value.append(contract_columns(grad_mix[:, cols], rounded(probability)))
        for j in range(SEQ // TILE):
            cols = slice(j * TILE, (j + 1) * TILE)
            key_part = sum(g[:, cols] for g in grad_key[j:]) * scale
            outcome[1, i, :, cols] = turned_head(key_part, cos[:, cols], -sin[:, cols])
            outcome[2, i, :, cols] = sum(g[:, cols] for g in grad_value[j:])

    def pair(i, carry):
        one(2 * i)
        one(2 * i + 1)
        return carry

    lax.fori_loop(0, STEP_HEADS // 2, pair, 0)
    for i, block in enumerate((grad_query_out, grad_key_out, grad_value_out)):
        block[...] = gathered_heads(outcome.at[i])


STEP_HEADS = 8
TILE = 256


def token_block(third=0):
    steps = HEADS // STEP_HEADS
    return pl.BlockSpec((SEQ, STEP_HEADS * HEAD_DIM), lambda h: (0, third * steps + h))


def attention_specs():
    half = pl.BlockSpec((HEAD_DIM // 2, SEQ), lambda h: (0, 0))
    return [
        token_block(0),
        token_block(1),
        token_block(2),
        half,
        half,
        pl.BlockSpec((SEQ, 1), lambda h: (0, 0)),
        pl.BlockSpec((1, SEQ), lambda h: (0, 0)),
    ]


def attention_call(kernel, in_specs, out_shape, out_specs, name, held, operands):
    return pl.pallas_call(
        kernel,
        grid=(HEADS // STEP_HEADS,),
        out_shape=out_shape,
        in_specs=in_specs,
        out_specs=out_specs,
        scratch_shapes=[pltpu.VMEM((SEQ, SEQ), jnp.float32)]
        + [pltpu.VMEM((*lead, STEP_HEADS, HEAD_DIM, SEQ), jnp.float32) for lead in held],
        cost_estimate=pl.CostEstimate(
            flops=8 * HEADS * SEQ * SEQ * HEAD_DIM,
            bytes_accessed=20 * HEADS * HEAD_DIM * SEQ,
            transcendentals=HEADS * SEQ * SEQ,
        ),
        compiler_params=pltpu.CompilerParams(vmem_limit_bytes=30 * 1024 * 1024),
        name=name,
    )(*operands)


TOTALS = pl.BlockSpec((STEP_HEADS, 1, SEQ), lambda h: (h, 0, 0))


def attend(qkv, cosines, sines, owners):
    operands = (qkv, qkv, qkv, cosines, sines, owners[:, None], owners[None, :])
    return attention_call(
        attend_kernel,
        attention_specs(),
        [
            jax.ShapeDtypeStruct((SEQ, HEADS * HEAD_DIM), jnp.bfloat16),
            jax.ShapeDtypeStruct((HEADS, 1, SEQ), jnp.float32),
        ],
        [token_block(), TOTALS],
        "attend",
        [(3,), ()],
        operands,
    )


def attend_back(qkv, cosines, sines, owners, log_totals, grad_mixed):
    operands = (qkv, qkv, qkv, cosines, sines, owners[:, None], owners[None, :], log_totals, grad_mixed)
    return attention_call(
        attend_back_kernel,
        attention_specs() + [TOTALS, token_block()],
        [jax.ShapeDtypeStruct((SEQ, HEADS * HEAD_DIM), jnp.bfloat16)] * 3,
        [token_block()] * 3,
        "attend_back",
        [(4,), (3,)],
        operands,
    )


def update(master, moment, average, gradient, rate):
    moment_new = MOMENTUM * moment + gradient
    master_new = master - rate * (gradient + MOMENTUM * moment_new)
    average_new = AVG_DECAY * average + (1.0 - AVG_DECAY) * master_new
    return (master_new, moment_new, average_new)


EVERYONE = ("dp", "head")


def summed(partial):
    return lax.psum_scatter(rounded(partial), EVERYONE, scatter_dimension=0, tiled=True).astype(
        jnp.float32
    )


def gather_in_parts(shards):
    early = gather(shards[:6], EARLY, LATE)
    late, _ = lax.optimization_barrier((jnp.concatenate(shards[6:], axis=1), early[0]))
    late = lax.all_gather(late, EVERYONE, axis=0, tiled=True)
    return early + [late[:, :D], late[:, D:]]


def owned(values):
    return values.reshape(16, 2, ROWS, -1).swapaxes(0, 1).reshape(2, 4, 2, 2, ROWS, -1)


def on_device(
    input_segments,
    filler_flags,
    sequence_owner,
    prediction_adjoint,
    quadratic_params,
    quadratic_velocity,
    quadratic_mean,
    perceptron_params,
    perceptron_velocity,
    perceptron_mean,
    embedder_params,
    embedder_velocity,
    embedder_mean,
    bias_gain_params,
    bias_gain_velocity,
    bias_gain_mean,
    readout_params,
    readout_velocity,
    readout_mean,
):
    dp_size, head_size = lax.axis_size("dp"), lax.axis_size("head")
    low_square, low_ffn = rounded(quadratic_params), rounded(perceptron_params)
    low_token, low_readout = rounded(embedder_params), rounded(readout_params)
    vector_columns = jnp.pad(rounded(bias_gain_params).T, ((0, 0), (0, 123)))
    own_readout = lax.all_to_all(low_readout, "head", split_axis=1, concat_axis=2, tiled=True)
    adjoint = lax.all_to_all(prediction_adjoint, "head", split_axis=0, concat_axis=1, tiled=True)
    shards = [
        jnp.concatenate([low_square[0], low_token[0], low_token[1], vector_columns], axis=1),
        jnp.concatenate([low_square[1], low_square[2], low_square[3]], axis=1),
        low_square[4],
        low_ffn[0],
        low_ffn[1],
        low_square[5],
        own_readout[0],
        own_readout[1],
    ]
    fast = (dp_size, head_size) == (8, 4) and perceptron_params.shape[2] == 4 * D
    first, qkv_w, attn_out_w, up_w, down_w, hidden_w, readout_w, shortcut_w = (
        gather_in_parts(shards)
        if fast
        else [lax.all_gather(s, EVERYONE, axis=0, tiled=True) for s in shards]
    )
    tok_out_w, tok_hidden_w, tok_skip_w = first[:, :D], first[:, D : D + 64], first[:, D + 64 : D + 128]
    vectors = first[:, D + 128 : D + 133].T.astype(jnp.float32)

    tok_count = input_segments.shape[0]
    seq_rows = tok_count // SEQ
    mask_float = filler_flags.astype(jnp.float32)
    tok_input = rounded(jnp.concatenate([input_segments * (1.0 - mask_float), mask_float], axis=1))
    tok_pre = flipped_bilinear(tok_input, tok_hidden_w) + vectors[2]
    tok_act = rounded(jax.nn.silu(tok_pre))
    stream_in = (
        matrix_multiply(tok_act, tok_out_w) + flipped_bilinear(tok_input, tok_skip_w) + vectors[3]
    )
    normed_one, norm_pull_one = jax.vjp(rms_gain, stream_in, vectors[0])
    normed_attn = rounded(normed_one)
    cosines, sines = rope_tables()
    row_tokens = [slice(r * SEQ, (r + 1) * SEQ) for r in range(seq_rows)]
    qkv = matrix_multiply(normed_attn, qkv_w)
    qkv = [qkv[part] for part in row_tokens]
    attended = [
        attend(heads, cosines, sines, sequence_owner[part]) for heads, part in zip(qkv, row_tokens)
    ]
    attn_mix = jnp.concatenate([mixed for mixed, _ in attended], axis=0)
    stream_mid = stream_in + matrix_multiply(attn_mix, attn_out_w)
    normed_two, norm_pull_two = jax.vjp(rms_gain, stream_mid, vectors[1])
    normed_ffn = rounded(normed_two)
    ffn_pre = matrix_multiply(normed_ffn, up_w)
    ffn_act = rounded(jax.nn.silu(ffn_pre))
    stream_out = stream_mid + flipped_bilinear(ffn_act, down_w)
    stream_low = rounded(stream_out)
    head_pre = matrix_multiply(stream_low, hidden_w) + vectors[4]
    head_act = rounded(jax.nn.silu(head_pre))
    own_prediction = rounded(
        matrix_multiply(head_act, readout_w) + matrix_multiply(stream_low, shortcut_w)
    )
    prediction = lax.all_to_all(own_prediction, "head", split_axis=1, concat_axis=0, tiled=True)

    shard_rows = D // (dp_size * head_size)
    head_left = jnp.stack([v.T.reshape(-1, shard_rows, tok_count) for v in (head_act, stream_low)], axis=1)
    head_share = summed(matrix_multiply(head_left.reshape(2 * D, tok_count), adjoint))
    head_share = head_share.reshape(2, shard_rows, head_size, -1).transpose(2, 0, 1, 3)
    grad_head_act = flipped_bilinear(adjoint, readout_w)
    grad_skip = flipped_bilinear(adjoint, shortcut_w)
    grad_head_pre = rounded(grad_head_act * silu_slope(head_pre))
    grad_bias_head = jnp.sum(grad_head_pre.astype(jnp.float32), axis=0)
    grad_stream_out = grad_skip + flipped_bilinear(grad_head_pre, hidden_w)
    grad_ffn_out = rounded(grad_stream_out)
    grad_ffn_pre = rounded(matrix_multiply(grad_ffn_out, down_w) * silu_slope(ffn_pre))
    grad_stream_norm, grad_gain_two = norm_pull_two(flipped_bilinear(grad_ffn_pre, up_w))
    grad_stream_mid = grad_stream_out + grad_stream_norm
    grad_attn_out = rounded(grad_stream_mid)
    grad_attn_mix = rounded(flipped_bilinear(grad_attn_out, attn_out_w))
    grad_heads = [
        attend_back(heads, cosines, sines, sequence_owner[part], log_totals, grad_attn_mix[part])
        for heads, part, (_, log_totals) in zip(qkv, row_tokens, attended)
    ]
    grad_qkv_pre = [jnp.concatenate([heads[i] for heads in grad_heads], axis=0) for i in range(3)]
    grad_normed = sum(
        flipped_bilinear(grad, qkv_w[:, D * i : D * (i + 1)]) for i, grad in enumerate(grad_qkv_pre)
    )
    grad_stream_first, grad_gain_one = norm_pull_one(grad_normed)
    grad_stream_in = grad_stream_mid + grad_stream_first
    grad_bias_out = jnp.sum(grad_stream_in, axis=0)
    grad_tok_out = rounded(grad_stream_in)
    grad_skip_tok = bilinear_flipped(grad_tok_out, tok_input)
    grad_tok_pre = rounded(flipped_bilinear(grad_tok_out, tok_out_w) * silu_slope(tok_pre))
    grad_bias_tok = jnp.sum(grad_tok_pre.astype(jnp.float32), axis=0)
    grad_hidden_tok = bilinear_flipped(grad_tok_pre, tok_input)
    grad_input = matrix_multiply(grad_tok_out, tok_skip_w) + matrix_multiply(
        grad_tok_pre, tok_hidden_w
    )
    segment_derivative = grad_input[:, :PATCH] * (1.0 - mask_float)
    grad_vector = jnp.stack(
        [grad_gain_one, grad_gain_two, grad_bias_tok, grad_bias_out, grad_bias_head], axis=1
    )
    small = rounded(
        jnp.concatenate([grad_hidden_tok, grad_skip_tok, jnp.pad(grad_vector, ((0, 0), (0, 123)))], axis=1)
    )
    wide = ffn_act.shape[1] // D
    pieces = [(0, 0, 0)]
    pieces += [(1, 1, D * j) for j in range(wide)] + [(2, 2, D * j) for j in range(wide)]
    pieces += [(3, 3, 0)] + [(4, 4 + j, 0) for j in range(3)] + [(5, 7, 0)]
    lefts = [stream_low, grad_ffn_out, normed_ffn, attn_mix, normed_attn, tok_act]
    rights = [grad_head_pre, ffn_act, grad_ffn_pre, grad_attn_out, *grad_qkv_pre, grad_tok_out]
    if fast:
        shares, small_share = reduce_products([turned(v) for v in lefts], rights, pieces, owned(small))
    else:
        shares = [
            summed(bilinear_flipped(lefts[i], rights[j][:, start : start + D])) for i, j, start in pieces
        ]
        small_share = summed(small)
    head_share = lax.all_to_all(head_share, "head", split_axis=0, concat_axis=0)
    head_share = head_share.transpose(1, 0, 2, 3).reshape(readout_params.shape)
    down_at = 1
    up_at = down_at + wide
    wo_at = up_at + wide
    square_share = jnp.stack(
        [shares[wo_at + 4], shares[wo_at + 1], shares[wo_at + 2], shares[wo_at + 3], shares[wo_at], shares[0]]
    )
    ffn_share = jnp.stack(
        [
            jnp.concatenate([shares[up_at + j] for j in range(wide)], axis=1),
            jnp.concatenate([shares[down_at + j] for j in range(wide)], axis=1),
        ]
    )
    token_share = jnp.stack([small_share[:, :64], small_share[:, 64:128]])
    vector_share = small_share[:, 128:133].T
    all_tokens = tok_count * lax.axis_size("dp") * lax.axis_size("head")
    matrix_rate = 0.5 / (D * all_tokens) ** 0.5
    quadratic_params_fresh, quadratic_velocity_fresh, quadratic_mean_fresh = update(
        quadratic_params, quadratic_velocity, quadratic_mean, square_share, matrix_rate
    )
    perceptron_params_fresh, perceptron_velocity_fresh, perceptron_mean_fresh = update(
        perceptron_params, perceptron_velocity, perceptron_mean, ffn_share, matrix_rate
    )
    embedder_params_fresh, embedder_velocity_fresh, embedder_mean_fresh = update(
        embedder_params,
        embedder_velocity,
        embedder_mean,
        token_share,
        0.5 / (2 * PATCH * all_tokens) ** 0.5,
    )
    bias_gain_params_fresh, bias_gain_velocity_fresh, bias_gain_mean_fresh = update(
        bias_gain_params, bias_gain_velocity, bias_gain_mean, vector_share, 0.3 / all_tokens**0.5
    )
    readout_params_fresh, readout_velocity_fresh, readout_mean_fresh = update(
        readout_params, readout_velocity, readout_mean, head_share, matrix_rate
    )
    return (
        prediction,
        segment_derivative,
        quadratic_params_fresh,
        quadratic_velocity_fresh,
        quadratic_mean_fresh,
        perceptron_params_fresh,
        perceptron_velocity_fresh,
        perceptron_mean_fresh,
        embedder_params_fresh,
        embedder_velocity_fresh,
        embedder_mean_fresh,
        bias_gain_params_fresh,
        bias_gain_velocity_fresh,
        bias_gain_mean_fresh,
        readout_params_fresh,
        readout_velocity_fresh,
        readout_mean_fresh,
    )


def solution(mesh):
    placed = (
        P(("dp", "head"), None),
        P(("dp", "head"), None),
        P(("dp", "head")),
        P("dp", "head"),
        P(None, ("dp", "head"), None),
        P(None, ("dp", "head"), None),
        P(None, ("dp", "head"), None),
        P(None, ("dp", "head"), None),
        P(None, ("dp", "head"), None),
        P(None, ("dp", "head"), None),
        P(None, ("dp", "head"), None),
        P(None, ("dp", "head"), None),
        P(None, ("dp", "head"), None),
        P(None, ("dp", "head")),
        P(None, ("dp", "head")),
        P(None, ("dp", "head")),
        P(None, "dp", "head"),
        P(None, "dp", "head"),
        P(None, "dp", "head"),
    )
    return jax.shard_map(
        on_device,
        mesh=mesh,
        in_specs=placed,
        out_specs=(
            P("dp", "head"),
            P(("dp", "head"), None),
            P(None, ("dp", "head"), None),
            P(None, ("dp", "head"), None),
            P(None, ("dp", "head"), None),
            P(None, ("dp", "head"), None),
            P(None, ("dp", "head"), None),
            P(None, ("dp", "head"), None),
            P(None, ("dp", "head"), None),
            P(None, ("dp", "head"), None),
            P(None, ("dp", "head"), None),
            P(None, ("dp", "head")),
            P(None, ("dp", "head")),
            P(None, ("dp", "head")),
            P(None, "dp", "head"),
            P(None, "dp", "head"),
            P(None, "dp", "head"),
        ),
        check_vma=False,
    )
```

```python
import functools
import jax, jax.numpy as jnp
from jax import lax
from jax.experimental import pallas as pl
from jax.experimental.pallas import tpu as pltpu
from jax.sharding import PartitionSpec as P

MESH = pl.DeviceIdType.MESH
ROWS = 40

def place():
    dp, hd = lax.axis_index("dp"), lax.axis_index("head")
    return dp // 2, dp % 2, hd // 2, hd % 2

def device(z, x, y, c):
    return (z * 2 + x, y * 2 + c)

def partners(z, x, y, c):
    found = [device((z + d) % 4, x, y, c) for d in (1, 2, 3)]
    return found + [device(z, 1 - x, y, c), device(z, x, 1 - y, c), device(z, x, y, 1 - c)]

def meet(z, x, y, c):
    barrier = pltpu.get_barrier_semaphore()
    for partner in partners(z, x, y, c):
        pl.semaphore_signal(barrier, inc=1, device_id=partner, device_id_type=MESH)
    pl.semaphore_wait(barrier, 6)

def gather_kernel(early, late, count, *refs):
    shards, full = refs[:count], refs[count : 2 * count]
    own_sem, z_sem, b_sem, s_sem, own_late, b_late, hop_sem, s_late = refs[2 * count :]
    z, x, y, c = place()
    meet(z, x, y, c)
    n, m = len(early), len(late)
    to_x, to_y, to_c = device(z, 1 - x, y, c), device(z, x, 1 - y, c), device(z, x, y, 1 - c)

    def remote(src, dst, sems, where):
        return pltpu.make_async_remote_copy(
            src_ref=src, dst_ref=dst, send_sem=sems[0], recv_sem=sems[1], device_id=where, device_id_type=MESH
        )

    def pair(sems, k, i):
        return sems.at[k, 2 * i], sems.at[k, 2 * i + 1]

    def halves(piece):
        _, start, width = piece
        return pl.ds(start, width), pl.ds(start, width // 2), pl.ds(start + width // 2, width // 2)

    own, along_z, second, third, sibling = [], [], [], [], []
    for k, piece in enumerate(early):
        cols, front, back = halves(piece)
        home, shard = full[piece[0]], shards[piece[0]]
        own.append(pltpu.make_async_copy(shard.at[:, cols], home.at[z, x, y, c, :, cols], own_sem.at[k]))
        along_z.append(
            [
                remote(
                    shard.at[:, cols],
                    home.at[z, x, y, c, :, cols],
                    pair(z_sem, k, d - 1),
                    device((z + d) % 4, x, y, c),
                )
                for d in (1, 2, 3)
            ]
        )
        a, b = home.at[:, x, y, c, :, front], home.at[:, x, y, c, :, back]
        second.append([remote(a, a, pair(b_sem, k, 0), to_y), remote(b, b, pair(b_sem, k, 1), to_x)])
        a, b = home.at[:, x, :, c, :, front], home.at[:, :, y, c, :, back]
        third.append([remote(a, a, pair(b_sem, k, 2), to_x), remote(b, b, pair(b_sem, k, 3), to_y)])
        a = home.at[:, :, :, c, :, cols]
        sibling.append(remote(a, a, pair(s_sem, k, 0), to_c))

    own_q, first_q, second_q, sibling_q = [], [], [], []
    for k, piece in enumerate(late):
        cols, front, back = halves(piece)
        home, shard = full[piece[0]], shards[piece[0]]
        own_q.append(pltpu.make_async_copy(shard.at[:, cols], home.at[z, x, y, c, :, cols], own_late.at[k]))
        first_q.append(
            [
                remote(shard.at[:, front], home.at[z, x, y, c, :, front], pair(b_late, k, 0), to_x),
                remote(shard.at[:, back], home.at[z, x, y, c, :, back], pair(b_late, k, 1), to_y),
            ]
        )
        a, b = home.at[z, :, y, c, :, front], home.at[z, x, :, c, :, back]
        second_q.append([remote(a, a, pair(b_late, k, 2), to_y), remote(b, b, pair(b_late, k, 3), to_x)])
        a = home.at[:, :, :, c, :, cols]
        sibling_q.append(remote(a, a, pair(s_late, k, 0), to_c))

    def hop(k, h, work):
        cols = halves(late[k])[0]
        home = full[late[k][0]]

        def copy(plane, direction, where):
            a = home.at[plane, :, :, c, :, cols]
            return remote(a, a, pair(hop_sem, k, 2 * h + direction), where)

        if work == "recv":
            cases = [(z >= h + 1, z - 1 - h, 0, (z + 3) % 4), (z <= 2 - h, z + 1 + h, 1, (z + 1) % 4)]
        else:
            cases = [((z <= 2) & (z >= h), z - h, 0, (z + 1) % 4), ((z >= 1) & (z <= 3 - h), z + h, 1, (z + 3) % 4)]
        for taken, plane, direction, other in cases:

            @pl.when(taken)
            def _():
                made = copy(plane, direction, device(other, x, y, c))
                if work == "recv":
                    made.wait_recv()
                elif work == "start":
                    made.start()
                else:
                    made.wait_send()

    ahead = 2

    def start_z(k):
        if k < n:
            for copy in along_z[k]:
                copy.start()
            own[k].start()

    for k in range(ahead):
        start_z(k)
    for k in range(m):
        own_q[k].start()
        for copy in first_q[k]:
            copy.start()
    for k in range(m):
        own_q[k].wait()
        for copy in first_q[k]:
            copy.wait_recv()
        for copy in second_q[k]:
            copy.start()
    hops = {}
    for k in range(m):
        begin = (3 * k) // 2
        for h in range(4):
            hops.setdefault(begin + 2 * h, []).append((k, h))
    for t in range(max(n + 2, max(hops) + 1)):
        start_z(t + ahead)
        if t < n:
            own[t].wait()
            for copy in along_z[t]:
                copy.wait_recv()
            for copy in second[t]:
                copy.start()
        k = t - 1
        if 0 <= k < n:
            for copy in second[k]:
                copy.wait_recv()
            for copy in third[k]:
                copy.start()
        for k, h in hops.get(t, []):
            if h == 0:
                for copy in second_q[k]:
                    copy.wait_recv()
            else:
                hop(k, h - 1, "recv")
            if h < 3:
                hop(k, h, "start")
            else:
                sibling_q[k].start()
        k = t - 2
        if 0 <= k < n:
            for copy in third[k]:
                copy.wait_recv()
            sibling[k].start()
    for k in range(m):
        sibling_q[k].wait_recv()
        for copy in first_q[k] + second_q[k] + [sibling_q[k]]:
            copy.wait_send()
        for h in range(3):
            hop(k, h, "sent")
    for k in range(n):
        sibling[k].wait_recv()
        for copy in along_z[k] + second[k] + third[k] + [sibling[k]]:
            copy.wait_send()


def gather(shards, early, late, cid=1):
    count, n, m = len(shards), len(early), len(late)
    dma = pltpu.SemaphoreType.DMA
    full = pl.pallas_call(
        functools.partial(gather_kernel, tuple(early), tuple(late), count),
        out_shape=[jax.ShapeDtypeStruct((4, 2, 2, 2, ROWS, s.shape[1]), jnp.bfloat16) for s in shards],
        in_specs=[pl.BlockSpec(memory_space=pltpu.VMEM)] * count,
        out_specs=[pl.BlockSpec(memory_space=pl.ANY)] * count,
        scratch_shapes=[dma((n,)), dma((n, 6)), dma((n, 8)), dma((n, 2))]
        + [dma((m,)), dma((m, 8)), dma((m, 12)), dma((m, 2))],
        compiler_params=pltpu.CompilerParams(collective_id=cid, has_side_effects=True),
        name="gather_weights",
    )(*shards)
    return [f.reshape(32 * ROWS, f.shape[-1]) for f in full]


EARLY = (
    [(0, 1280, 256), (0, 0, 1280)]
    + [(1, 1280 * j, 1280) for j in range(3)]
    + [(2, 0, 1280)]
    + [(4, 1280 * j, 1280) for j in range(4)]
    + [(3, 3072, 768), (3, 3840, 1280), (5, 0, 768), (5, 768, 512)]
)
LATE = [(3, 512 * j, 512) for j in range(6)]


RING = 3

def reduce_kernel(pieces, lefts_n, rights_n, n, width, small_width, *refs):
    lefts, rights, small = refs[:lefts_n], refs[lefts_n:lefts_n + rights_n], refs[lefts_n + rights_n]
    refs = refs[lefts_n + rights_n + 1:]
    out, small_out = refs[:2]
    left_buf, right_buf, flipped, load_sem = refs[2:6]
    main_bufs, small_bufs = refs[6 : 6 + 16], refs[6 + 16 : 6 + 32]
    z, x, y, c = place()
    meet(z, x, y, c)
    f32, low = jnp.float32, jnp.bfloat16

    def lane(bufs, ring, total, columns):
        both, in_s, in_a, in_b, sum_a, sum_b, in_c, in_d, last, in_z, s_sem, p_sem, q_sem, z_sem, credit, credit_z = bufs
        half = columns // 2
        front, back = pl.ds(0, half), pl.ds(half, half)
        to_x, to_y, to_c = device(z, 1 - x, y, c), device(z, x, 1 - y, c), device(z, x, y, 1 - c)

        def remote(src, dst, sems, where):
            return pltpu.make_async_remote_copy(
                src_ref=src, dst_ref=dst, send_sem=sems[0], recv_sem=sems[1], device_id=where, device_id_type=MESH)

        def sibling(k):
            s = k % ring
            return remote(both.at[1 - c, s], in_s.at[s], (s_sem.at[s, 0], s_sem.at[s, 1]), to_c)

        def first(k):
            s = k % ring
            return (remote(both.at[c, s, :, :, 1 - y, :, front], in_a.at[s], (p_sem.at[s, 0], p_sem.at[s, 1]), to_y),
                    remote(both.at[c, s, :, 1 - x, :, :, back], in_b.at[s], (p_sem.at[s, 2], p_sem.at[s, 3]), to_x))

        def second(k):
            s = k % ring
            return (remote(sum_a.at[s, :, 1 - x], in_c.at[s], (q_sem.at[s, 0], q_sem.at[s, 1]), to_x),
                    remote(sum_b.at[s, :, 1 - y], in_d.at[s], (q_sem.at[s, 2], q_sem.at[s, 3]), to_y))

        def third(k):
            s = k % ring
            return tuple(remote(last.at[s, (z + d) % 4], in_z.at[s, d - 1], (z_sem.at[s, d - 1], z_sem.at[s, d + 2]),
                                device((z + d) % 4, x, y, c)) for d in (1, 2, 3))

        def give(index, k, where):
            @pl.when(k + ring < total)
            def _():
                pl.semaphore_signal(credit.at[index], inc=1, device_id=where, device_id_type=MESH)

        def take(ref, k):
            @pl.when(k >= ring)
            def _():
                pl.semaphore_wait(ref, 1)

        def reuse(k, copies):
            @pl.when(k >= ring)
            def _():
                for copy in copies(k - ring):
                    copy.wait_send()

        def add(left, right):
            return (left.astype(f32) + right.astype(f32)).astype(low)

        def send_sibling(k):
            take(credit.at[0], k)
            sibling(k).start()

        def stage_one(k):
            s = k % ring
            sibling(k).wait_recv()

            def body(i, carry):
                both[c, s, i] = add(both[c, s, i], in_s[s, i])
                return carry
            lax.fori_loop(0, 4, body, 0)
            give(0, k, to_c)
            take(credit.at[1], k)
            take(credit.at[2], k)
            for copy in first(k):
                copy.start()

        def stage_two(k):
            s = k % ring
            reuse(k, second)
            for copy in first(k):
                copy.wait_recv()

            def body(i, carry):
                for j in range(2):
                    sum_a[s, i, j] = add(both[c, s, i, j, y, :, :half], in_a[s, i, j])
                    sum_b[s, i, j] = add(both[c, s, i, x, j, :, half:], in_b[s, i, j])
                return carry
            lax.fori_loop(0, 4, body, 0)
            give(1, k, to_y)
            give(2, k, to_x)
            take(credit.at[3], k)
            take(credit.at[4], k)
            for copy in second(k):
                copy.start()

        def stage_three(k):
            s = k % ring
            reuse(k, third)
            for copy in second(k):
                copy.wait_recv()

            def body(i, carry):
                last[s, i, :, :half] = add(sum_a[s, i, x], in_c[s, i])
                last[s, i, :, half:] = add(sum_b[s, i, y], in_d[s, i])
                return carry
            lax.fori_loop(0, 4, body, 0)
            give(3, k, to_x)
            give(4, k, to_y)
            for d in (1, 2, 3):
                take(credit_z.at[d - 1], k)
            for copy in third(k):
                copy.start()

        def stage_four(k, target):
            s = k % ring
            for copy in third(k):
                copy.wait_recv()
            value = last[s, z].astype(f32)
            for d in (1, 2, 3):
                value = value + in_z[s, d - 1].astype(f32)
            target[...] = value
            for d in (1, 2, 3):
                @pl.when(k + ring < total)
                def _():
                    pl.semaphore_signal(credit_z.at[d - 1], inc=1, device_id=device((z + 4 - d) % 4, x, y, c), device_id_type=MESH)

        def drain(k):
            for copies in ((sibling(k),), first(k), second(k), third(k)):
                for copy in copies:
                    copy.wait_send()

        def fresh(k):
            reuse(k, lambda j: (sibling(j),) + first(j))

        return fresh, send_sibling, stage_one, stage_two, stage_three, stage_four, drain

    fresh, send_sibling, one, two, three, four, drain = lane(main_bufs, RING, n, width)
    _, small_sibling, small_one, small_two, small_three, small_four, small_drain = lane(small_bufs, 1, 1, small_width)
    both, small_both = main_bufs[0], small_bufs[0]

    def load(k, start):
        for number, (i, j, begin) in enumerate(pieces):
            @pl.when(k == number)
            def _():
                s = number % 2
                for copy in (pltpu.make_async_copy(lefts[i], left_buf.at[s], load_sem.at[s, 0]),
                             pltpu.make_async_copy(rights[j].at[:, pl.ds(begin, width)], right_buf.at[s], load_sem.at[s, 1])):
                    copy.start() if start else copy.wait()

    def multiply(k):
        flipped[...] = left_buf[k % 2].T
        tile, rows = 256, 16 * ROWS

        def body(j, carry):
            cols = pl.ds(pl.multiple_of(j * tile, tile), tile)
            for part in range(2):
                value = jnp.dot(
                    flipped[part * rows : (part + 1) * rows], right_buf[k % 2, :, cols], preferred_element_type=f32
                )
                for r in range(16):
                    i = part * 16 + r
                    both[i % 2, k % RING, i // 8, (i // 4) % 2, (i // 2) % 2, :, cols] = value[
                        r * ROWS : (r + 1) * ROWS
                    ].astype(low)
            return carry

        lax.fori_loop(0, width // tile, body, 0)

    load(0, True)
    small_both[:, 0] = small[...]

    def step(t, carry):
        @pl.when(t < n)
        def _():
            load(t + 1, True)
            load(t, False)
            fresh(t)
            multiply(t)
            send_sibling(t)
        for j, work in enumerate((lambda: small_sibling(0), lambda: small_one(0), lambda: small_two(0),
                                  lambda: small_three(0), lambda: small_four(0, small_out))):
            @pl.when(t == j)
            def _():
                work()
        for lag, work in ((1, one), (2, two), (3, three)):
            @pl.when((t >= lag) & (t < n + lag))
            def _():
                work(t - lag)

        @pl.when(t >= 4)
        def _():
            four(t - 4, out.at[t - 4])
        return carry
    lax.fori_loop(0, n + 4, step, 0)
    for k in range(n - RING, n):
        drain(k)
    small_drain(0)

def buffers(ring, columns):
    dma, reg = pltpu.SemaphoreType.DMA, pltpu.SemaphoreType.REGULAR
    half, low = columns // 2, jnp.bfloat16
    block = [pltpu.VMEM((2, ring, 4, 2, 2, ROWS, columns), low), pltpu.VMEM((ring, 4, 2, 2, ROWS, columns), low)]
    halves = [pltpu.VMEM((ring, 4, 2, ROWS, half), low)] * 4
    quarters = [pltpu.VMEM((ring, 4, ROWS, half), low)] * 2
    ends = [pltpu.VMEM((ring, 4, ROWS, columns), low), pltpu.VMEM((ring, 3, ROWS, columns), low)]
    return block + halves + quarters + ends + [dma((ring, 2)), dma((ring, 4)), dma((ring, 4)), dma((ring, 6)), reg((5,)), reg((3,))]

def reduce_products(lefts, rights, pieces, small, width=1280, cid=2):
    n = len(pieces)
    small_width = small.shape[-1]
    tokens = rights[0].shape[0]
    hbm, vmem = pl.BlockSpec(memory_space=pl.ANY), pl.BlockSpec(memory_space=pltpu.VMEM)
    return pl.pallas_call(
        functools.partial(reduce_kernel, tuple(pieces), len(lefts), len(rights), n, width, small_width),
        out_shape=[jax.ShapeDtypeStruct((n, ROWS, width), jnp.float32), jax.ShapeDtypeStruct((ROWS, small_width), jnp.float32)],
        in_specs=[hbm] * (len(lefts) + len(rights)) + [vmem],
        out_specs=[vmem, vmem],
        scratch_shapes=[pltpu.VMEM((2, tokens, 32 * ROWS), jnp.bfloat16), pltpu.VMEM((2, tokens, width), jnp.bfloat16),
                        pltpu.VMEM((32 * ROWS, tokens), jnp.bfloat16),
                        pltpu.SemaphoreType.DMA((2, 2))] + buffers(RING, width) + buffers(1, small_width),
        compiler_params=pltpu.CompilerParams(collective_id=cid, has_side_effects=True, vmem_limit_bytes=60 * 1024 * 1024),
        name="reduce_products",
    )(*lefts, *rights, small)

D = 1280
HEADS = 16
HEAD_DIM = 80
PATCH = 32
SEQ = 512


EPSILON = 1e-06
MOMENTUM = 0.9
AVG_DECAY = 0.9


def matrix_multiply(left_mat, right_mat):
    return jnp.dot(left_mat, right_mat, preferred_element_type=jnp.float32)


def flipped_bilinear(left_mat, right_mat):
    return lax.dot_general(
        left_mat, right_mat, (((1,), (1,)), ((), ())), preferred_element_type=jnp.float32
    )


def bilinear_flipped(left_mat, right_mat):
    return lax.dot_general(
        left_mat, right_mat, (((0,), (0,)), ((), ())), preferred_element_type=jnp.float32
    )


def rounded(values_in):
    return values_in.astype(jnp.bfloat16)


def rms_gain(values_in, gains_in):
    return (
        values_in
        * lax.rsqrt(jnp.mean(values_in * values_in, axis=-1, keepdims=True) + EPSILON)
        * gains_in
    )


def silu_slope(values_in):
    logistic = jax.nn.sigmoid(values_in)
    return logistic * (1.0 + values_in * (1.0 - logistic))


def rope_tables():
    half_dim = HEAD_DIM // 2
    position = jnp.arange(SEQ, dtype=jnp.float32)[:, None]
    spacing = 10000.0 ** (-jnp.arange(half_dim, dtype=jnp.float32) / half_dim)
    angles = (position * spacing[None, :]).T
    return (jnp.cos(angles), jnp.sin(angles))


def contract_rows(left_mat, right_mat):
    return lax.dot_general(
        left_mat, right_mat, (((0,), (0,)), ((), ())), preferred_element_type=jnp.float32
    )


def contract_columns(left_mat, right_mat):
    return lax.dot_general(
        left_mat, right_mat, (((1,), (1,)), ((), ())), preferred_element_type=jnp.float32
    )


def turned_head(head, cosines, sines):
    lower, upper = head[: HEAD_DIM // 2], head[HEAD_DIM // 2 :]
    return jnp.concatenate([lower * cosines - upper * sines, upper * cosines + lower * sines], axis=0)


def fill_bias(bias, owner_column, owner_row):
    @pl.when(pl.program_id(0) == 0)
    def _():
        keys = lax.broadcasted_iota(jnp.int32, (SEQ, SEQ), 0)
        queries = lax.broadcasted_iota(jnp.int32, (SEQ, SEQ), 1)
        allowed = (keys <= queries) & (owner_column[...] == owner_row[...])
        bias[...] = jnp.where(allowed, 0.0, -1e30)


def spread(target, block):
    target[...] = block.astype(jnp.float32).T.reshape(target.shape)


def gathered_heads(source):
    return source[...].reshape(STEP_HEADS * HEAD_DIM, SEQ).T.astype(jnp.bfloat16)


def attend_kernel(
    query_in, key_in, value_in, cosines, sines, owner_column, owner_row, mixed, log_totals, bias, heads, outcome
):
    fill_bias(bias, owner_column, owner_row)
    cos, sin = cosines[...], sines[...]
    for i, block in enumerate((query_in, key_in, value_in)):
        spread(heads.at[i], block[...])

    def one(i):
        query = rounded(turned_head(heads[0, i], cos, sin))
        key = rounded(turned_head(heads[1, i], cos, sin))
        value = rounded(heads[2, i])
        for j in range(SEQ // TILE):
            cols, rows = slice(j * TILE, (j + 1) * TILE), (j + 1) * TILE
            scores = contract_rows(key[:, :rows], query[:, cols]) * HEAD_DIM ** (-0.5) + bias[:rows, cols]
            top = jnp.max(scores, axis=0, keepdims=True)
            expo = jnp.exp(scores - top)
            total = jnp.sum(expo, axis=0, keepdims=True)
            probability = rounded(expo * (1.0 / total))
            outcome[i, :, cols] = matrix_multiply(value[:, :rows], probability)
            log_totals[i, :, cols] = top + jnp.log(total)

    def pair(i, carry):
        one(2 * i)
        one(2 * i + 1)
        return carry

    lax.fori_loop(0, STEP_HEADS // 2, pair, 0)
    mixed[...] = gathered_heads(outcome)


def attend_back_kernel(
    query_in,
    key_in,
    value_in,
    cosines,
    sines,
    owner_column,
    owner_row,
    log_totals,
    grad_mixed,
    grad_query_out,
    grad_key_out,
    grad_value_out,
    bias,
    heads,
    outcome,
):
    fill_bias(bias, owner_column, owner_row)
    cos, sin = cosines[...], sines[...]
    scale = HEAD_DIM ** (-0.5)
    for i, block in enumerate((query_in, key_in, value_in, grad_mixed)):
        spread(heads.at[i], block[...])

    def one(i):
        query = rounded(turned_head(heads[0, i], cos, sin))
        key = rounded(turned_head(heads[1, i], cos, sin))
        value, grad_mix = rounded(heads[2, i]), rounded(heads[3, i])
        grad_key, grad_value = [], []
        for j in range(SEQ // TILE):
            cols, rows = slice(j * TILE, (j + 1) * TILE), (j + 1) * TILE
            scores = contract_rows(key[:, :rows], query[:, cols]) * scale + bias[:rows, cols]
            probability = jnp.exp(scores - log_totals[i, :, cols])
            grad_probs = contract_rows(value[:, :rows], grad_mix[:, cols])
            inner_sum = jnp.sum(probability * grad_probs, axis=0, keepdims=True)
            grad_scores = rounded(probability * (grad_probs - inner_sum))
            grad_query = matrix_multiply(key[:, :rows], grad_scores) * scale
            outcome[0, i, :, cols] = turned_head(grad_query, cos[:, cols], -sin[:, cols])
            grad_key.append(contract_columns(query[:, cols], grad_scores))
            grad_value.append(contract_columns(grad_mix[:, cols], rounded(probability)))
        for j in range(SEQ // TILE):
            cols = slice(j * TILE, (j + 1) * TILE)
            key_part = sum(g[:, cols] for g in grad_key[j:]) * scale
            outcome[1, i, :, cols] = turned_head(key_part, cos[:, cols], -sin[:, cols])
            outcome[2, i, :, cols] = sum(g[:, cols] for g in grad_value[j:])

    def pair(i, carry):
        one(2 * i)
        one(2 * i + 1)
        return carry

    lax.fori_loop(0, STEP_HEADS // 2, pair, 0)
    for i, block in enumerate((grad_query_out, grad_key_out, grad_value_out)):
        block[...] = gathered_heads(outcome.at[i])


STEP_HEADS = 8
TILE = 256


def token_block(third=0):
    steps = HEADS // STEP_HEADS
    return pl.BlockSpec((SEQ, STEP_HEADS * HEAD_DIM), lambda h: (0, third * steps + h))


def attention_specs():
    half = pl.BlockSpec((HEAD_DIM // 2, SEQ), lambda h: (0, 0))
    return [
        token_block(0),
        token_block(1),
        token_block(2),
        half,
        half,
        pl.BlockSpec((SEQ, 1), lambda h: (0, 0)),
        pl.BlockSpec((1, SEQ), lambda h: (0, 0)),
    ]


def attention_call(kernel, in_specs, out_shape, out_specs, name, held, operands):
    return pl.pallas_call(
        kernel,
        grid=(HEADS // STEP_HEADS,),
        out_shape=out_shape,
        in_specs=in_specs,
        out_specs=out_specs,
        scratch_shapes=[pltpu.VMEM((SEQ, SEQ), jnp.float32)]
        + [pltpu.VMEM((*lead, STEP_HEADS, HEAD_DIM, SEQ), jnp.float32) for lead in held],
        cost_estimate=pl.CostEstimate(
            flops=8 * HEADS * SEQ * SEQ * HEAD_DIM,
            bytes_accessed=20 * HEADS * HEAD_DIM * SEQ,
            transcendentals=HEADS * SEQ * SEQ,
        ),
        compiler_params=pltpu.CompilerParams(vmem_limit_bytes=30 * 1024 * 1024),
        name=name,
    )(*operands)


TOTALS = pl.BlockSpec((STEP_HEADS, 1, SEQ), lambda h: (h, 0, 0))


def attend(qkv, cosines, sines, owners):
    operands = (qkv, qkv, qkv, cosines, sines, owners[:, None], owners[None, :])
    return attention_call(
        attend_kernel,
        attention_specs(),
        [
            jax.ShapeDtypeStruct((SEQ, HEADS * HEAD_DIM), jnp.bfloat16),
            jax.ShapeDtypeStruct((HEADS, 1, SEQ), jnp.float32),
        ],
        [token_block(), TOTALS],
        "attend",
        [(3,), ()],
        operands,
    )


def attend_back(qkv, cosines, sines, owners, log_totals, grad_mixed):
    operands = (qkv, qkv, qkv, cosines, sines, owners[:, None], owners[None, :], log_totals, grad_mixed)
    return attention_call(
        attend_back_kernel,
        attention_specs() + [TOTALS, token_block()],
        [jax.ShapeDtypeStruct((SEQ, HEADS * HEAD_DIM), jnp.bfloat16)] * 3,
        [token_block()] * 3,
        "attend_back",
        [(4,), (3,)],
        operands,
    )


def update(master, moment, average, gradient, rate):
    moment_new = MOMENTUM * moment + gradient
    master_new = master - rate * (gradient + MOMENTUM * moment_new)
    average_new = AVG_DECAY * average + (1.0 - AVG_DECAY) * master_new
    return (master_new, moment_new, average_new)


EVERYONE = ("dp", "head")


def summed(partial):
    return lax.psum_scatter(rounded(partial), EVERYONE, scatter_dimension=0, tiled=True).astype(
        jnp.float32
    )


def gather_in_parts(shards):
    early = gather(shards[:6], EARLY, LATE)
    late, _ = lax.optimization_barrier((jnp.concatenate(shards[6:], axis=1), early[0]))
    late = lax.all_gather(late, EVERYONE, axis=0, tiled=True)
    return early + [late[:, :D], late[:, D:]]


def owned(values):
    return values.reshape(16, 2, ROWS, -1).swapaxes(0, 1).reshape(2, 4, 2, 2, ROWS, -1)


def on_device(
    input_segments,
    filler_flags,
    sequence_owner,
    prediction_adjoint,
    quadratic_params,
    quadratic_velocity,
    quadratic_mean,
    perceptron_params,
    perceptron_velocity,
    perceptron_mean,
    embedder_params,
    embedder_velocity,
    embedder_mean,
    bias_gain_params,
    bias_gain_velocity,
    bias_gain_mean,
    readout_params,
    readout_velocity,
    readout_mean,
):
    dp_size, head_size = lax.axis_size("dp"), lax.axis_size("head")
    low_square, low_ffn = rounded(quadratic_params), rounded(perceptron_params)
    low_token, low_readout = rounded(embedder_params), rounded(readout_params)
    vector_columns = jnp.pad(rounded(bias_gain_params).T, ((0, 0), (0, 123)))
    own_readout = lax.all_to_all(low_readout, "head", split_axis=1, concat_axis=2, tiled=True)
    adjoint = lax.all_to_all(prediction_adjoint, "head", split_axis=0, concat_axis=1, tiled=True)
    shards = [
        jnp.concatenate([low_square[0], low_token[0], low_token[1], vector_columns], axis=1),
        jnp.concatenate([low_square[1], low_square[2], low_square[3]], axis=1),
        low_square[4],
        low_ffn[0],
        low_ffn[1],
        low_square[5],
        own_readout[0],
        own_readout[1],
    ]
    fast = (dp_size, head_size) == (8, 4) and perceptron_params.shape[2] == 4 * D
    first, qkv_w, attn_out_w, up_w, down_w, hidden_w, readout_w, shortcut_w = (
        gather_in_parts(shards)
        if fast
        else [lax.all_gather(s, EVERYONE, axis=0, tiled=True) for s in shards]
    )
    tok_out_w, tok_hidden_w, tok_skip_w = first[:, :D], first[:, D : D + 64], first[:, D + 64 : D + 128]
    vectors = first[:, D + 128 : D + 133].T.astype(jnp.float32)

    tok_count = input_segments.shape[0]
    seq_rows = tok_count // SEQ
    mask_float = filler_flags.astype(jnp.float32)
    tok_input = rounded(jnp.concatenate([input_segments * (1.0 - mask_float), mask_float], axis=1))
    tok_pre = flipped_bilinear(tok_input, tok_hidden_w) + vectors[2]
    tok_act = rounded(jax.nn.silu(tok_pre))
    stream_in = (
        matrix_multiply(tok_act, tok_out_w) + flipped_bilinear(tok_input, tok_skip_w) + vectors[3]
    )
    normed_one, norm_pull_one = jax.vjp(rms_gain, stream_in, vectors[0])
    normed_attn = rounded(normed_one)
    cosines, sines = rope_tables()
    row_tokens = [slice(r * SEQ, (r + 1) * SEQ) for r in range(seq_rows)]
    qkv = matrix_multiply(normed_attn, qkv_w)
    qkv = [qkv[part] for part in row_tokens]
    attended = [
        attend(heads, cosines, sines, sequence_owner[part]) for heads, part in zip(qkv, row_tokens)
    ]
    attn_mix = jnp.concatenate([mixed for mixed, _ in attended], axis=0)
    stream_mid = stream_in + matrix_multiply(attn_mix, attn_out_w)
    normed_two, norm_pull_two = jax.vjp(rms_gain, stream_mid, vectors[1])
    normed_ffn = rounded(normed_two)
    ffn_pre = matrix_multiply(normed_ffn, up_w)
    ffn_act = rounded(jax.nn.silu(ffn_pre))
    stream_out = stream_mid + flipped_bilinear(ffn_act, down_w)
    stream_low = rounded(stream_out)
    head_pre = matrix_multiply(stream_low, hidden_w) + vectors[4]
    head_act = rounded(jax.nn.silu(head_pre))
    own_prediction = rounded(
        matrix_multiply(head_act, readout_w) + matrix_multiply(stream_low, shortcut_w)
    )
    prediction = lax.all_to_all(own_prediction, "head", split_axis=1, concat_axis=0, tiled=True)

    shard_rows = D // (dp_size * head_size)
    head_left = jnp.stack([v.T.reshape(-1, shard_rows, tok_count) for v in (head_act, stream_low)], axis=1)
    head_share = summed(matrix_multiply(head_left.reshape(2 * D, tok_count), adjoint))
    head_share = head_share.reshape(2, shard_rows, head_size, -1).transpose(2, 0, 1, 3)
    grad_head_act = flipped_bilinear(adjoint, readout_w)
    grad_skip = flipped_bilinear(adjoint, shortcut_w)
    grad_head_pre = rounded(grad_head_act * silu_slope(head_pre))
    grad_bias_head = jnp.sum(grad_head_pre.astype(jnp.float32), axis=0)
    grad_stream_out = grad_skip + flipped_bilinear(grad_head_pre, hidden_w)
    grad_ffn_out = rounded(grad_stream_out)
    grad_ffn_pre = rounded(matrix_multiply(grad_ffn_out, down_w) * silu_slope(ffn_pre))
    grad_stream_norm, grad_gain_two = norm_pull_two(flipped_bilinear(grad_ffn_pre, up_w))
    grad_stream_mid = grad_stream_out + grad_stream_norm
    grad_attn_out = rounded(grad_stream_mid)
    grad_attn_mix = rounded(flipped_bilinear(grad_attn_out, attn_out_w))
    grad_heads = [
        attend_back(heads, cosines, sines, sequence_owner[part], log_totals, grad_attn_mix[part])
        for heads, part, (_, log_totals) in zip(qkv, row_tokens, attended)
    ]
    grad_qkv_pre = [jnp.concatenate([heads[i] for heads in grad_heads], axis=0) for i in range(3)]
    grad_normed = sum(
        flipped_bilinear(grad, qkv_w[:, D * i : D * (i + 1)]) for i, grad in enumerate(grad_qkv_pre)
    )
    grad_stream_first, grad_gain_one = norm_pull_one(grad_normed)
    grad_stream_in = grad_stream_mid + grad_stream_first
    grad_bias_out = jnp.sum(grad_stream_in, axis=0)
    grad_tok_out = rounded(grad_stream_in)
    grad_skip_tok = bilinear_flipped(grad_tok_out, tok_input)
    grad_tok_pre = rounded(flipped_bilinear(grad_tok_out, tok_out_w) * silu_slope(tok_pre))
    grad_bias_tok = jnp.sum(grad_tok_pre.astype(jnp.float32), axis=0)
    grad_hidden_tok = bilinear_flipped(grad_tok_pre, tok_input)
    grad_input = matrix_multiply(grad_tok_out, tok_skip_w) + matrix_multiply(
        grad_tok_pre, tok_hidden_w
    )
    segment_derivative = grad_input[:, :PATCH] * (1.0 - mask_float)
    grad_vector = jnp.stack(
        [grad_gain_one, grad_gain_two, grad_bias_tok, grad_bias_out, grad_bias_head], axis=1
    )
    small = rounded(
        jnp.concatenate([grad_hidden_tok, grad_skip_tok, jnp.pad(grad_vector, ((0, 0), (0, 123)))], axis=1)
    )
    wide = ffn_act.shape[1] // D
    pieces = [(0, 0, 0)]
    pieces += [(1, 1, D * j) for j in range(wide)] + [(2, 2, D * j) for j in range(wide)]
    pieces += [(3, 3, 0)] + [(4, 4 + j, 0) for j in range(3)] + [(5, 7, 0)]
    lefts = [stream_low, grad_ffn_out, normed_ffn, attn_mix, normed_attn, tok_act]
    rights = [grad_head_pre, ffn_act, grad_ffn_pre, grad_attn_out, *grad_qkv_pre, grad_tok_out]
    if fast:
        shares, small_share = reduce_products(lefts, rights, pieces, owned(small))
    else:
        shares = [
            summed(bilinear_flipped(lefts[i], rights[j][:, start : start + D])) for i, j, start in pieces
        ]
        small_share = summed(small)
    head_share = lax.all_to_all(head_share, "head", split_axis=0, concat_axis=0)
    head_share = head_share.transpose(1, 0, 2, 3).reshape(readout_params.shape)
    down_at = 1
    up_at = down_at + wide
    wo_at = up_at + wide
    square_share = jnp.stack(
        [shares[wo_at + 4], shares[wo_at + 1], shares[wo_at + 2], shares[wo_at + 3], shares[wo_at], shares[0]]
    )
    ffn_share = jnp.stack(
        [
            jnp.concatenate([shares[up_at + j] for j in range(wide)], axis=1),
            jnp.concatenate([shares[down_at + j] for j in range(wide)], axis=1),
        ]
    )
    token_share = jnp.stack([small_share[:, :64], small_share[:, 64:128]])
    vector_share = small_share[:, 128:133].T
    all_tokens = tok_count * lax.axis_size("dp") * lax.axis_size("head")
    matrix_rate = 0.5 / (D * all_tokens) ** 0.5
    quadratic_params_fresh, quadratic_velocity_fresh, quadratic_mean_fresh = update(
        quadratic_params, quadratic_velocity, quadratic_mean, square_share, matrix_rate
    )
    perceptron_params_fresh, perceptron_velocity_fresh, perceptron_mean_fresh = update(
        perceptron_params, perceptron_velocity, perceptron_mean, ffn_share, matrix_rate
    )
    embedder_params_fresh, embedder_velocity_fresh, embedder_mean_fresh = update(
        embedder_params,
        embedder_velocity,
        embedder_mean,
        token_share,
        0.5 / (2 * PATCH * all_tokens) ** 0.5,
    )
    bias_gain_params_fresh, bias_gain_velocity_fresh, bias_gain_mean_fresh = update(
        bias_gain_params, bias_gain_velocity, bias_gain_mean, vector_share, 0.3 / all_tokens**0.5
    )
    readout_params_fresh, readout_velocity_fresh, readout_mean_fresh = update(
        readout_params, readout_velocity, readout_mean, head_share, matrix_rate
    )
    return (
        prediction,
        segment_derivative,
        quadratic_params_fresh,
        quadratic_velocity_fresh,
        quadratic_mean_fresh,
        perceptron_params_fresh,
        perceptron_velocity_fresh,
        perceptron_mean_fresh,
        embedder_params_fresh,
        embedder_velocity_fresh,
        embedder_mean_fresh,
        bias_gain_params_fresh,
        bias_gain_velocity_fresh,
        bias_gain_mean_fresh,
        readout_params_fresh,
        readout_velocity_fresh,
        readout_mean_fresh,
    )


def solution(mesh):
    placed = (
        P(("dp", "head"), None),
        P(("dp", "head"), None),
        P(("dp", "head")),
        P("dp", "head"),
        P(None, ("dp", "head"), None),
        P(None, ("dp", "head"), None),
        P(None, ("dp", "head"), None),
        P(None, ("dp", "head"), None),
        P(None, ("dp", "head"), None),
        P(None, ("dp", "head"), None),
        P(None, ("dp", "head"), None),
        P(None, ("dp", "head"), None),
        P(None, ("dp", "head"), None),
        P(None, ("dp", "head")),
        P(None, ("dp", "head")),
        P(None, ("dp", "head")),
        P(None, "dp", "head"),
        P(None, "dp", "head"),
        P(None, "dp", "head"),
    )
    return jax.shard_map(
        on_device,
        mesh=mesh,
        in_specs=placed,
        out_specs=(
            P("dp", "head"),
            P(("dp", "head"), None),
            P(None, ("dp", "head"), None),
            P(None, ("dp", "head"), None),
            P(None, ("dp", "head"), None),
            P(None, ("dp", "head"), None),
            P(None, ("dp", "head"), None),
            P(None, ("dp", "head"), None),
            P(None, ("dp", "head"), None),
            P(None, ("dp", "head"), None),
            P(None, ("dp", "head"), None),
            P(None, ("dp", "head")),
            P(None, ("dp", "head")),
            P(None, ("dp", "head")),
            P(None, "dp", "head"),
            P(None, "dp", "head"),
            P(None, "dp", "head"),
        ),
        check_vma=False,
    )
```

```python
import functools
import jax, jax.numpy as jnp
from jax import lax
from jax.experimental import pallas as pl
from jax.experimental.pallas import tpu as pltpu
from jax.sharding import PartitionSpec as P

MESH = pl.DeviceIdType.MESH
ROWS = 40

def place():
    dp, hd = lax.axis_index("dp"), lax.axis_index("head")
    return dp // 2, dp % 2, hd // 2, hd % 2

def device(z, x, y, c):
    return (z * 2 + x, y * 2 + c)

def partners(z, x, y, c):
    found = [device((z + d) % 4, x, y, c) for d in (1, 2, 3)]
    return found + [device(z, 1 - x, y, c), device(z, x, 1 - y, c), device(z, x, y, 1 - c)]

def meet(z, x, y, c):
    barrier = pltpu.get_barrier_semaphore()
    for partner in partners(z, x, y, c):
        pl.semaphore_signal(barrier, inc=1, device_id=partner, device_id_type=MESH)
    pl.semaphore_wait(barrier, 6)

def gather_kernel(early, late, count, *refs):
    shards, full = refs[:count], refs[count : 2 * count]
    own_sem, z_sem, b_sem, s_sem, own_late, b_late, hop_sem, s_late = refs[2 * count :]
    z, x, y, c = place()
    meet(z, x, y, c)
    n, m = len(early), len(late)
    to_x, to_y, to_c = device(z, 1 - x, y, c), device(z, x, 1 - y, c), device(z, x, y, 1 - c)

    def remote(src, dst, sems, where):
        return pltpu.make_async_remote_copy(
            src_ref=src, dst_ref=dst, send_sem=sems[0], recv_sem=sems[1], device_id=where, device_id_type=MESH
        )

    def pair(sems, k, i):
        return sems.at[k, 2 * i], sems.at[k, 2 * i + 1]

    def halves(piece):
        _, start, width = piece
        return pl.ds(start, width), pl.ds(start, width // 2), pl.ds(start + width // 2, width // 2)

    own, along_z, second, third, sibling = [], [], [], [], []
    for k, piece in enumerate(early):
        cols, front, back = halves(piece)
        home, shard = full[piece[0]], shards[piece[0]]
        own.append(pltpu.make_async_copy(shard.at[:, cols], home.at[z, x, y, c, :, cols], own_sem.at[k]))
        along_z.append(
            [
                remote(
                    shard.at[:, cols],
                    home.at[z, x, y, c, :, cols],
                    pair(z_sem, k, d - 1),
                    device((z + d) % 4, x, y, c),
                )
                for d in (1, 2, 3)
            ]
        )
        a, b = home.at[:, x, y, c, :, front], home.at[:, x, y, c, :, back]
        second.append([remote(a, a, pair(b_sem, k, 0), to_y), remote(b, b, pair(b_sem, k, 1), to_x)])
        a, b = home.at[:, x, :, c, :, front], home.at[:, :, y, c, :, back]
        third.append([remote(a, a, pair(b_sem, k, 2), to_x), remote(b, b, pair(b_sem, k, 3), to_y)])
        a = home.at[:, :, :, c, :, cols]
        sibling.append(remote(a, a, pair(s_sem, k, 0), to_c))

    own_q, first_q, second_q, sibling_q = [], [], [], []
    for k, piece in enumerate(late):
        cols, front, back = halves(piece)
        home, shard = full[piece[0]], shards[piece[0]]
        own_q.append(pltpu.make_async_copy(shard.at[:, cols], home.at[z, x, y, c, :, cols], own_late.at[k]))
        first_q.append(
            [
                remote(shard.at[:, front], home.at[z, x, y, c, :, front], pair(b_late, k, 0), to_x),
                remote(shard.at[:, back], home.at[z, x, y, c, :, back], pair(b_late, k, 1), to_y),
            ]
        )
        a, b = home.at[z, :, y, c, :, front], home.at[z, x, :, c, :, back]
        second_q.append([remote(a, a, pair(b_late, k, 2), to_y), remote(b, b, pair(b_late, k, 3), to_x)])
        a = home.at[:, :, :, c, :, cols]
        sibling_q.append(remote(a, a, pair(s_late, k, 0), to_c))

    def hop(k, h, work):
        cols = halves(late[k])[0]
        home = full[late[k][0]]

        def copy(plane, direction, where):
            a = home.at[plane, :, :, c, :, cols]
            return remote(a, a, pair(hop_sem, k, 2 * h + direction), where)

        if work == "recv":
            cases = [(z >= h + 1, z - 1 - h, 0, (z + 3) % 4), (z <= 2 - h, z + 1 + h, 1, (z + 1) % 4)]
        else:
            cases = [((z <= 2) & (z >= h), z - h, 0, (z + 1) % 4), ((z >= 1) & (z <= 3 - h), z + h, 1, (z + 3) % 4)]
        for taken, plane, direction, other in cases:

            @pl.when(taken)
            def _():
                made = copy(plane, direction, device(other, x, y, c))
                if work == "recv":
                    made.wait_recv()
                elif work == "start":
                    made.start()
                else:
                    made.wait_send()

    ahead = 2

    def start_z(k):
        if k < n:
            for copy in along_z[k]:
                copy.start()
            own[k].start()

    for k in range(ahead):
        start_z(k)
    for k in range(m):
        own_q[k].start()
        for copy in first_q[k]:
            copy.start()
    for k in range(m):
        own_q[k].wait()
        for copy in first_q[k]:
            copy.wait_recv()
        for copy in second_q[k]:
            copy.start()
    hops = {}
    for k in range(m):
        begin = (3 * k) // 2
        for h in range(4):
            hops.setdefault(begin + 2 * h, []).append((k, h))
    for t in range(max(n + 2, max(hops) + 1)):
        start_z(t + ahead)
        if t < n:
            own[t].wait()
            for copy in along_z[t]:
                copy.wait_recv()
            for copy in second[t]:
                copy.start()
        k = t - 1
        if 0 <= k < n:
            for copy in second[k]:
                copy.wait_recv()
            for copy in third[k]:
                copy.start()
        for k, h in hops.get(t, []):
            if h == 0:
                for copy in second_q[k]:
                    copy.wait_recv()
            else:
                hop(k, h - 1, "recv")
            if h < 3:
                hop(k, h, "start")
            else:
                sibling_q[k].start()
        k = t - 2
        if 0 <= k < n:
            for copy in third[k]:
                copy.wait_recv()
            sibling[k].start()
    for k in range(m):
        sibling_q[k].wait_recv()
        for copy in first_q[k] + second_q[k] + [sibling_q[k]]:
            copy.wait_send()
        for h in range(3):
            hop(k, h, "sent")
    for k in range(n):
        sibling[k].wait_recv()
        for copy in along_z[k] + second[k] + third[k] + [sibling[k]]:
            copy.wait_send()


def gather(shards, early, late, cid=1):
    count, n, m = len(shards), len(early), len(late)
    dma = pltpu.SemaphoreType.DMA
    full = pl.pallas_call(
        functools.partial(gather_kernel, tuple(early), tuple(late), count),
        out_shape=[jax.ShapeDtypeStruct((4, 2, 2, 2, ROWS, s.shape[1]), jnp.bfloat16) for s in shards],
        in_specs=[pl.BlockSpec(memory_space=pltpu.VMEM)] * count,
        out_specs=[pl.BlockSpec(memory_space=pl.ANY)] * count,
        scratch_shapes=[dma((n,)), dma((n, 6)), dma((n, 8)), dma((n, 2))]
        + [dma((m,)), dma((m, 8)), dma((m, 12)), dma((m, 2))],
        compiler_params=pltpu.CompilerParams(collective_id=cid, has_side_effects=True),
        name="gather_weights",
    )(*shards)
    return [f.reshape(32 * ROWS, f.shape[-1]) for f in full]


EARLY = (
    [(0, 1280, 256), (0, 0, 1280)]
    + [(1, 1280 * j, 1280) for j in range(3)]
    + [(2, 0, 1280)]
    + [(4, 1280 * j, 1280) for j in range(4)]
    + [(3, 3072, 768), (3, 3840, 1280), (5, 0, 768), (5, 768, 512)]
)
LATE = [(3, 512 * j, 512) for j in range(6)]


RING = 3
SLOW_EVERY = 3
SLOW_STEPS = (1, 4, 7, 9, 10, 11)
LAST_LAG = 5

def reduce_kernel(pieces, lefts_n, rights_n, n, m, width, small_width, *refs):
    lefts, rights, small = refs[:lefts_n], refs[lefts_n:lefts_n + rights_n], refs[lefts_n + rights_n]
    refs = refs[lefts_n + rights_n + 1:]
    out, small_out = refs[:2]
    left_buf, right_buf, flipped, load_sem = refs[2:6]
    main_bufs, small_bufs, slow_bufs = refs[6 : 6 + 16], refs[6 + 16 : 6 + 32], refs[6 + 32 :]
    z, x, y, c = place()
    meet(z, x, y, c)
    f32, low = jnp.float32, jnp.bfloat16

    def lane(bufs, ring, total, columns):
        both, in_s, in_a, in_b, sum_a, sum_b, in_c, in_d, last, in_z, s_sem, p_sem, q_sem, z_sem, credit, credit_z = bufs
        half = columns // 2
        front, back = pl.ds(0, half), pl.ds(half, half)
        to_x, to_y, to_c = device(z, 1 - x, y, c), device(z, x, 1 - y, c), device(z, x, y, 1 - c)

        def remote(src, dst, sems, where):
            return pltpu.make_async_remote_copy(
                src_ref=src, dst_ref=dst, send_sem=sems[0], recv_sem=sems[1], device_id=where, device_id_type=MESH)

        def sibling(k):
            s = k % ring
            return remote(both.at[1 - c, s], in_s.at[s], (s_sem.at[s, 0], s_sem.at[s, 1]), to_c)

        def first(k):
            s = k % ring
            return (remote(both.at[c, s, :, :, 1 - y, :, front], in_a.at[s], (p_sem.at[s, 0], p_sem.at[s, 1]), to_y),
                    remote(both.at[c, s, :, 1 - x, :, :, back], in_b.at[s], (p_sem.at[s, 2], p_sem.at[s, 3]), to_x))

        def second(k):
            s = k % ring
            return (remote(sum_a.at[s, :, 1 - x], in_c.at[s], (q_sem.at[s, 0], q_sem.at[s, 1]), to_x),
                    remote(sum_b.at[s, :, 1 - y], in_d.at[s], (q_sem.at[s, 2], q_sem.at[s, 3]), to_y))

        def third(k):
            s = k % ring
            return tuple(remote(last.at[s, (z + d) % 4], in_z.at[s, d - 1], (z_sem.at[s, d - 1], z_sem.at[s, d + 2]),
                                device((z + d) % 4, x, y, c)) for d in (1, 2, 3))

        def give(index, k, where):
            @pl.when(k + ring < total)
            def _():
                pl.semaphore_signal(credit.at[index], inc=1, device_id=where, device_id_type=MESH)

        def take(ref, k):
            @pl.when(k >= ring)
            def _():
                pl.semaphore_wait(ref, 1)

        def reuse(k, copies):
            @pl.when(k >= ring)
            def _():
                for copy in copies(k - ring):
                    copy.wait_send()

        def add(left, right):
            return (left.astype(f32) + right.astype(f32)).astype(low)

        def send_sibling(k):
            take(credit.at[0], k)
            sibling(k).start()

        def stage_one(k):
            s = k % ring
            sibling(k).wait_recv()

            def body(i, carry):
                both[c, s, i] = add(both[c, s, i], in_s[s, i])
                return carry
            lax.fori_loop(0, 4, body, 0)
            give(0, k, to_c)
            take(credit.at[1], k)
            take(credit.at[2], k)
            for copy in first(k):
                copy.start()

        def stage_two(k):
            s = k % ring
            reuse(k, second)
            for copy in first(k):
                copy.wait_recv()

            def body(i, carry):
                for j in range(2):
                    sum_a[s, i, j] = add(both[c, s, i, j, y, :, :half], in_a[s, i, j])
                    sum_b[s, i, j] = add(both[c, s, i, x, j, :, half:], in_b[s, i, j])
                return carry
            lax.fori_loop(0, 4, body, 0)
            give(1, k, to_y)
            give(2, k, to_x)
            take(credit.at[3], k)
            take(credit.at[4], k)
            for copy in second(k):
                copy.start()

        def stage_three(k):
            s = k % ring
            reuse(k, third)
            for copy in second(k):
                copy.wait_recv()

            def body(i, carry):
                last[s, i, :, :half] = add(sum_a[s, i, x], in_c[s, i])
                last[s, i, :, half:] = add(sum_b[s, i, y], in_d[s, i])
                return carry
            lax.fori_loop(0, 4, body, 0)
            give(3, k, to_x)
            give(4, k, to_y)
            for d in (1, 2, 3):
                take(credit_z.at[d - 1], k)
            for copy in third(k):
                copy.start()

        def stage_four(k, target):
            s = k % ring
            for copy in third(k):
                copy.wait_recv()
            value = last[s, z].astype(f32)
            for d in (1, 2, 3):
                value = value + in_z[s, d - 1].astype(f32)
            target[...] = value
            for d in (1, 2, 3):
                @pl.when(k + ring < total)
                def _():
                    pl.semaphore_signal(credit_z.at[d - 1], inc=1, device_id=device((z + 4 - d) % 4, x, y, c), device_id_type=MESH)

        def drain(k):
            for copies in ((sibling(k),), first(k), second(k), third(k)):
                for copy in copies:
                    copy.wait_send()

        def fresh(k):
            reuse(k, lambda j: (sibling(j),) + first(j))

        return fresh, send_sibling, stage_one, stage_two, stage_three, stage_four, drain

    fresh, send_sibling, one, two, three, four, drain = lane(main_bufs, RING, n, width)
    _, small_sibling, small_one, small_two, small_three, small_four, small_drain = lane(small_bufs, 1, 1, small_width)
    both, small_both = main_bufs[0], small_bufs[0]

    def slow_lane(k):
        whole, in_s, up_in, down_in, total, in_a, in_b, sum_a, sum_b, in_c, in_d, s_sem, up_sem, down_sem, p_sem = slow_bufs
        half = width // 2
        front, back = pl.ds(0, half), pl.ds(half, half)
        to_x, to_y, to_c = device(z, 1 - x, y, c), device(z, x, 1 - y, c), device(z, x, y, 1 - c)

        def remote(src, dst, sems, i, where):
            return pltpu.make_async_remote_copy(
                src_ref=src,
                dst_ref=dst,
                send_sem=sems.at[k, 2 * i],
                recv_sem=sems.at[k, 2 * i + 1],
                device_id=where,
                device_id_type=MESH,
            )

        def add(left, right):
            return (left.astype(f32) + right.astype(f32)).astype(low)

        def sibling():
            return remote(whole.at[1 - c, k], in_s.at[k], s_sem, 0, to_c)

        def up(b):
            return remote(whole.at[c, k, b], up_in.at[k, b - 1], up_sem, b - 1, device((z + 1) % 4, x, y, c))

        def down(b):
            return remote(whole.at[c, k, b], down_in.at[k, b], down_sem, b, device((z + 3) % 4, x, y, c))

        def first():
            return (
                remote(total.at[k, :, 1 - y, :, front], in_a.at[k], p_sem, 0, to_y),
                remote(total.at[k, 1 - x, :, :, back], in_b.at[k], p_sem, 1, to_x),
            )

        def second():
            return (
                remote(sum_a.at[k, 1 - x], in_c.at[k], p_sem, 2, to_x),
                remote(sum_b.at[k, 1 - y], in_d.at[k], p_sem, 3, to_y),
            )

        def take(copy, planes):
            for b in planes:
                copy(b).wait_recv()

        def pass_on(copy, source, planes):
            for b in planes:
                whole[c, k, b] = add(whole[c, k, b], source(b))
            for b in planes:
                copy(b).start()

        def from_below(b):
            return up_in[k, b - 1]

        def from_above(b):
            return down_in[k, b]

        def stage_one():
            sibling().wait_recv()

            def body(i, carry):
                whole[c, k, i] = add(whole[c, k, i], in_s[k, i])
                return carry

            lax.fori_loop(0, 4, body, 0)

            @pl.when(z == 0)
            def _():
                for b in (3, 2, 1):
                    up(b).start()

            @pl.when(z == 3)
            def _():
                for b in (0, 1, 2):
                    down(b).start()

        def stage_two():
            @pl.when(z == 1)
            def _():
                take(up, (3, 2, 1))
                pass_on(up, from_below, (3, 2))

            @pl.when(z == 2)
            def _():
                take(down, (0, 1, 2))
                pass_on(down, from_above, (0, 1))

        def stage_three():
            @pl.when(z == 2)
            def _():
                take(up, (3, 2))
                pass_on(up, from_below, (3,))

            @pl.when(z == 1)
            def _():
                take(down, (0, 1))
                pass_on(down, from_above, (0,))

        def stage_four():
            for b in range(4):

                @pl.when(z == b)
                def _():
                    if b == 3:
                        take(up, (3,))
                    if b == 0:
                        take(down, (0,))
                    value = whole[c, k, b].astype(f32)
                    if b > 0:
                        value = value + from_below(b).astype(f32)
                    if b < 3:
                        value = value + from_above(b).astype(f32)
                    total[k] = value.astype(low)

            for copy in first():
                copy.start()

        def stage_five():
            for copy in first():
                copy.wait_recv()
            for j in range(2):
                sum_a[k, j] = add(total[k, j, y, :, :half], in_a[k, j])
                sum_b[k, j] = add(total[k, x, j, :, half:], in_b[k, j])
            for copy in second():
                copy.start()

        def stage_six():
            for copy in second():
                copy.wait_recv()
            out[n + k, :, :half] = sum_a[k, x].astype(f32) + in_c[k].astype(f32)
            out[n + k, :, half:] = sum_b[k, y].astype(f32) + in_d[k].astype(f32)

        def drain():
            for copy in (sibling(), *first(), *second()):
                copy.wait_send()
            for copy, chip, planes in (
                (up, 0, (3, 2, 1)),
                (up, 1, (3, 2)),
                (up, 2, (3,)),
                (down, 3, (0, 1, 2)),
                (down, 2, (0, 1)),
                (down, 1, (0,)),
            ):

                @pl.when(z == chip)
                def _():
                    for b in planes:
                        copy(b).wait_send()

        return lambda: sibling().start(), stage_one, stage_two, stage_three, stage_four, stage_five, stage_six, drain

    def load_piece(number, s, start):
        i, j, begin = pieces[number]
        for copy in (
            pltpu.make_async_copy(lefts[i], left_buf.at[s], load_sem.at[s, 0]),
            pltpu.make_async_copy(rights[j].at[:, pl.ds(begin, width)], right_buf.at[s], load_sem.at[s, 1]),
        ):
            copy.start() if start else copy.wait()

    def load(k, start):
        for number in range(n):

            @pl.when(k == number)
            def _():
                load_piece(number, number % 2, start)

    def multiply(slot, target, place_in):
        flipped[...] = left_buf[slot].T
        tile, rows = 256, 16 * ROWS

        def body(j, carry):
            cols = pl.ds(pl.multiple_of(j * tile, tile), tile)
            for part in range(2):
                value = jnp.dot(
                    flipped[part * rows : (part + 1) * rows], right_buf[slot, :, cols], preferred_element_type=f32
                )
                for r in range(16):
                    i = part * 16 + r
                    target[i % 2, place_in, i // 8, (i // 4) % 2, (i // 2) % 2, :, cols] = value[
                        r * ROWS : (r + 1) * ROWS
                    ].astype(low)
            return carry

        lax.fori_loop(0, width // tile, body, 0)

    load(0, True)
    slow = [slow_lane(k) for k in range(m)]
    if m:
        load_piece(n, 2, True)
    small_both[:, 0] = small[...]

    def step(t, carry):
        @pl.when(t < n)
        def _():
            load(t + 1, True)
            load(t, False)
            fresh(t)
            multiply(t % 2, both, t % RING)
            send_sibling(t)
        for k in range(m):

            @pl.when(t == SLOW_EVERY * k)
            def _():
                load_piece(n + k, 2, False)
                multiply(2, slow_bufs[0], k)
                slow[k][0]()
                if k + 1 < m:
                    load_piece(n + k + 1, 2, True)

        for k in range(m):
            for stage, at in enumerate(SLOW_STEPS):

                @pl.when(t == SLOW_EVERY * k + at)
                def _():
                    slow[k][stage + 1]()

        for j, work in enumerate((lambda: small_sibling(0), lambda: small_one(0), lambda: small_two(0),
                                  lambda: small_three(0), lambda: small_four(0, small_out))):
            @pl.when(t == j)
            def _():
                work()
        for lag, work in ((1, one), (2, two), (3, three)):
            @pl.when((t >= lag) & (t < n + lag))
            def _():
                work(t - lag)

        @pl.when(t >= LAST_LAG)
        def _():
            four(t - LAST_LAG, out.at[t - LAST_LAG])
        return carry
    lax.fori_loop(0, n + LAST_LAG, step, 0)
    for k in range(n - RING, n):
        drain(k)
    small_drain(0)
    for k in range(m):
        slow[k][-1]()

def buffers(ring, columns):
    dma, reg = pltpu.SemaphoreType.DMA, pltpu.SemaphoreType.REGULAR
    half, low = columns // 2, jnp.bfloat16
    block = [pltpu.VMEM((2, ring, 4, 2, 2, ROWS, columns), low), pltpu.VMEM((ring, 4, 2, 2, ROWS, columns), low)]
    halves = [pltpu.VMEM((ring, 4, 2, ROWS, half), low)] * 4
    quarters = [pltpu.VMEM((ring, 4, ROWS, half), low)] * 2
    ends = [pltpu.VMEM((ring, 4, ROWS, columns), low), pltpu.VMEM((ring, 3, ROWS, columns), low)]
    return block + halves + quarters + ends + [dma((ring, 2)), dma((ring, 4)), dma((ring, 4)), dma((ring, 6)), reg((5,)), reg((3,))]

def slow_buffers(m, columns):
    dma, half, low = pltpu.SemaphoreType.DMA, columns // 2, jnp.bfloat16
    lead = [(2, m, 4, 2, 2), (m, 4, 2, 2), (m, 3, 2, 2), (m, 3, 2, 2), (m, 2, 2)]
    return (
        [pltpu.VMEM((*shape, ROWS, columns), low) for shape in lead]
        + [pltpu.VMEM((m, 2, ROWS, half), low)] * 4
        + [pltpu.VMEM((m, ROWS, half), low)] * 2
        + [dma((m, 2)), dma((m, 6)), dma((m, 6)), dma((m, 8))]
    )


def reduce_products(lefts, rights, pieces, m, small, width=1280, cid=2):
    n = len(pieces) - m
    small_width = small.shape[-1]
    tokens = rights[0].shape[0]
    hbm, vmem = pl.BlockSpec(memory_space=pl.ANY), pl.BlockSpec(memory_space=pltpu.VMEM)
    return pl.pallas_call(
        functools.partial(reduce_kernel, tuple(pieces), len(lefts), len(rights), n, m, width, small_width),
        out_shape=[
            jax.ShapeDtypeStruct((n + m, ROWS, width), jnp.float32),
            jax.ShapeDtypeStruct((ROWS, small_width), jnp.float32),
        ],
        in_specs=[hbm] * (len(lefts) + len(rights)) + [vmem],
        out_specs=[vmem, vmem],
        scratch_shapes=[
            pltpu.VMEM((3, tokens, 32 * ROWS), jnp.bfloat16),
            pltpu.VMEM((3, tokens, width), jnp.bfloat16),
            pltpu.VMEM((32 * ROWS, tokens), jnp.bfloat16),
            pltpu.SemaphoreType.DMA((3, 2)),
        ]
        + buffers(RING, width)
        + buffers(1, small_width)
        + slow_buffers(m, width),
        compiler_params=pltpu.CompilerParams(
            collective_id=cid, has_side_effects=True, vmem_limit_bytes=60 * 1024 * 1024
        ),
        name="reduce_products",
    )(*lefts, *rights, small)

D = 1280
HEADS = 16
HEAD_DIM = 80
PATCH = 32
SEQ = 512


EPSILON = 1e-06
MOMENTUM = 0.9
AVG_DECAY = 0.9


def matrix_multiply(left_mat, right_mat):
    return jnp.dot(left_mat, right_mat, preferred_element_type=jnp.float32)


def flipped_bilinear(left_mat, right_mat):
    return lax.dot_general(
        left_mat, right_mat, (((1,), (1,)), ((), ())), preferred_element_type=jnp.float32
    )


def bilinear_flipped(left_mat, right_mat):
    return lax.dot_general(
        left_mat, right_mat, (((0,), (0,)), ((), ())), preferred_element_type=jnp.float32
    )


def rounded(values_in):
    return values_in.astype(jnp.bfloat16)


def rms_gain(values_in, gains_in):
    return (
        values_in
        * lax.rsqrt(jnp.mean(values_in * values_in, axis=-1, keepdims=True) + EPSILON)
        * gains_in
    )


def silu_slope(values_in):
    logistic = jax.nn.sigmoid(values_in)
    return logistic * (1.0 + values_in * (1.0 - logistic))


def rope_tables():
    half_dim = HEAD_DIM // 2
    position = jnp.arange(SEQ, dtype=jnp.float32)[:, None]
    spacing = 10000.0 ** (-jnp.arange(half_dim, dtype=jnp.float32) / half_dim)
    angles = (position * spacing[None, :]).T
    return (jnp.cos(angles), jnp.sin(angles))


def contract_rows(left_mat, right_mat):
    return lax.dot_general(
        left_mat, right_mat, (((0,), (0,)), ((), ())), preferred_element_type=jnp.float32
    )


def contract_columns(left_mat, right_mat):
    return lax.dot_general(
        left_mat, right_mat, (((1,), (1,)), ((), ())), preferred_element_type=jnp.float32
    )


def turned_head(head, cosines, sines):
    lower, upper = head[: HEAD_DIM // 2], head[HEAD_DIM // 2 :]
    return jnp.concatenate([lower * cosines - upper * sines, upper * cosines + lower * sines], axis=0)


def fill_bias(bias, owner_column, owner_row):
    @pl.when(pl.program_id(0) == 0)
    def _():
        keys = lax.broadcasted_iota(jnp.int32, (SEQ, SEQ), 0)
        queries = lax.broadcasted_iota(jnp.int32, (SEQ, SEQ), 1)
        allowed = (keys <= queries) & (owner_column[...] == owner_row[...])
        bias[...] = jnp.where(allowed, 0.0, -1e30)


def spread(target, block):
    target[...] = block.astype(jnp.float32).T.reshape(target.shape)


def gathered_heads(source):
    return source[...].reshape(STEP_HEADS * HEAD_DIM, SEQ).T.astype(jnp.bfloat16)


def attend_kernel(
    query_in, key_in, value_in, cosines, sines, owner_column, owner_row, mixed, log_totals, bias, heads, outcome
):
    fill_bias(bias, owner_column, owner_row)
    cos, sin = cosines[...], sines[...]
    for i, block in enumerate((query_in, key_in, value_in)):
        spread(heads.at[i], block[...])

    def one(i):
        query = rounded(turned_head(heads[0, i], cos, sin))
        key = rounded(turned_head(heads[1, i], cos, sin))
        value = rounded(heads[2, i])
        for j in range(SEQ // TILE):
            cols, rows = slice(j * TILE, (j + 1) * TILE), (j + 1) * TILE
            scores = contract_rows(key[:, :rows], query[:, cols]) * HEAD_DIM ** (-0.5) + bias[:rows, cols]
            top = jnp.max(scores, axis=0, keepdims=True)
            expo = jnp.exp(scores - top)
            total = jnp.sum(expo, axis=0, keepdims=True)
            probability = rounded(expo * (1.0 / total))
            outcome[i, :, cols] = matrix_multiply(value[:, :rows], probability)
            log_totals[i, :, cols] = top + jnp.log(total)

    def pair(i, carry):
        one(2 * i)
        one(2 * i + 1)
        return carry

    lax.fori_loop(0, STEP_HEADS // 2, pair, 0)
    mixed[...] = gathered_heads(outcome)


def attend_back_kernel(
    query_in,
    key_in,
    value_in,
    cosines,
    sines,
    owner_column,
    owner_row,
    log_totals,
    grad_mixed,
    grad_query_out,
    grad_key_out,
    grad_value_out,
    bias,
    heads,
    outcome,
):
    fill_bias(bias, owner_column, owner_row)
    cos, sin = cosines[...], sines[...]
    scale = HEAD_DIM ** (-0.5)
    for i, block in enumerate((query_in, key_in, value_in, grad_mixed)):
        spread(heads.at[i], block[...])

    def one(i):
        query = rounded(turned_head(heads[0, i], cos, sin))
        key = rounded(turned_head(heads[1, i], cos, sin))
        value, grad_mix = rounded(heads[2, i]), rounded(heads[3, i])
        grad_key, grad_value = [], []
        for j in range(SEQ // TILE):
            cols, rows = slice(j * TILE, (j + 1) * TILE), (j + 1) * TILE
            scores = contract_rows(key[:, :rows], query[:, cols]) * scale + bias[:rows, cols]
            probability = jnp.exp(scores - log_totals[i, :, cols])
            grad_probs = contract_rows(value[:, :rows], grad_mix[:, cols])
            inner_sum = jnp.sum(probability * grad_probs, axis=0, keepdims=True)
            grad_scores = rounded(probability * (grad_probs - inner_sum))
            grad_query = matrix_multiply(key[:, :rows], grad_scores) * scale
            outcome[0, i, :, cols] = turned_head(grad_query, cos[:, cols], -sin[:, cols])
            grad_key.append(contract_columns(query[:, cols], grad_scores))
            grad_value.append(contract_columns(grad_mix[:, cols], rounded(probability)))
        for j in range(SEQ // TILE):
            cols = slice(j * TILE, (j + 1) * TILE)
            key_part = sum(g[:, cols] for g in grad_key[j:]) * scale
            outcome[1, i, :, cols] = turned_head(key_part, cos[:, cols], -sin[:, cols])
            outcome[2, i, :, cols] = sum(g[:, cols] for g in grad_value[j:])

    def pair(i, carry):
        one(2 * i)
        one(2 * i + 1)
        return carry

    lax.fori_loop(0, STEP_HEADS // 2, pair, 0)
    for i, block in enumerate((grad_query_out, grad_key_out, grad_value_out)):
        block[...] = gathered_heads(outcome.at[i])


STEP_HEADS = 8
TILE = 256


def token_block(third=0):
    steps = HEADS // STEP_HEADS
    return pl.BlockSpec((SEQ, STEP_HEADS * HEAD_DIM), lambda h: (0, third * steps + h))


def attention_specs():
    half = pl.BlockSpec((HEAD_DIM // 2, SEQ), lambda h: (0, 0))
    return [
        token_block(0),
        token_block(1),
        token_block(2),
        half,
        half,
        pl.BlockSpec((SEQ, 1), lambda h: (0, 0)),
        pl.BlockSpec((1, SEQ), lambda h: (0, 0)),
    ]


def attention_call(kernel, in_specs, out_shape, out_specs, name, held, operands):
    return pl.pallas_call(
        kernel,
        grid=(HEADS // STEP_HEADS,),
        out_shape=out_shape,
        in_specs=in_specs,
        out_specs=out_specs,
        scratch_shapes=[pltpu.VMEM((SEQ, SEQ), jnp.float32)]
        + [pltpu.VMEM((*lead, STEP_HEADS, HEAD_DIM, SEQ), jnp.float32) for lead in held],
        cost_estimate=pl.CostEstimate(
            flops=8 * HEADS * SEQ * SEQ * HEAD_DIM,
            bytes_accessed=20 * HEADS * HEAD_DIM * SEQ,
            transcendentals=HEADS * SEQ * SEQ,
        ),
        compiler_params=pltpu.CompilerParams(vmem_limit_bytes=30 * 1024 * 1024),
        name=name,
    )(*operands)


TOTALS = pl.BlockSpec((STEP_HEADS, 1, SEQ), lambda h: (h, 0, 0))


def attend(qkv, cosines, sines, owners):
    operands = (qkv, qkv, qkv, cosines, sines, owners[:, None], owners[None, :])
    return attention_call(
        attend_kernel,
        attention_specs(),
        [
            jax.ShapeDtypeStruct((SEQ, HEADS * HEAD_DIM), jnp.bfloat16),
            jax.ShapeDtypeStruct((HEADS, 1, SEQ), jnp.float32),
        ],
        [token_block(), TOTALS],
        "attend",
        [(3,), ()],
        operands,
    )


def attend_back(qkv, cosines, sines, owners, log_totals, grad_mixed):
    operands = (qkv, qkv, qkv, cosines, sines, owners[:, None], owners[None, :], log_totals, grad_mixed)
    return attention_call(
        attend_back_kernel,
        attention_specs() + [TOTALS, token_block()],
        [jax.ShapeDtypeStruct((SEQ, HEADS * HEAD_DIM), jnp.bfloat16)] * 3,
        [token_block()] * 3,
        "attend_back",
        [(4,), (3,)],
        operands,
    )


def update(master, moment, average, gradient, rate):
    moment_new = MOMENTUM * moment + gradient
    master_new = master - rate * (gradient + MOMENTUM * moment_new)
    average_new = AVG_DECAY * average + (1.0 - AVG_DECAY) * master_new
    return (master_new, moment_new, average_new)


EVERYONE = ("dp", "head")


def summed(partial):
    return lax.psum_scatter(rounded(partial), EVERYONE, scatter_dimension=0, tiled=True).astype(
        jnp.float32
    )


def gather_in_parts(shards):
    early = gather(shards[:6], EARLY, LATE)
    late, _ = lax.optimization_barrier((jnp.concatenate(shards[6:], axis=1), early[0]))
    late = lax.all_gather(late, EVERYONE, axis=0, tiled=True)
    return early + [late[:, :D], late[:, D:]]


def owned(values):
    return values.reshape(16, 2, ROWS, -1).swapaxes(0, 1).reshape(2, 4, 2, 2, ROWS, -1)


def on_device(
    input_segments,
    filler_flags,
    sequence_owner,
    prediction_adjoint,
    quadratic_params,
    quadratic_velocity,
    quadratic_mean,
    perceptron_params,
    perceptron_velocity,
    perceptron_mean,
    embedder_params,
    embedder_velocity,
    embedder_mean,
    bias_gain_params,
    bias_gain_velocity,
    bias_gain_mean,
    readout_params,
    readout_velocity,
    readout_mean,
):
    dp_size, head_size = lax.axis_size("dp"), lax.axis_size("head")
    low_square, low_ffn = rounded(quadratic_params), rounded(perceptron_params)
    low_token, low_readout = rounded(embedder_params), rounded(readout_params)
    vector_columns = jnp.pad(rounded(bias_gain_params).T, ((0, 0), (0, 123)))
    own_readout = lax.all_to_all(low_readout, "head", split_axis=1, concat_axis=2, tiled=True)
    adjoint = lax.all_to_all(prediction_adjoint, "head", split_axis=0, concat_axis=1, tiled=True)
    shards = [
        jnp.concatenate([low_square[0], low_token[0], low_token[1], vector_columns], axis=1),
        jnp.concatenate([low_square[1], low_square[2], low_square[3]], axis=1),
        low_square[4],
        low_ffn[0],
        low_ffn[1],
        low_square[5],
        own_readout[0],
        own_readout[1],
    ]
    fast = (dp_size, head_size) == (8, 4) and perceptron_params.shape[2] == 4 * D
    first, qkv_w, attn_out_w, up_w, down_w, hidden_w, readout_w, shortcut_w = (
        gather_in_parts(shards)
        if fast
        else [lax.all_gather(s, EVERYONE, axis=0, tiled=True) for s in shards]
    )
    tok_out_w, tok_hidden_w, tok_skip_w = first[:, :D], first[:, D : D + 64], first[:, D + 64 : D + 128]
    vectors = first[:, D + 128 : D + 133].T.astype(jnp.float32)

    tok_count = input_segments.shape[0]
    seq_rows = tok_count // SEQ
    mask_float = filler_flags.astype(jnp.float32)
    tok_input = rounded(jnp.concatenate([input_segments * (1.0 - mask_float), mask_float], axis=1))
    tok_pre = flipped_bilinear(tok_input, tok_hidden_w) + vectors[2]
    tok_act = rounded(jax.nn.silu(tok_pre))
    stream_in = (
        matrix_multiply(tok_act, tok_out_w) + flipped_bilinear(tok_input, tok_skip_w) + vectors[3]
    )
    normed_one, norm_pull_one = jax.vjp(rms_gain, stream_in, vectors[0])
    normed_attn = rounded(normed_one)
    cosines, sines = rope_tables()
    row_tokens = [slice(r * SEQ, (r + 1) * SEQ) for r in range(seq_rows)]
    qkv = matrix_multiply(normed_attn, qkv_w)
    qkv = [qkv[part] for part in row_tokens]
    attended = [
        attend(heads, cosines, sines, sequence_owner[part]) for heads, part in zip(qkv, row_tokens)
    ]
    attn_mix = jnp.concatenate([mixed for mixed, _ in attended], axis=0)
    stream_mid = stream_in + matrix_multiply(attn_mix, attn_out_w)
    normed_two, norm_pull_two = jax.vjp(rms_gain, stream_mid, vectors[1])
    normed_ffn = rounded(normed_two)
    ffn_pre = matrix_multiply(normed_ffn, up_w)
    ffn_act = rounded(jax.nn.silu(ffn_pre))
    stream_out = stream_mid + flipped_bilinear(ffn_act, down_w)
    stream_low = rounded(stream_out)
    head_pre = matrix_multiply(stream_low, hidden_w) + vectors[4]
    head_act = rounded(jax.nn.silu(head_pre))
    own_prediction = rounded(
        matrix_multiply(head_act, readout_w) + matrix_multiply(stream_low, shortcut_w)
    )
    prediction = lax.all_to_all(own_prediction, "head", split_axis=1, concat_axis=0, tiled=True)

    shard_rows = D // (dp_size * head_size)
    head_left = jnp.stack([v.T.reshape(-1, shard_rows, tok_count) for v in (head_act, stream_low)], axis=1)
    head_share = summed(matrix_multiply(head_left.reshape(2 * D, tok_count), adjoint))
    head_share = head_share.reshape(2, shard_rows, head_size, -1).transpose(2, 0, 1, 3)
    grad_head_act = flipped_bilinear(adjoint, readout_w)
    grad_skip = flipped_bilinear(adjoint, shortcut_w)
    grad_head_pre = rounded(grad_head_act * silu_slope(head_pre))
    grad_bias_head = jnp.sum(grad_head_pre.astype(jnp.float32), axis=0)
    grad_stream_out = grad_skip + flipped_bilinear(grad_head_pre, hidden_w)
    grad_ffn_out = rounded(grad_stream_out)
    grad_ffn_pre = rounded(matrix_multiply(grad_ffn_out, down_w) * silu_slope(ffn_pre))
    grad_stream_norm, grad_gain_two = norm_pull_two(flipped_bilinear(grad_ffn_pre, up_w))
    grad_stream_mid = grad_stream_out + grad_stream_norm
    grad_attn_out = rounded(grad_stream_mid)
    grad_attn_mix = rounded(flipped_bilinear(grad_attn_out, attn_out_w))
    grad_heads = [
        attend_back(heads, cosines, sines, sequence_owner[part], log_totals, grad_attn_mix[part])
        for heads, part, (_, log_totals) in zip(qkv, row_tokens, attended)
    ]
    grad_qkv_pre = [jnp.concatenate([heads[i] for heads in grad_heads], axis=0) for i in range(3)]
    grad_normed = sum(
        flipped_bilinear(grad, qkv_w[:, D * i : D * (i + 1)]) for i, grad in enumerate(grad_qkv_pre)
    )
    grad_stream_first, grad_gain_one = norm_pull_one(grad_normed)
    grad_stream_in = grad_stream_mid + grad_stream_first
    grad_bias_out = jnp.sum(grad_stream_in, axis=0)
    grad_tok_out = rounded(grad_stream_in)
    grad_skip_tok = bilinear_flipped(grad_tok_out, tok_input)
    grad_tok_pre = rounded(flipped_bilinear(grad_tok_out, tok_out_w) * silu_slope(tok_pre))
    grad_bias_tok = jnp.sum(grad_tok_pre.astype(jnp.float32), axis=0)
    grad_hidden_tok = bilinear_flipped(grad_tok_pre, tok_input)
    grad_input = matrix_multiply(grad_tok_out, tok_skip_w) + matrix_multiply(
        grad_tok_pre, tok_hidden_w
    )
    segment_derivative = grad_input[:, :PATCH] * (1.0 - mask_float)
    grad_vector = jnp.stack(
        [grad_gain_one, grad_gain_two, grad_bias_tok, grad_bias_out, grad_bias_head], axis=1
    )
    small = rounded(
        jnp.concatenate([grad_hidden_tok, grad_skip_tok, jnp.pad(grad_vector, ((0, 0), (0, 123)))], axis=1)
    )
    wide = ffn_act.shape[1] // D
    pieces = [(0, 0, 0)]
    pieces += [(1, 1, D * j) for j in range(wide)] + [(2, 2, D * j) for j in range(wide)]
    pieces += [(3, 3, 0)] + [(4, 4 + j, 0) for j in range(3)] + [(5, 7, 0)]
    lefts = [stream_low, grad_ffn_out, normed_ffn, attn_mix, normed_attn, tok_act]
    rights = [grad_head_pre, ffn_act, grad_ffn_pre, grad_attn_out, *grad_qkv_pre, grad_tok_out]
    down_at = 1
    if fast:
        slow = [down_at, down_at + 1]
        order = [i for i in range(len(pieces)) if i not in slow] + slow
        summed_shares, small_share = reduce_products(
            lefts, rights, [pieces[i] for i in order], len(slow), owned(small)
        )
        shares = [summed_shares[order.index(i)] for i in range(len(pieces))]
    else:
        shares = [
            summed(bilinear_flipped(lefts[i], rights[j][:, start : start + D])) for i, j, start in pieces
        ]
        small_share = summed(small)
    head_share = lax.all_to_all(head_share, "head", split_axis=0, concat_axis=0)
    head_share = head_share.transpose(1, 0, 2, 3).reshape(readout_params.shape)
    up_at = down_at + wide
    wo_at = up_at + wide
    square_share = jnp.stack(
        [shares[wo_at + 4], shares[wo_at + 1], shares[wo_at + 2], shares[wo_at + 3], shares[wo_at], shares[0]]
    )
    ffn_share = jnp.stack(
        [
            jnp.concatenate([shares[up_at + j] for j in range(wide)], axis=1),
            jnp.concatenate([shares[down_at + j] for j in range(wide)], axis=1),
        ]
    )
    token_share = jnp.stack([small_share[:, :64], small_share[:, 64:128]])
    vector_share = small_share[:, 128:133].T
    all_tokens = tok_count * lax.axis_size("dp") * lax.axis_size("head")
    matrix_rate = 0.5 / (D * all_tokens) ** 0.5
    quadratic_params_fresh, quadratic_velocity_fresh, quadratic_mean_fresh = update(
        quadratic_params, quadratic_velocity, quadratic_mean, square_share, matrix_rate
    )
    perceptron_params_fresh, perceptron_velocity_fresh, perceptron_mean_fresh = update(
        perceptron_params, perceptron_velocity, perceptron_mean, ffn_share, matrix_rate
    )
    embedder_params_fresh, embedder_velocity_fresh, embedder_mean_fresh = update(
        embedder_params,
        embedder_velocity,
        embedder_mean,
        token_share,
        0.5 / (2 * PATCH * all_tokens) ** 0.5,
    )
    bias_gain_params_fresh, bias_gain_velocity_fresh, bias_gain_mean_fresh = update(
        bias_gain_params, bias_gain_velocity, bias_gain_mean, vector_share, 0.3 / all_tokens**0.5
    )
    readout_params_fresh, readout_velocity_fresh, readout_mean_fresh = update(
        readout_params, readout_velocity, readout_mean, head_share, matrix_rate
    )
    return (
        prediction,
        segment_derivative,
        quadratic_params_fresh,
        quadratic_velocity_fresh,
        quadratic_mean_fresh,
        perceptron_params_fresh,
        perceptron_velocity_fresh,
        perceptron_mean_fresh,
        embedder_params_fresh,
        embedder_velocity_fresh,
        embedder_mean_fresh,
        bias_gain_params_fresh,
        bias_gain_velocity_fresh,
        bias_gain_mean_fresh,
        readout_params_fresh,
        readout_velocity_fresh,
        readout_mean_fresh,
    )


def solution(mesh):
    placed = (
        P(("dp", "head"), None),
        P(("dp", "head"), None),
        P(("dp", "head")),
        P("dp", "head"),
        P(None, ("dp", "head"), None),
        P(None, ("dp", "head"), None),
        P(None, ("dp", "head"), None),
        P(None, ("dp", "head"), None),
        P(None, ("dp", "head"), None),
        P(None, ("dp", "head"), None),
        P(None, ("dp", "head"), None),
        P(None, ("dp", "head"), None),
        P(None, ("dp", "head"), None),
        P(None, ("dp", "head")),
        P(None, ("dp", "head")),
        P(None, ("dp", "head")),
        P(None, "dp", "head"),
        P(None, "dp", "head"),
        P(None, "dp", "head"),
    )
    return jax.shard_map(
        on_device,
        mesh=mesh,
        in_specs=placed,
        out_specs=(
            P("dp", "head"),
            P(("dp", "head"), None),
            P(None, ("dp", "head"), None),
            P(None, ("dp", "head"), None),
            P(None, ("dp", "head"), None),
            P(None, ("dp", "head"), None),
            P(None, ("dp", "head"), None),
            P(None, ("dp", "head"), None),
            P(None, ("dp", "head"), None),
            P(None, ("dp", "head"), None),
            P(None, ("dp", "head"), None),
            P(None, ("dp", "head")),
            P(None, ("dp", "head")),
            P(None, ("dp", "head")),
            P(None, "dp", "head"),
            P(None, "dp", "head"),
            P(None, "dp", "head"),
        ),
        check_vma=False,
    )
```
